128 devices in a mesh: dp: 8 (over y, z_lo), seq: 16 (over x, z_hi, core).
Axes of the slice: x: 4, y: 4, z: 4 (z_hi: 2, z_lo: 2; z = z_hi * 2 + z_lo), core: 2. Of those that a mesh axis runs over, the one named last changes fastest.
Arguments:
- video: bfloat16 [8, 64, 256, 768], P('dp', 'seq'), may hold values from -6 to 6
- space_qkv: bfloat16 [768, 2304], replicated, may hold values from -0.21875 to 0.21875
- space_out: bfloat16 [768, 768], replicated, may hold values from -0.21875 to 0.21875
- time_qkv: bfloat16 [768, 2304], replicated, may hold values from -0.21875 to 0.21875
- time_out: bfloat16 [768, 768], replicated, may hold values from -0.21875 to 0.21875
- proj_weight: bfloat16 [768, 128], replicated, may hold values from -0.21875 to 0.21875
- queries: bfloat16 [64, 32, 128], P('dp'), may hold values from -6 to 6
- query_len: int32 [64], P('dp'), may hold values from 1 to 32, 1280 in all
- positive: int32 [64], P('dp'), may hold values from 0 to 7
Outputs:
- video_grad: bfloat16 [8, 64, 256, 128], P('dp', None, 'seq')
- query_grad: bfloat16 [64, 32, 128], P('dp')
- pair_loss: float32 [64, 8], P(None, 'dp')
The draws below stay inside these ranges and needn't reach their ends.
Inputs may be any that keep to these rules, and one draw needn't show every extreme that they name: `query_len`: the query lengths sum to 5 / 8 of all slots and the longest query fills all 32 slots.
All inputs are finite; a program needn't handle non-finite values. No bound on the sum of `query_len` on one device may be relied on, other than what follows from the above.
Results may differ from the reference program's by a relative error of at most 0.028.
Values may be sent and summed in bfloat16 or wider, within the bound.
No kernel may reach another device: no remote copies, remote signals or barrier semaphores. Data moves between devices by JAX's collectives and lax.ppermute only.
A program may use at most 128 MiB of HBM per device.

```python
import math
import jax
import jax.numpy as jnp
import numpy as np
from jax import lax

D = 768
HEADS = 12
E = 128
P_SIZE = 256
LQ = 32
F = 64
V = 8
Q = 64


def touch_ends(drawn, stream_key, low, largest):
    shape = drawn.shape
    index_at = [jax.random.randint(jax.random.fold_in(stream_key, axis), (), 0, shape[axis]) for axis in range(len(shape))]
    drawn = drawn.at[tuple(index_at)].set(low)
    longest = shape.index(max(shape))
    index_at[longest] = (index_at[longest] + 1) % shape[longest]
    return drawn.at[tuple(index_at)].set(largest)


def levels(own_key, shape, shards, smallest, top_value):
    loudness = 1.0
    for position, shards_of in shards:
        heights = jax.random.uniform(jax.random.fold_in(jax.random.fold_in(own_key, 6), position), (shards_of,), jnp.float32, smallest / len(shards), top_value / len(shards))
        loudness = loudness * jnp.repeat(jnp.exp(heights), shape[position] // shards_of).reshape((-1,) + (1,) * (len(shape) - 1 - position))
    return loudness


def split_up(number_of, total, limit, skew):
    loads = [(1 << 20) // math.isqrt(grade ** skew) + 1 for grade in range(2, number_of + 1)]
    spare, given = total - limit - (number_of - 1), [1] * (number_of - 1)
    while spare > 0:
        movable = [i for i in range(number_of - 1) if given[i] < limit]
        whole, remaining = sum([loads[i] for i in movable]), spare
        for i in movable:
            addition = min(limit - given[i], max(1, remaining * loads[i] // whole), spare)
            given[i] = given[i] + addition
            spare = spare - addition
    return np.array([limit] + given)


def ragged_sizes(rng, count, total, limit, lean):
    if count == 2:
        one = jax.random.randint(rng, (), max(1, total - limit), min(limit, total - 1) + 1)
        return jnp.stack([one, total - one])
    sizes = jnp.asarray(split_up(count, total, limit, lean), jnp.int32)
    pairs = (count - 1) // 2
    source_of, taker = sizes[1:1 + 2 * pairs:2], sizes[2:2 + 2 * pairs:2]
    slack = jnp.minimum(source_of - 1, limit - taker)
    shifted = jax.random.randint(jax.random.fold_in(rng, 1), (pairs,), 0, 1 << 20) % (slack + 1)
    sizes = sizes.at[1:1 + 2 * pairs:2].set(source_of - shifted).at[2:2 + 2 * pairs:2].set(taker + shifted)
    return sizes[jax.random.permutation(jax.random.fold_in(rng, 2), count)]


def noise(stream_key, shape, scale, bound, split=(), kind=jnp.bfloat16):
    values = scale * jax.random.normal(stream_key, shape, jnp.float32)
    if split:
        values = values * levels(stream_key, shape, split, -0.22, 0.18)
    return jnp.clip(values, -bound, bound).astype(kind)


def setup_inputs(seed: int = 0) -> dict:
    arg_keys = jax.random.split(jax.random.key(seed), 10)
    return {
        "video": noise(arg_keys[0], (V, F, P_SIZE, D), 1.0, 6.0, ((0, 8), (1, 16))),
        "space_qkv": noise(arg_keys[1], (D, 3 * D), D ** -0.5, 0.21875),
        "space_out": noise(arg_keys[2], (D, D), D ** -0.5, 0.21875),
        "time_qkv": noise(arg_keys[3], (D, 3 * D), D ** -0.5, 0.21875),
        "time_out": noise(arg_keys[4], (D, D), D ** -0.5, 0.21875),
        "proj_weight": noise(arg_keys[5], (D, E), D ** -0.5, 0.21875),
        "queries": noise(arg_keys[6], (Q, LQ, E), 1.0, 6.0, ((0, 8),)),
        "query_len": ragged_sizes(arg_keys[7], Q, Q * LQ * 5 // 8, LQ, 1).astype(jnp.int32),
        "positive": touch_ends(jax.random.randint(arg_keys[8], (Q,), 0, V), jax.random.fold_in(arg_keys[8], 1), 0, V - 1).astype(jnp.int32),
    }


TEMPER = 0.05
SLOPE = 10.0
OFFSET = -5.0
SHARP = 10.0

def layer_norm(tokens):
    values = tokens.astype(jnp.float32)
    center = values - lax.optimization_barrier(jnp.mean(values, axis=-1, keepdims=True))
    spread = lax.optimization_barrier(jnp.mean(center * center, axis=-1, keepdims=True))
    return (center / jnp.sqrt(spread + 1e-05)).astype(jnp.bfloat16)

def unit_rows(values):
    values = values.astype(jnp.float32)
    return values / jnp.sqrt(lax.optimization_barrier(jnp.sum(values * values, axis=-1, keepdims=True)) + 1e-06)

def attend(tokens, qkv_weight, out_weight):
    groups, extent, feature = tokens.shape
    normed = layer_norm(tokens)
    packed = jnp.einsum('nld,de->nle', normed.astype(jnp.float32), qkv_weight.astype(jnp.float32)).astype(jnp.bfloat16)
    packed = packed.reshape(groups, extent, 3, HEADS, feature // HEADS)
    query_rows = unit_rows(packed[:, :, 0]).astype(jnp.bfloat16)
    key_rows = unit_rows(packed[:, :, 1]).astype(jnp.bfloat16)
    scores = jnp.einsum('nqhc,nkhc->nhqk', query_rows.astype(jnp.float32), key_rows.astype(jnp.float32))
    weights = jnp.exp(SHARP * scores)
    weights = (weights / lax.optimization_barrier(jnp.sum(weights, axis=-1, keepdims=True))).astype(jnp.bfloat16)
    blended = jnp.einsum('nhqk,nkhc->nqhc', weights.astype(jnp.float32), packed[:, :, 2].astype(jnp.float32))
    blended = blended.astype(jnp.bfloat16).reshape(groups, extent, feature)
    update = jnp.einsum('nld,de->nle', blended.astype(jnp.float32), out_weight.astype(jnp.float32))
    return (tokens.astype(jnp.float32) + update).astype(jnp.bfloat16)

def reference(video, space_qkv, space_out, time_qkv, time_out, proj_weight, queries, query_len, positive):

    def encode(one_video):
        spatial = attend(one_video, space_qkv, space_out)
        columns = jnp.transpose(spatial, (1, 0, 2))
        mixed_cols = attend(columns, time_qkv, time_out)
        projected = jnp.dot(layer_norm(mixed_cols).reshape(-1, D), proj_weight, preferred_element_type=jnp.float32)
        embedded = unit_rows(projected).astype(jnp.bfloat16).reshape(P_SIZE, F, E)
        return jnp.transpose(embedded, (1, 0, 2)).reshape(F * P_SIZE, E)
    token_emb = lax.map(encode, video)
    unit_query = unit_rows(queries).astype(jnp.bfloat16).reshape(Q * LQ, E)

    def video_sums(key_rows):
        dot_raw = jnp.dot(unit_query, key_rows.T, preferred_element_type=jnp.float32)
        return lax.optimization_barrier(jnp.sum(jnp.exp((dot_raw - 1.0) / TEMPER), axis=-1))
    totals = lax.map(video_sums, token_emb)
    smooth = (1.0 + TEMPER * jnp.log(totals)).T.reshape(Q, LQ, V)
    token_mask = (jnp.arange(LQ, dtype=jnp.int32)[None, :] < query_len[:, None]).astype(jnp.float32)
    token_count = query_len.astype(jnp.float32)
    scores_pair = lax.optimization_barrier(jnp.sum(smooth * token_mask[:, :, None], axis=1)) / token_count[:, None]
    pair_sign = jnp.where(positive[:, None] == jnp.arange(V, dtype=jnp.int32)[None, :], 1.0, -1.0)
    margin = pair_sign * (SLOPE * scores_pair + OFFSET)
    pair_loss = jax.nn.softplus(-margin)
    pair_grad = -pair_sign * SLOPE * jax.nn.sigmoid(-margin)
    token_coeff = pair_grad[:, None, :] * (token_mask / token_count[:, None])[:, :, None]
    coeff_rows = token_coeff.reshape(Q * LQ, V).T

    def video_grads(running, inputs):
        key_rows, row_total, weight = inputs
        dot_raw = jnp.dot(unit_query, key_rows.T, preferred_element_type=jnp.float32)
        expo_terms = jnp.exp((dot_raw - 1.0) / TEMPER)
        weights_bf = (expo_terms / row_total[:, None] * weight[:, None]).astype(jnp.bfloat16)
        key_grad = jnp.dot(weights_bf.T, unit_query, preferred_element_type=jnp.float32)
        return (running + jnp.dot(weights_bf, key_rows, preferred_element_type=jnp.float32), key_grad)
    query_total, key_grads = lax.scan(video_grads, jnp.zeros((Q * LQ, E), jnp.float32), (token_emb, totals, coeff_rows))
    video_grad = (F * P_SIZE * key_grads).astype(jnp.bfloat16).reshape(V, F, P_SIZE, E)
    query_grad = (LQ * query_total).astype(jnp.bfloat16).reshape(Q, LQ, E)
    return (video_grad, query_grad, pair_loss)
```

```python
import jax
import jax.numpy as jnp
from jax import lax
from jax.experimental import pallas as pl
from jax.experimental.pallas import tpu as pltpu
from jax.sharding import PartitionSpec as P

HEADS = 12
P_SIZE = 256
TEMPER = 0.05
SLOPE = 10.0
OFFSET = -5.0
SHARP = 10.0
LOG2E = 1.4426950408889634

D = 768
HEAD = D // HEADS
PAIR = 2 * HEAD
PAIRS = HEADS // 2
TILE = 256
SUB = 128
E = 128
F32 = jnp.float32
BF16 = jnp.bfloat16


def dot(a, b):
    return lax.dot_general(a, b, (((1,), (0,)), ((), ())), preferred_element_type=F32)


def dot_t(a, b):
    return lax.dot_general(a, b, (((1,), (1,)), ((), ())), preferred_element_type=F32)


def iota(shape, dim):
    return lax.broadcasted_iota(jnp.int32, shape, dim)


def layer_norm(tokens):
    values = tokens.astype(F32)
    center = values - jnp.mean(values, axis=-1, keepdims=True)
    spread = jnp.mean(center * center, axis=-1, keepdims=True)
    return (center * lax.rsqrt(spread + 1e-05)).astype(BF16)


def unit_heads(values, gain):
    same = (iota((TILE, TILE), 0) // HEAD == iota((TILE, TILE), 1) // HEAD).astype(BF16)
    parts = []
    for at in range(0, values.shape[1], TILE):
        part = values[:, at : at + TILE]
        squares = dot((part * part).astype(BF16), same)
        parts.append((part * (lax.rsqrt(squares + 1e-06) * gain)).astype(BF16))
    return jnp.concatenate(parts, axis=1)


def qkv_rows(tokens, weight_ref):
    packed = dot(layer_norm(tokens), weight_ref[...])
    query = unit_heads(packed[:, :D], SHARP * LOG2E)
    key = unit_heads(packed[:, D : 2 * D], 1.0)
    return query, key, packed[:, 2 * D :].astype(BF16)


def pair_blend(query, key, value, keep):
    extent = key.shape[0]
    low = iota((extent, PAIR), 1) < HEAD
    zero = jnp.zeros((extent, PAIR), BF16)
    one = jnp.ones((extent, PAIR), BF16)
    keys = jnp.concatenate([jnp.where(low, key, zero), jnp.where(low, zero, key)], axis=0)
    values = jnp.concatenate(
        [
            jnp.concatenate([jnp.where(low, value, zero), jnp.where(low, one, zero)], axis=1),
            jnp.concatenate([jnp.where(low, zero, value), jnp.where(low, zero, one)], axis=1),
        ],
        axis=0,
    )
    weights = jnp.exp2(dot_t(query, keys))
    if keep is not None:
        weights = jnp.where(keep, weights, 0.0)
    mixed = dot(weights.astype(BF16), values)
    return (mixed[:, :PAIR] / mixed[:, PAIR:]).astype(BF16)


def space_kernel(video_ref, qkv_ref, out_w_ref, out_ref):
    tokens = video_ref[0]
    query, key, value = qkv_rows(tokens, qkv_ref)
    blended = []
    for pair in range(PAIRS):
        at = slice(pair * PAIR, (pair + 1) * PAIR)
        blended.append(pair_blend(query[:, at], key[:, at], value[:, at], None))
    update = dot(jnp.concatenate(blended, axis=1), out_w_ref[...])
    result = (tokens.astype(F32) + update).astype(BF16)
    out_ref[...] = result.reshape(out_ref.shape)


def space(video, qkv_weight, out_weight, shards):
    frames, patches, _ = video.shape
    local = patches // shards
    return pl.pallas_call(
        space_kernel,
        grid=(frames,),
        in_specs=[
            pl.BlockSpec((1, patches, D), lambda f: (f, 0, 0)),
            pl.BlockSpec((D, 3 * D), lambda f: (0, 0)),
            pl.BlockSpec((D, D), lambda f: (0, 0)),
        ],
        out_specs=pl.BlockSpec((shards, 1, local, D), lambda f: (0, f, 0, 0)),
        out_shape=jax.ShapeDtypeStruct((shards, frames, local, D), BF16),
        compiler_params=pltpu.CompilerParams(vmem_limit_bytes=48 * 2**20),
        name="space",
    )(video, qkv_weight, out_weight)


def swap_rows(rows, side):
    extent = side * side
    row, col = iota((extent, extent), 0), iota((extent, extent), 1)
    swap = (col == (row % side) * side + row // side).astype(BF16)
    return dot(swap, rows).astype(BF16)


def time_kernel(x_ref, qkv_ref, out_w_ref, proj_ref, khat_ref, x_s, q_s, k_s, v_s, kh_s):
    step = pl.program_id(0)
    side = x_s.shape[0]
    tiles = pl.num_programs(0) // 2
    groups = TILE // x_s.shape[1]

    @pl.when(step < tiles)
    def _():
        tokens = swap_rows(x_ref[...], side)
        query, key, value = qkv_rows(tokens, qkv_ref)
        at = pl.ds(pl.multiple_of(step * side, side), side)
        x_s[:, at, :] = tokens.reshape(side, side, D)
        q_s[:, at, :] = query.reshape(side, side, D)
        k_s[:, at, :] = key.reshape(side, side, D)
        v_s[:, at, :] = value.reshape(side, side, D)

    @pl.when(step >= tiles)
    def _():
        at = pl.ds((step - tiles) * groups, groups)
        extent = x_s.shape[1]
        query = q_s[at].reshape(TILE, D)
        key = k_s[at].reshape(TILE, D)
        value = v_s[at].reshape(TILE, D)
        keep = iota((SUB, 2 * SUB), 0) // extent == (iota((SUB, 2 * SUB), 1) % SUB) // extent
        rows = []
        for sub in range(TILE // SUB):
            down = slice(sub * SUB, (sub + 1) * SUB)
            cols = []
            for pair in range(PAIRS):
                across = slice(pair * PAIR, (pair + 1) * PAIR)
                cols.append(
                    pair_blend(query[down, across], key[down, across], value[down, across], keep)
                )
            rows.append(jnp.concatenate(cols, axis=1))
        update = dot(jnp.concatenate(rows, axis=0), out_w_ref[...])
        tokens = x_s[at].reshape(TILE, D)
        mixed = (tokens.astype(F32) + update).astype(BF16)
        projected = dot(layer_norm(mixed), proj_ref[...])
        norm = jnp.sum(projected * projected, axis=-1, keepdims=True)
        unit = (projected * lax.rsqrt(norm + 1e-06)).astype(BF16)
        kh_s[at] = unit.reshape(groups, extent, E)

    @pl.when(step == 2 * tiles - 1)
    def _():
        for tile in range(khat_ref.shape[0] // TILE):
            rows = kh_s[:, tile * side : (tile + 1) * side, :].reshape(TILE, E)
            khat_ref[tile * TILE : (tile + 1) * TILE, :] = swap_rows(rows, side)


def time(x, qkv_weight, out_weight, proj_weight, patches):
    rows = x.shape[0]
    frames = rows // patches
    tiles = rows // TILE
    whole = lambda s: (0, 0)
    return pl.pallas_call(
        time_kernel,
        grid=(2 * tiles,),
        in_specs=[
            pl.BlockSpec((TILE, D), lambda s: (jnp.minimum(s, tiles - 1), 0)),
            pl.BlockSpec((D, 3 * D), whole),
            pl.BlockSpec((D, D), whole),
            pl.BlockSpec((D, E), whole),
        ],
        out_specs=pl.BlockSpec((rows, E), whole),
        out_shape=jax.ShapeDtypeStruct((rows, E), BF16),
        scratch_shapes=[pltpu.VMEM((patches, frames, D), BF16)] * 4
        + [pltpu.VMEM((patches, frames, E), BF16)],
        compiler_params=pltpu.CompilerParams(vmem_limit_bytes=48 * 2**20),
        name="time",
    )(x, qkv_weight, out_weight, proj_weight)


EXTRA = 16


def query_kernel(len_ref, pos_ref, q_ref, out_ref):
    rows = q_ref.shape[0]
    values = q_ref[...].astype(F32)
    norm = jnp.sum(values * values, axis=-1, keepdims=True)
    unit = (values / jnp.sqrt(norm + 1e-06)).astype(BF16)
    slots = rows // len_ref.shape[0]
    row, lane = iota((EXTRA, E), 0), iota((EXTRA, E), 1)
    owner = ((row % 2) * E + lane) // slots
    extra = jnp.zeros((EXTRA, E), F32)
    for query in range(len_ref.shape[0]):
        picked = jnp.where(row < 2, len_ref[query], pos_ref[query]).astype(F32)
        extra = jnp.where((owner == query) & (row < 4), picked, extra)
    for copy in range(out_ref.shape[0]):
        out_ref[copy, :rows, :] = unit
        out_ref[copy, rows:, :] = extra.astype(BF16)


def pack_queries(queries, query_len, positive, copies):
    rows = queries.shape[0]
    return pl.pallas_call(
        query_kernel,
        in_specs=[
            pl.BlockSpec(memory_space=pltpu.SMEM),
            pl.BlockSpec(memory_space=pltpu.SMEM),
            pl.BlockSpec(memory_space=pltpu.VMEM),
        ],
        out_specs=pl.BlockSpec(memory_space=pltpu.VMEM),
        out_shape=jax.ShapeDtypeStruct((copies, rows + EXTRA, E), BF16),
        name="pack_queries",
    )(query_len, positive, queries)


def terms_kernel(q_ref, khat_ref, expo_ref, blend_ref, sums_ref):
    rows = expo_ref.shape[0]
    khat = khat_ref[...]
    dots = dot_t(q_ref[0, :rows, :], khat)
    gain = LOG2E / TEMPER
    expo = jnp.exp2(dots * gain - gain).astype(BF16)
    expo_ref[...] = expo
    wide = jnp.concatenate([khat, jnp.ones_like(khat)], axis=1)
    both = dot(expo, wide)
    blend_ref[...] = both[:, :E]
    eye = iota((E, E), 0) == iota((E, E), 1)
    for part in range(rows // E):
        block = both[part * E : (part + 1) * E, E:]
        sums_ref[0, part : part + 1, :] = jnp.sum(
            jnp.where(eye, block, 0.0), axis=0, keepdims=True
        )


def terms(packed, khat):
    blocks, rows, _ = packed.shape
    rows = rows - EXTRA
    tokens = khat.shape[0]
    return pl.pallas_call(
        terms_kernel,
        grid=(blocks,),
        in_specs=[
            pl.BlockSpec((1, rows + EXTRA, E), lambda b: (b, 0, 0)),
            pl.BlockSpec((tokens, E), lambda b: (0, 0)),
        ],
        out_specs=[
            pl.BlockSpec((rows, tokens), lambda b: (b, 0)),
            pl.BlockSpec((rows, E), lambda b: (b, 0)),
            pl.BlockSpec((1, rows // E, E), lambda b: (b, 0, 0)),
        ],
        out_shape=[
            jax.ShapeDtypeStruct((blocks * rows, tokens), BF16),
            jax.ShapeDtypeStruct((blocks * rows, E), F32),
            jax.ShapeDtypeStruct((blocks, rows // E, E), F32),
        ],
        compiler_params=pltpu.CompilerParams(vmem_limit_bytes=48 * 2**20),
        name="terms",
    )(packed, khat)


def scale_kernel(slots, video_ref, sums_ref, packed_ref, blend_ref, part_ref, qt_ref, loss_ref):
    blocks, rows, _ = packed_ref.shape
    rows = rows - EXTRA
    per = rows // E
    total = jnp.sum(sums_ref[...], axis=0)
    lens = jnp.concatenate(
        [packed_ref[b, rows : rows + EXTRA, :].astype(F32)[:per] for b in range(blocks)], axis=0
    )
    pos = jnp.concatenate(
        [packed_ref[b, rows : rows + EXTRA, :].astype(F32)[2 : 2 + per] for b in range(blocks)],
        axis=0,
    )
    lane = iota(total.shape, 1)
    mask = ((lane % slots).astype(F32) < lens).astype(F32)
    smooth = (1.0 + TEMPER * jnp.log(total)) * mask
    same = (iota((E, E), 0) // slots == iota((E, E), 1) // slots).astype(F32)
    score = (
        lax.dot_general(
            smooth,
            same,
            (((1,), (0,)), ((), ())),
            preferred_element_type=F32,
            precision=lax.Precision.HIGHEST,
        )
        / lens
    )
    sign = jnp.where(pos == video_ref[0].astype(F32), 1.0, -1.0)
    margin = sign * (SLOPE * score + OFFSET)
    loss_ref[...] = jnp.maximum(-margin, 0.0) + jnp.log1p(jnp.exp(-jnp.abs(margin)))
    coeff = -SLOPE * sign / (1.0 + jnp.exp(margin)) * mask / lens
    scale = (coeff / total).T
    for b in range(blocks):
        for part in range(per):
            at = b * per + part
            column = scale[:, at : at + 1]
            down = slice(part * E, (part + 1) * E)
            flat = slice(at * E, (at + 1) * E)
            part_ref[b, down, :] = (blend_ref[flat, :] * column).astype(BF16)
            scaled = packed_ref[b, down, :].astype(F32) * column
            qt_ref[:, flat] = scaled.T.astype(BF16)


def scales(sums, packed, blend, video_id, slots):
    blocks, rows, _ = packed.shape
    rows = rows - EXTRA
    vmem = pl.BlockSpec(memory_space=pltpu.VMEM)
    return pl.pallas_call(
        lambda *refs: scale_kernel(slots, *refs),
        in_specs=[pl.BlockSpec(memory_space=pltpu.SMEM), vmem, vmem, vmem],
        out_specs=[vmem, vmem, vmem],
        out_shape=[
            jax.ShapeDtypeStruct((blocks, rows, E), BF16),
            jax.ShapeDtypeStruct((E, blocks * rows), BF16),
            jax.ShapeDtypeStruct(sums.shape[1:], F32),
        ],
        compiler_params=pltpu.CompilerParams(vmem_limit_bytes=32 * 2**20),
        name="scales",
    )(video_id, sums, packed, blend)


def keys_kernel(gain, qt_ref, expo_ref, out_ref, acc_ref):
    step = pl.program_id(0)
    product = dot(qt_ref[...], expo_ref[...])

    @pl.when(step == 0)
    def _():
        acc_ref[...] = product

    @pl.when(step > 0)
    def _():
        acc_ref[...] += product

    @pl.when(step == pl.num_programs(0) - 1)
    def _():
        out_ref[...] = (acc_ref[...].T * gain).astype(BF16)


def keys(qt, expo, gain):
    rows, tokens = expo.shape
    return pl.pallas_call(
        lambda *refs: keys_kernel(gain, *refs),
        grid=(rows // TILE,),
        in_specs=[
            pl.BlockSpec((E, TILE), lambda b: (0, b)),
            pl.BlockSpec((TILE, tokens), lambda b: (b, 0)),
        ],
        out_specs=pl.BlockSpec((tokens, E), lambda b: (0, 0)),
        out_shape=jax.ShapeDtypeStruct((tokens, E), BF16),
        scratch_shapes=[pltpu.VMEM((E, tokens), F32)],
        compiler_params=pltpu.CompilerParams(vmem_limit_bytes=32 * 2**20),
        name="keys",
    )(qt, expo)


def body(
    video, space_qkv, space_out, time_qkv, time_out, proj_weight, queries, query_len, positive
):
    _, frames_dev, patches, _ = video.shape
    shards = lax.axis_size("seq")
    blocks = lax.axis_size("dp")
    patch_loc = patches // shards
    frames = frames_dev * shards
    query_dev, slots, _ = queries.shape
    rows = query_dev * slots

    mine = pack_queries(queries.reshape(rows, E), query_len, positive, blocks)
    packed = lax.all_to_all(mine, "dp", 0, 0, tiled=True)

    spatial = space(video[0], space_qkv, space_out, shards)
    items = lax.all_to_all(spatial, "seq", 0, 0, tiled=True)
    khat = time(items.reshape(-1, D), time_qkv, time_out, proj_weight, patch_loc)

    expo, blend, sums = terms(packed, khat)
    sums = sums.reshape(-1, E)
    sums = lax.all_to_all(
        jnp.broadcast_to(sums[None], (shards,) + sums.shape), "seq", 0, 0, tiled=True
    )
    video_id = lax.axis_index("dp").astype(jnp.int32).reshape(1)
    parts, qt, loss = scales(sums, packed, blend, video_id, slots)
    parts = lax.all_to_all(parts, "dp", 0, 0, tiled=True)
    video_grad = keys(qt, expo, float(frames * P_SIZE)).reshape(1, frames, patch_loc, E)
    summed = jnp.sum(parts.astype(F32), axis=0).astype(BF16)
    summed = lax.all_to_all(
        jnp.broadcast_to(summed[None], (shards,) + summed.shape), "seq", 0, 0, tiled=True
    )
    total = jnp.sum(summed.astype(F32), axis=0)
    query_grad = (slots * total).astype(BF16).reshape(query_dev, slots, E)
    pair_loss = loss[:, ::slots].reshape(-1, 1)
    return (video_grad, query_grad, pair_loss)


def solution(mesh):
    placed = (
        P("dp", "seq", None, None),
        P(),
        P(),
        P(),
        P(),
        P(),
        P("dp", None, None),
        P("dp"),
        P("dp"),
    )
    return jax.shard_map(
        body,
        mesh=mesh,
        in_specs=placed,
        out_specs=(P("dp", None, "seq", None), P("dp", None, None), P(None, "dp")),
        check_vma=False,
    )
```

```python
import jax
import jax.numpy as jnp
from jax import lax
from jax.experimental import pallas as pl
from jax.experimental.pallas import tpu as pltpu
from jax.sharding import PartitionSpec as P

HEADS = 12
P_SIZE = 256
TEMPER = 0.05
SLOPE = 10.0
OFFSET = -5.0
SHARP = 10.0
LOG2E = 1.4426950408889634

D = 768
HEAD = D // HEADS
PAIR = 2 * HEAD
PAIRS = HEADS // 2
TILE = 256
SUB = 128
E = 128
F32 = jnp.float32
BF16 = jnp.bfloat16
VMEM = pl.BlockSpec(memory_space=pltpu.VMEM)
SMEM = pl.BlockSpec(memory_space=pltpu.SMEM)
HBM = pl.BlockSpec(memory_space=pltpu.HBM)


def limit(mib):
    return pltpu.CompilerParams(vmem_limit_bytes=mib * 2**20)


def dot(a, b):
    return lax.dot_general(a, b, (((1,), (0,)), ((), ())), preferred_element_type=F32)


def dot_t(a, b):
    return lax.dot_general(a, b, (((1,), (1,)), ((), ())), preferred_element_type=F32)


def iota(shape, dim):
    return lax.broadcasted_iota(jnp.int32, shape, dim)


def layer_norm(tokens):
    values = tokens.astype(F32)
    center = values - jnp.mean(values, axis=-1, keepdims=True)
    spread = jnp.mean(center * center, axis=-1, keepdims=True)
    return (center * lax.rsqrt(spread + 1e-05)).astype(BF16)


def unit_heads(values, gain):
    same = (iota((TILE, TILE), 0) // HEAD == iota((TILE, TILE), 1) // HEAD).astype(BF16)
    parts = []
    for at in range(0, values.shape[1], TILE):
        part = values[:, at : at + TILE]
        squares = dot((part * part).astype(BF16), same)
        parts.append((part * (lax.rsqrt(squares + 1e-06) * gain)).astype(BF16))
    return jnp.concatenate(parts, axis=1)


def qkv_rows(tokens, weight_ref):
    packed = dot(layer_norm(tokens), weight_ref[...])
    query = unit_heads(packed[:, :D], SHARP * LOG2E)
    key = unit_heads(packed[:, D : 2 * D], 1.0)
    return query, key, packed[:, 2 * D :].astype(BF16)


def pair_blend(query, key, value, keep):
    extent = key.shape[0]
    low = iota((extent, PAIR), 1) < HEAD
    zero = jnp.zeros((extent, PAIR), BF16)
    one = jnp.ones((extent, PAIR), BF16)
    keys = jnp.concatenate([jnp.where(low, key, zero), jnp.where(low, zero, key)], axis=0)
    values = jnp.concatenate(
        [
            jnp.concatenate([jnp.where(low, value, zero), jnp.where(low, one, zero)], axis=1),
            jnp.concatenate([jnp.where(low, zero, value), jnp.where(low, zero, one)], axis=1),
        ],
        axis=0,
    )
    weights = jnp.exp2(dot_t(query, keys))
    if keep is not None:
        weights = jnp.where(keep, weights, 0.0)
    mixed = dot(weights.astype(BF16), values)
    return (mixed[:, :PAIR] / mixed[:, PAIR:]).astype(BF16)


def space_kernel(video_ref, qkv_ref, out_w_ref, out_ref):
    tokens = video_ref[0]
    query, key, value = qkv_rows(tokens, qkv_ref)
    blended = []
    for pair in range(PAIRS):
        at = slice(pair * PAIR, (pair + 1) * PAIR)
        blended.append(pair_blend(query[:, at], key[:, at], value[:, at], None))
    update = dot(jnp.concatenate(blended, axis=1), out_w_ref[...])
    result = (tokens.astype(F32) + update).astype(BF16)
    out_ref[...] = result.reshape(out_ref.shape)


def space(video, qkv_weight, out_weight, shards):
    frames, patches, _ = video.shape
    local = patches // shards
    return pl.pallas_call(
        space_kernel,
        grid=(frames,),
        in_specs=[
            pl.BlockSpec((1, patches, D), lambda f: (f, 0, 0)),
            pl.BlockSpec((D, 3 * D), lambda f: (0, 0)),
            pl.BlockSpec((D, D), lambda f: (0, 0)),
        ],
        out_specs=pl.BlockSpec((shards, 1, local, D), lambda f: (0, f, 0, 0)),
        out_shape=jax.ShapeDtypeStruct((shards, frames, local, D), BF16),
        compiler_params=limit(28),
        name="space",
    )(video, qkv_weight, out_weight)


def swap_rows(rows, side):
    extent = side * side
    row, col = iota((extent, extent), 0), iota((extent, extent), 1)
    swap = (col == (row % side) * side + row // side).astype(BF16)
    return dot(swap, rows).astype(BF16)


def time_kernel(x_ref, qkv_ref, out_w_ref, proj_ref, khat_ref, x_s, q_s, k_s, v_s, kh_s):
    step = pl.program_id(0)
    side = x_s.shape[0]
    tiles = pl.num_programs(0) // 2
    groups = TILE // x_s.shape[1]

    @pl.when(step < tiles)
    def _():
        tokens = swap_rows(x_ref[...], side)
        query, key, value = qkv_rows(tokens, qkv_ref)
        at = pl.ds(pl.multiple_of(step * side, side), side)
        x_s[:, at, :] = tokens.reshape(side, side, D)
        q_s[:, at, :] = query.reshape(side, side, D)
        k_s[:, at, :] = key.reshape(side, side, D)
        v_s[:, at, :] = value.reshape(side, side, D)

    @pl.when(step >= tiles)
    def _():
        at = pl.ds((step - tiles) * groups, groups)
        extent = x_s.shape[1]
        query = q_s[at].reshape(TILE, D)
        key = k_s[at].reshape(TILE, D)
        value = v_s[at].reshape(TILE, D)
        keep = iota((SUB, 2 * SUB), 0) // extent == (iota((SUB, 2 * SUB), 1) % SUB) // extent
        rows = []
        for sub in range(TILE // SUB):
            down = slice(sub * SUB, (sub + 1) * SUB)
            cols = []
            for pair in range(PAIRS):
                across = slice(pair * PAIR, (pair + 1) * PAIR)
                cols.append(
                    pair_blend(query[down, across], key[down, across], value[down, across], keep)
                )
            rows.append(jnp.concatenate(cols, axis=1))
        update = dot(jnp.concatenate(rows, axis=0), out_w_ref[...])
        tokens = x_s[at].reshape(TILE, D)
        mixed = (tokens.astype(F32) + update).astype(BF16)
        projected = dot(layer_norm(mixed), proj_ref[...])
        norm = jnp.sum(projected * projected, axis=-1, keepdims=True)
        unit = (projected * lax.rsqrt(norm + 1e-06)).astype(BF16)
        kh_s[at] = unit.reshape(groups, extent, E)

    @pl.when(step == 2 * tiles - 1)
    def _():
        for tile in range(khat_ref.shape[0] // TILE):
            rows = kh_s[:, tile * side : (tile + 1) * side, :].reshape(TILE, E)
            khat_ref[tile * TILE : (tile + 1) * TILE, :] = swap_rows(rows, side)


def time(x, qkv_weight, out_weight, proj_weight, patches):
    rows = x.shape[0]
    frames = rows // patches
    tiles = rows // TILE
    whole = lambda s: (0, 0)
    return pl.pallas_call(
        time_kernel,
        grid=(2 * tiles,),
        in_specs=[
            pl.BlockSpec((TILE, D), lambda s: (jnp.minimum(s, tiles - 1), 0)),
            pl.BlockSpec((D, 3 * D), whole),
            pl.BlockSpec((D, D), whole),
            pl.BlockSpec((D, E), whole),
        ],
        out_specs=pl.BlockSpec((rows, E), whole),
        out_shape=jax.ShapeDtypeStruct((rows, E), BF16),
        scratch_shapes=[pltpu.VMEM((patches, frames, D), BF16)] * 4
        + [pltpu.VMEM((patches, frames, E), BF16)],
        compiler_params=limit(32),
        name="time",
    )(x, qkv_weight, out_weight, proj_weight)


EXTRA = 16


def query_kernel(len_ref, pos_ref, q_ref, out_ref):
    rows = q_ref.shape[0]
    values = q_ref[...].astype(F32)
    norm = jnp.sum(values * values, axis=-1, keepdims=True)
    out_ref[:rows, :] = (values / jnp.sqrt(norm + 1e-06)).astype(BF16)
    slots = rows // len_ref.shape[0]
    row, lane = iota((EXTRA, E), 0), iota((EXTRA, E), 1)
    owner = ((row % 2) * E + lane) // slots
    extra = jnp.zeros((EXTRA, E), F32)
    for query in range(len_ref.shape[0]):
        picked = jnp.where(row < 2, len_ref[query], pos_ref[query]).astype(F32)
        extra = jnp.where((owner == query) & (row < 4), picked, extra)
    out_ref[rows:, :] = extra.astype(BF16)


def pack_queries(queries, query_len, positive):
    rows = queries.shape[0]
    return pl.pallas_call(
        query_kernel,
        in_specs=[SMEM, SMEM, VMEM],
        out_specs=VMEM,
        out_shape=jax.ShapeDtypeStruct((rows + EXTRA, E), BF16),
        name="pack_queries",
    )(query_len, positive, queries)


def terms_kernel(blocks, at_ref, khat_ref, *refs):
    packed_refs = refs[:blocks]
    expo_ref, keep_ref, send_ref, sums_ref, expo_s, sem = refs[blocks:]
    rows = packed_refs[0].shape[0] - EXTRA
    first = at_ref[1] == 0
    khat = khat_ref[...]
    wide = jnp.concatenate([khat, jnp.ones_like(khat)], axis=1)
    gain = LOG2E / TEMPER
    eye = iota((E, E), 0) == iota((E, E), 1)
    sums = []
    for block in range(blocks):
        dots = dot_t(packed_refs[block][:rows, :], khat)
        expo = jnp.exp2(dots * gain - gain).astype(BF16)
        expo_s[block] = expo
        pltpu.make_async_copy(expo_s.at[block], expo_ref.at[block], sem.at[block]).start()
        both = dot(expo, wide)
        low, high = both[:E, :E], both[E:, :E]
        keep_ref[block] = jnp.where(first, low, high)
        send_ref[block] = jnp.where(first, high, low).astype(BF16)
        for part in range(rows // E):
            square = both[part * E : (part + 1) * E, E:]
            sums.append(jnp.sum(jnp.where(eye, square, 0.0), axis=0, keepdims=True))
    sums = jnp.concatenate(sums, axis=0)
    for copy in range(sums_ref.shape[0]):
        sums_ref[copy] = sums
    for block in range(blocks):
        pltpu.make_async_copy(expo_s.at[block], expo_ref.at[block], sem.at[block]).wait()


def terms(packed, khat, place, shards):
    blocks, rows = len(packed), packed[0].shape[0] - EXTRA
    tokens = khat.shape[0]
    return pl.pallas_call(
        lambda *refs: terms_kernel(blocks, *refs),
        in_specs=[SMEM] + [VMEM] * (1 + blocks),
        out_specs=[HBM] + [VMEM] * 3,
        out_shape=[
            pltpu.HBM((blocks, rows, tokens), BF16),
            jax.ShapeDtypeStruct((blocks, rows // 2, E), F32),
            jax.ShapeDtypeStruct((blocks, rows // 2, E), BF16),
            jax.ShapeDtypeStruct((shards, blocks * rows // E, E), F32),
        ],
        scratch_shapes=[
            pltpu.VMEM((blocks, rows, tokens), BF16),
            pltpu.SemaphoreType.DMA((blocks,)),
        ],
        compiler_params=limit(16),
        name="terms",
    )(place, khat, *packed)


def scale_kernel(slots, blocks, at_ref, sums_ref, keep_ref, got_ref, *refs):
    packed_refs, (part_ref, scale_ref, loss_ref) = refs[:blocks], refs[blocks:]
    rows = packed_refs[0].shape[0] - EXTRA
    per = rows // E
    total = jnp.sum(sums_ref[...], axis=0)
    notes = [packed_refs[b][rows:, :].astype(F32) for b in range(blocks)]
    lens = jnp.concatenate([note[:per] for note in notes], axis=0)
    pos = jnp.concatenate([note[per : 2 * per] for note in notes], axis=0)
    mask = ((iota(total.shape, 1) % slots).astype(F32) < lens).astype(F32)
    smooth = (1.0 + TEMPER * jnp.log(total)) * mask
    same = (iota((E, E), 0) // slots == iota((E, E), 1) // slots).astype(F32)
    score = (
        lax.dot_general(
            smooth,
            same,
            (((1,), (0,)), ((), ())),
            preferred_element_type=F32,
            precision=lax.Precision.HIGHEST,
        )
        / lens
    )
    sign = jnp.where(pos == at_ref[0].astype(F32), 1.0, -1.0)
    margin = sign * (SLOPE * score + OFFSET)
    loss = jnp.maximum(-margin, 0.0) + jnp.log1p(jnp.exp(-jnp.abs(margin)))
    coeff = -SLOPE * sign / (1.0 + jnp.exp(margin)) * mask / lens
    scale = (coeff / total).T
    scale_ref[...] = scale
    first = at_ref[1] == 0
    for block in range(blocks):
        group = lax.rem(at_ref[0] + blocks - block, blocks)
        at = block * per
        column = jnp.where(first, scale[:, at : at + 1], scale[:, at + 1 : at + 2])
        part_ref[group] = ((keep_ref[block] + got_ref[block].astype(F32)) * column).astype(BF16)
        loss_ref[group] = loss[at : at + per]


def scales(sums, keep, got, packed, place, slots):
    blocks, rows = len(packed), packed[0].shape[0] - EXTRA
    return pl.pallas_call(
        lambda *refs: scale_kernel(slots, blocks, *refs),
        in_specs=[SMEM] + [VMEM] * (3 + blocks),
        out_specs=[VMEM] * 3,
        out_shape=[
            jax.ShapeDtypeStruct(keep.shape, BF16),
            jax.ShapeDtypeStruct((E, blocks * rows // E), F32),
            jax.ShapeDtypeStruct((blocks, rows // E, E), F32),
        ],
        compiler_params=limit(8),
        name="scales",
    )(place, sums, keep, got, *packed)


def keys_kernel(gain, blocks, scale_ref, expo_ref, *refs):
    packed_refs, (out_ref, expo_s, sem) = refs[:blocks], refs[blocks:]
    for block in range(blocks):
        pltpu.make_async_copy(expo_ref.at[block], expo_s.at[block], sem.at[block]).start()
    rows = packed_refs[0].shape[0] - EXTRA
    per = rows // E
    total = jnp.zeros((E, expo_ref.shape[2]), F32)
    for block in range(blocks):
        parts = []
        for part in range(per):
            at = block * per + part
            query = packed_refs[block][part * E : (part + 1) * E, :].astype(F32)
            parts.append((query * scale_ref[:, at : at + 1]).T.astype(BF16))
        pltpu.make_async_copy(expo_ref.at[block], expo_s.at[block], sem.at[block]).wait()
        total = total + dot(jnp.concatenate(parts, axis=1), expo_s[block])
    out_ref[...] = (total.T * gain).astype(BF16)


def keys(scale, expo, packed, gain):
    tokens = expo.shape[2]
    return pl.pallas_call(
        lambda *refs: keys_kernel(gain, len(packed), *refs),
        in_specs=[VMEM, HBM] + [VMEM] * len(packed),
        out_specs=VMEM,
        out_shape=jax.ShapeDtypeStruct((tokens, E), BF16),
        scratch_shapes=[
            pltpu.VMEM(expo.shape, BF16),
            pltpu.SemaphoreType.DMA((len(packed),)),
        ],
        compiler_params=limit(16),
        name="keys",
    )(scale, pltpu.with_memory_space_constraint(expo, pltpu.HBM), *packed)


def fold_kernel(gain, in_ref, out_ref):
    total = jnp.sum(in_ref[...].astype(F32), axis=0) * gain
    for copy in range(out_ref.shape[0]):
        out_ref[copy] = total.astype(BF16)


def fold(parts, gain, copies):
    return pl.pallas_call(
        lambda *refs: fold_kernel(gain, *refs),
        in_specs=[VMEM],
        out_specs=VMEM,
        out_shape=jax.ShapeDtypeStruct((copies,) + parts.shape[1:], BF16),
        compiler_params=limit(4),
        name="fold",
    )(parts)


def body(
    video, space_qkv, space_out, time_qkv, time_out, proj_weight, queries, query_len, positive
):
    _, frames_dev, patches, _ = video.shape
    shards = lax.axis_size("seq")
    blocks = lax.axis_size("dp")
    patch_loc = patches // shards
    frames = frames_dev * shards
    query_dev, slots, _ = queries.shape
    rows = query_dev * slots
    core = lax.rem(lax.axis_index("seq"), 2)
    place = jnp.stack([lax.axis_index("dp"), core]).astype(jnp.int32)
    partner = [(i, i ^ 1) for i in range(shards)]
    chips = [[2 * chip + own for chip in range(shards // 2)] for own in range(2)]

    spatial = space(video[0], space_qkv, space_out, shards)
    spatial, flat = lax.optimization_barrier((spatial, queries.reshape(rows, E)))
    items = lax.all_to_all(spatial, "seq", 0, 0, tiled=True)
    mine = pack_queries(flat, query_len, positive)
    packed = [mine] + [
        lax.ppermute(mine, "dp", [(i, (i + by) % blocks) for i in range(blocks)])
        for by in range(1, blocks)
    ]
    khat = time(items.reshape(-1, D), time_qkv, time_out, proj_weight, patch_loc)

    expo, keep, send, sums = terms(packed, khat, place, shards)
    sums = lax.all_to_all(sums, "seq", 0, 0, tiled=True)
    got = lax.ppermute(send, "seq", partner)
    parts, scale, loss = scales(sums, keep, got, packed, place, slots)
    parts = lax.all_to_all(parts, "dp", 0, 0, tiled=True)
    video_grad = keys(scale, expo, packed, float(frames * P_SIZE))
    halves = fold(parts, 1.0, shards // 2)
    halves = lax.all_to_all(halves, "seq", 0, 0, tiled=True, axis_index_groups=chips)
    halves, video_grad = lax.optimization_barrier((halves, video_grad))
    half = fold(halves, float(slots), 1)[0]
    other = lax.ppermute(half, "seq", partner)
    first = core == 0
    query_grad = jnp.concatenate(
        [jnp.where(first, half, other), jnp.where(first, other, half)], axis=0
    )
    return (
        video_grad.reshape(1, frames, patch_loc, E),
        query_grad.reshape(query_dev, slots, E),
        loss[:, :, ::slots].reshape(-1, 1),
    )


def solution(mesh):
    placed = (
        P("dp", "seq", None, None),
        P(),
        P(),
        P(),
        P(),
        P(),
        P("dp", None, None),
        P("dp"),
        P("dp"),
    )
    return jax.shard_map(
        body,
        mesh=mesh,
        in_specs=placed,
        out_specs=(P("dp", None, "seq", None), P("dp", None, None), P(None, "dp")),
        check_vma=False,
    )
```

```python
import jax
import jax.numpy as jnp
from jax import lax
from jax.experimental import pallas as pl
from jax.experimental.pallas import tpu as pltpu
from jax.sharding import PartitionSpec as P

HEADS = 12
P_SIZE = 256
TEMPER = 0.05
SLOPE = 10.0
OFFSET = -5.0
SHARP = 10.0
LOG2E = 1.4426950408889634

D = 768
HEAD = D // HEADS
PAIR = 2 * HEAD
PAIRS = HEADS // 2
TILE = 256
SUB = 128
E = 128
F32 = jnp.float32
BF16 = jnp.bfloat16
VMEM = pl.BlockSpec(memory_space=pltpu.VMEM)
SMEM = pl.BlockSpec(memory_space=pltpu.SMEM)
HBM = pl.BlockSpec(memory_space=pltpu.HBM)


def limit(mib):
    return pltpu.CompilerParams(vmem_limit_bytes=mib * 2**20)


def dot(a, b):
    return lax.dot_general(a, b, (((1,), (0,)), ((), ())), preferred_element_type=F32)


def dot_t(a, b):
    return lax.dot_general(a, b, (((1,), (1,)), ((), ())), preferred_element_type=F32)


def iota(shape, dim):
    return lax.broadcasted_iota(jnp.int32, shape, dim)


def layer_norm(tokens):
    values = tokens.astype(F32)
    center = values - jnp.mean(values, axis=-1, keepdims=True)
    spread = jnp.mean(center * center, axis=-1, keepdims=True)
    return (center * lax.rsqrt(spread + 1e-05)).astype(BF16)


def unit_heads(values, gain):
    same = (iota((TILE, TILE), 0) // HEAD == iota((TILE, TILE), 1) // HEAD).astype(BF16)
    parts = []
    for at in range(0, values.shape[1], TILE):
        part = values[:, at : at + TILE]
        squares = dot((part * part).astype(BF16), same)
        parts.append((part * (lax.rsqrt(squares + 1e-06) * gain)).astype(BF16))
    return jnp.concatenate(parts, axis=1)


def pair_blend(query, key, value, keep):
    extent = key.shape[0]
    low = iota((extent, PAIR), 1) < HEAD
    zero = jnp.zeros((extent, PAIR), BF16)
    one = jnp.ones((extent, PAIR), BF16)
    keys = jnp.concatenate([jnp.where(low, key, zero), jnp.where(low, zero, key)], axis=0)
    values = jnp.concatenate(
        [
            jnp.concatenate([jnp.where(low, value, zero), jnp.where(low, one, zero)], axis=1),
            jnp.concatenate([jnp.where(low, zero, value), jnp.where(low, zero, one)], axis=1),
        ],
        axis=0,
    )
    weights = jnp.exp2(dot_t(query, keys))
    if keep is not None:
        weights = jnp.where(keep, weights, 0.0)
    mixed = dot(weights.astype(BF16), values)
    return (mixed[:, :PAIR] / mixed[:, PAIR:]).astype(BF16)


def fetch(pairs, sem):
    copies = [pltpu.make_async_copy(a, b, sem.at[i]) for i, (a, b) in enumerate(pairs)]
    for copy in copies:
        copy.start()
    return copies


def columns(ref, third):
    return ref.at[:, pl.ds(third * D, D)]


def in_hbm(*arrays):
    return [pltpu.with_memory_space_constraint(array, pltpu.HBM) for array in arrays]


def qkv_all(normed, weight_s, copies, outs):
    for third, (out, gain) in enumerate(zip(outs, (SHARP * LOG2E, 1.0, None))):
        copies[third].wait()
        part = dot(normed, weight_s[:, third * D : (third + 1) * D])
        out[...] = part.astype(BF16) if gain is None else unit_heads(part, gain)


def space_kernel(
    video_ref, qkv_ref, out_w_ref, out_ref, x_s, qkv_s, w_s, n_s, q_s, k_s, v_s, y_s, sem, out_sem
):
    frames, patches, _ = x_s.shape
    video = fetch([(video_ref.at[f], x_s.at[f]) for f in range(frames)], sem)
    weights = fetch(
        [(columns(qkv_ref, i), columns(qkv_s, i)) for i in range(3)] + [(out_w_ref, w_s)],
        sem.at[pl.ds(frames, 4)],
    )
    for f in range(frames):
        video[f].wait()
        n_s[f * patches : (f + 1) * patches, :] = layer_norm(x_s[f])
    qkv_all(n_s[...], qkv_s, weights, (q_s, k_s, v_s))
    weights[3].wait()
    stores = []
    for f in range(frames):
        down = slice(f * patches, (f + 1) * patches)
        blended = []
        for pair in range(PAIRS):
            at = slice(pair * PAIR, (pair + 1) * PAIR)
            blended.append(pair_blend(q_s[down, at], k_s[down, at], v_s[down, at], None))
        update = dot(jnp.concatenate(blended, axis=1), w_s[...])
        y_s[f] = (x_s[f].astype(F32) + update).astype(BF16).reshape(y_s.shape[1:])
        stores.append(pltpu.make_async_copy(y_s.at[f], out_ref.at[:, f], out_sem.at[f]))
        stores[-1].start()
    for store in stores:
        store.wait()


def space(video, qkv_weight, out_weight, shards):
    frames, patches, _ = video.shape
    local = patches // shards
    return pl.pallas_call(
        space_kernel,
        in_specs=[HBM] * 3,
        out_specs=HBM,
        out_shape=pltpu.HBM((shards, frames, local, D), BF16),
        scratch_shapes=[
            pltpu.VMEM((frames, patches, D), BF16),
            pltpu.VMEM((D, 3 * D), BF16),
            pltpu.VMEM((D, D), BF16),
        ]
        + [pltpu.VMEM((frames * patches, D), BF16)] * 4
        + [
            pltpu.VMEM((frames, shards, local, D), BF16),
            pltpu.SemaphoreType.DMA((frames + 4,)),
            pltpu.SemaphoreType.DMA((frames,)),
        ],
        compiler_params=limit(40),
        name="space",
    )(*in_hbm(video, qkv_weight, out_weight))


def swap_rows(rows, side):
    extent = side * side
    row, col = iota((extent, extent), 0), iota((extent, extent), 1)
    swap = (col == (row % side) * side + row // side).astype(BF16)
    return dot(swap, rows).astype(BF16)


def time_kernel(
    x_ref, qkv_ref, out_w_ref, proj_ref, khat_ref,
    x_s, n_s, qkv_s, w_s, p_s, q_s, k_s, v_s, b_s, kh_s, sem,
):
    side, frames, _ = x_s.shape
    rows = x_ref.shape[0]
    weights = fetch(
        [(columns(qkv_ref, i), columns(qkv_s, i)) for i in range(3)]
        + [(out_w_ref, w_s), (proj_ref, p_s)],
        sem,
    )
    for tile in range(rows // TILE):
        tokens = swap_rows(x_ref[tile * TILE : (tile + 1) * TILE, :], side)
        at = slice(tile * side, (tile + 1) * side)
        x_s[:, at, :] = tokens.reshape(side, side, D)
        n_s[:, at, :] = layer_norm(tokens).reshape(side, side, D)
    qkv_all(n_s[...].reshape(rows, D), qkv_s, weights, (q_s, k_s, v_s))
    keep = iota((SUB, 2 * SUB), 0) // frames == (iota((SUB, 2 * SUB), 1) % SUB) // frames
    for sub in range(rows // SUB):
        down = slice(sub * SUB, (sub + 1) * SUB)
        for pair in range(PAIRS):
            at = slice(pair * PAIR, (pair + 1) * PAIR)
            b_s[down, at] = pair_blend(q_s[down, at], k_s[down, at], v_s[down, at], keep)
    weights[3].wait()
    weights[4].wait()
    update = dot(b_s[...], w_s[...])
    mixed = (x_s[...].reshape(rows, D).astype(F32) + update).astype(BF16)
    projected = dot(layer_norm(mixed), p_s[...])
    norm = jnp.sum(projected * projected, axis=-1, keepdims=True)
    kh_s[...] = (projected * lax.rsqrt(norm + 1e-06)).astype(BF16).reshape(kh_s.shape)
    for tile in range(rows // TILE):
        part = kh_s[:, tile * side : (tile + 1) * side, :].reshape(TILE, E)
        khat_ref[tile * TILE : (tile + 1) * TILE, :] = swap_rows(part, side)


def time(x, qkv_weight, out_weight, proj_weight, patches):
    rows = x.shape[0]
    frames = rows // patches
    return pl.pallas_call(
        time_kernel,
        in_specs=[VMEM] + [HBM] * 3,
        out_specs=VMEM,
        out_shape=jax.ShapeDtypeStruct((rows, E), BF16),
        scratch_shapes=[
            pltpu.VMEM((patches, frames, D), BF16),
            pltpu.VMEM((patches, frames, D), BF16),
            pltpu.VMEM((D, 3 * D), BF16),
            pltpu.VMEM((D, D), BF16),
            pltpu.VMEM((D, E), BF16),
        ]
        + [pltpu.VMEM((rows, D), BF16)] * 4
        + [pltpu.VMEM((patches, frames, E), BF16), pltpu.SemaphoreType.DMA((5,))],
        compiler_params=limit(40),
        name="time",
    )(x, *in_hbm(qkv_weight, out_weight, proj_weight))


EXTRA = 16


def query_kernel(len_ref, pos_ref, q_ref, out_ref):
    rows = q_ref.shape[0]
    values = q_ref[...].astype(F32)
    norm = jnp.sum(values * values, axis=-1, keepdims=True)
    out_ref[:rows, :] = (values / jnp.sqrt(norm + 1e-06)).astype(BF16)
    slots = rows // len_ref.shape[0]
    row, lane = iota((EXTRA, E), 0), iota((EXTRA, E), 1)
    owner = ((row % 2) * E + lane) // slots
    extra = jnp.zeros((EXTRA, E), F32)
    for query in range(len_ref.shape[0]):
        picked = jnp.where(row < 2, len_ref[query], pos_ref[query]).astype(F32)
        extra = jnp.where((owner == query) & (row < 4), picked, extra)
    out_ref[rows:, :] = extra.astype(BF16)


def pack_queries(queries, query_len, positive):
    rows = queries.shape[0]
    return pl.pallas_call(
        query_kernel,
        in_specs=[SMEM, SMEM, VMEM],
        out_specs=VMEM,
        out_shape=jax.ShapeDtypeStruct((rows + EXTRA, E), BF16),
        name="pack_queries",
    )(query_len, positive, queries)


def group_of(mine, blocks, block):
    return lax.rem(mine + blocks - block // 2 * 2, blocks) ^ (block % 2)


def terms_kernel(blocks, at_ref, khat_ref, *refs):
    packed_refs = refs[: blocks // 2]
    expo_ref, keep_ref, send_ref, sums_ref, expo_s, sem = refs[blocks // 2 :]
    rows = expo_s.shape[1]
    first = at_ref[1] == 0
    khat = khat_ref[...]
    wide = jnp.concatenate([khat, jnp.ones_like(khat)], axis=1)
    gain = LOG2E / TEMPER
    eye = iota((E, E), 0) == iota((E, E), 1)
    sums = []
    for block in range(blocks):
        dots = dot_t(packed_refs[block // 2][block % 2, :rows, :], khat)
        expo = jnp.exp2(dots * gain - gain).astype(BF16)
        expo_s[block] = expo
        pltpu.make_async_copy(expo_s.at[block], expo_ref.at[block], sem.at[block]).start()
        both = dot(expo, wide)
        low, high = both[:E, :E], both[E:, :E]
        keep_ref[block] = jnp.where(first, low, high)
        send_ref[block] = jnp.where(first, high, low).astype(BF16)
        for part in range(rows // E):
            square = both[part * E : (part + 1) * E, E:]
            sums.append(jnp.sum(jnp.where(eye, square, 0.0), axis=0, keepdims=True))
    sums_ref[...] = jnp.concatenate(sums, axis=0)
    for block in range(blocks):
        pltpu.make_async_copy(expo_s.at[block], expo_ref.at[block], sem.at[block]).wait()


def terms(packed, khat, place):
    blocks, rows = 2 * len(packed), packed[0].shape[1] - EXTRA
    tokens = khat.shape[0]
    return pl.pallas_call(
        lambda *refs: terms_kernel(blocks, *refs),
        in_specs=[SMEM] + [VMEM] * (1 + len(packed)),
        out_specs=[HBM] + [VMEM] * 3,
        out_shape=[
            pltpu.HBM((blocks, rows, tokens), BF16),
            jax.ShapeDtypeStruct((blocks, rows // 2, E), F32),
            jax.ShapeDtypeStruct((blocks, rows // 2, E), BF16),
            jax.ShapeDtypeStruct((blocks * rows // E, E), F32),
        ],
        scratch_shapes=[
            pltpu.VMEM((blocks, rows, tokens), BF16),
            pltpu.SemaphoreType.DMA((blocks,)),
        ],
        compiler_params=limit(16),
        name="terms",
    )(place, khat, *packed)


def join_kernel(keep_ref, got_ref, sums_ref, others_ref, out_ref):
    blocks, half, _ = keep_ref.shape
    chips = out_ref.shape[0]
    piece = half // chips
    sums = sums_ref[...] + others_ref[...]
    upper = sums.astype(BF16)
    lower = (sums - upper.astype(F32)).astype(BF16)
    notes = jnp.concatenate([upper, lower], axis=0)
    for block in range(blocks):
        both = (keep_ref[block] + got_ref[block].astype(F32)).astype(BF16)
        for chip in range(chips):
            out_ref[chip, block * piece : (block + 1) * piece, :] = both[
                chip * piece : (chip + 1) * piece
            ]
    for chip in range(chips):
        out_ref[chip, blocks * piece :, :] = notes


def join(keep, got, sums, others, chips):
    blocks, half, _ = keep.shape
    return pl.pallas_call(
        join_kernel,
        in_specs=[VMEM] * 4,
        out_specs=VMEM,
        out_shape=jax.ShapeDtypeStruct(
            (chips, blocks * half // chips + 2 * sums.shape[0], E), BF16
        ),
        compiler_params=limit(8),
        name="join",
    )(keep, got, sums, others)


def scale_kernel(slots, at_ref, got_ref, *refs):
    packed_refs, (part_ref, scale_ref, loss_ref) = refs[:-3], refs[-3:]
    blocks, shards, piece, _ = part_ref.shape
    rows = packed_refs[0].shape[1] - EXTRA
    per = rows // E
    got = jnp.sum(got_ref[...].astype(F32), axis=0)
    blend, notes = got[: blocks * piece], got[blocks * piece :]
    total = notes[: blocks * per] + notes[blocks * per :]
    notes = [packed_refs[b // 2][b % 2, rows:, :].astype(F32) for b in range(blocks)]
    lens = jnp.concatenate([note[:per] for note in notes], axis=0)
    pos = jnp.concatenate([note[per : 2 * per] for note in notes], axis=0)
    mask = ((iota(total.shape, 1) % slots).astype(F32) < lens).astype(F32)
    smooth = (1.0 + TEMPER * jnp.log(total)) * mask
    same = (iota((E, E), 0) // slots == iota((E, E), 1) // slots).astype(F32)
    score = (
        lax.dot_general(
            smooth,
            same,
            (((1,), (0,)), ((), ())),
            preferred_element_type=F32,
            precision=lax.Precision.HIGHEST,
        )
        / lens
    )
    sign = jnp.where(pos == at_ref[0].astype(F32), 1.0, -1.0)
    margin = sign * (SLOPE * score + OFFSET)
    loss = jnp.maximum(-margin, 0.0) + jnp.log1p(jnp.exp(-jnp.abs(margin)))
    coeff = -SLOPE * sign / (1.0 + jnp.exp(margin)) * mask / lens
    scale_ref[...] = (coeff / total).T
    scale = scale_ref[pl.ds(pl.multiple_of(at_ref[2] * piece, piece), piece), :]
    first = at_ref[1] == 0
    for block in range(blocks):
        group = group_of(at_ref[0], blocks, block)
        at = block * per
        column = jnp.where(first, scale[:, at : at + 1], scale[:, at + 1 : at + 2])
        part = (blend[block * piece : (block + 1) * piece] * column).astype(BF16)
        for shard in range(shards):
            part_ref[group, shard] = part
        loss_ref[group] = loss[at : at + per]


def scales(got, packed, place, slots, shards):
    blocks, rows = 2 * len(packed), packed[0].shape[1] - EXTRA
    piece = rows // shards
    return pl.pallas_call(
        lambda *refs: scale_kernel(slots, *refs),
        in_specs=[SMEM] + [VMEM] * (1 + len(packed)),
        out_specs=[VMEM] * 3,
        out_shape=[
            jax.ShapeDtypeStruct((blocks, shards, piece, E), BF16),
            jax.ShapeDtypeStruct((E, blocks * rows // E), F32),
            jax.ShapeDtypeStruct((blocks, rows // E, E), F32),
        ],
        compiler_params=limit(8),
        name="scales",
    )(place, got, *packed)


def keys_kernel(gain, blocks, scale_ref, expo_ref, *refs):
    packed_refs, (out_ref, expo_s, sem) = refs[:-3], refs[-3:]
    copies = fetch([(expo_ref.at[b], expo_s.at[b]) for b in range(blocks)], sem)
    rows = expo_s.shape[1]
    per = rows // E
    total = jnp.zeros((E, expo_s.shape[2]), F32)
    for block in range(blocks):
        parts = []
        for part in range(per):
            at = block * per + part
            down = slice(part * E, (part + 1) * E)
            query = packed_refs[block // 2][block % 2, down, :].astype(F32)
            parts.append((query * scale_ref[:, at : at + 1]).T.astype(BF16))
        copies[block].wait()
        total = total + dot(jnp.concatenate(parts, axis=1), expo_s[block])
    out_ref[...] = (total.T * gain).astype(BF16)


def keys(scale, expo, packed, gain):
    blocks, _, tokens = expo.shape
    return pl.pallas_call(
        lambda *refs: keys_kernel(gain, blocks, *refs),
        in_specs=[VMEM, HBM] + [VMEM] * len(packed),
        out_specs=VMEM,
        out_shape=jax.ShapeDtypeStruct((tokens, E), BF16),
        scratch_shapes=[
            pltpu.VMEM(expo.shape, BF16),
            pltpu.SemaphoreType.DMA((blocks,)),
        ],
        compiler_params=limit(16),
        name="keys",
    )(scale, *in_hbm(expo), *packed)


def total_kernel(gain, in_ref, out_ref):
    _, shards, piece, _ = in_ref.shape
    total = (jnp.sum(in_ref[...].astype(F32), axis=0) * gain).astype(BF16)
    for shard in range(shards):
        at = (shard % 2) * (shards // 2) + shard // 2
        out_ref[at * piece : (at + 1) * piece, :] = total[shard]


def totals(parts, gain):
    _, shards, piece, _ = parts.shape
    return pl.pallas_call(
        lambda *refs: total_kernel(gain, *refs),
        in_specs=[VMEM],
        out_specs=VMEM,
        out_shape=jax.ShapeDtypeStruct((shards * piece, E), BF16),
        compiler_params=limit(4),
        name="totals",
    )(parts)


def body(
    video, space_qkv, space_out, time_qkv, time_out, proj_weight, queries, query_len, positive
):
    _, frames_dev, patches, _ = video.shape
    shards = lax.axis_size("seq")
    blocks = lax.axis_size("dp")
    patch_loc = patches // shards
    frames = frames_dev * shards
    query_dev, slots, _ = queries.shape
    rows = query_dev * slots
    seat = lax.axis_index("seq")
    place = jnp.stack([lax.axis_index("dp"), lax.rem(seat, 2), seat // 2]).astype(jnp.int32)
    partner = [(i, i ^ 1) for i in range(shards)]
    chips = [[2 * chip + own for chip in range(shards // 2)] for own in range(2)]

    spatial = space(video[0], space_qkv, space_out, shards)
    spatial, flat = lax.optimization_barrier((spatial, queries.reshape(rows, E)))
    items = lax.all_to_all(spatial, "seq", 0, 0, tiled=True)
    mine = pack_queries(flat, query_len, positive)
    near = lax.ppermute(mine, "dp", [(i, i ^ 1) for i in range(blocks)])
    mine = jnp.stack([mine, near])
    packed = [mine] + [
        lax.ppermute(mine, "dp", [(i, (i + by) % blocks) for i in range(blocks)])
        for by in range(2, blocks, 2)
    ]
    khat = time(items.reshape(-1, D), time_qkv, time_out, proj_weight, patch_loc)

    expo, keep, send, sums = terms(packed, khat, place)
    got = lax.ppermute(send, "seq", partner)
    others = lax.ppermute(sums, "seq", partner)
    joined = join(keep, got, sums, others, shards // 2)
    joined = lax.all_to_all(joined, "seq", 0, 0, tiled=True, axis_index_groups=chips)
    parts, scale, loss = scales(joined, packed, place, slots, shards)
    parts = lax.all_to_all(
        parts.reshape((-1,) + parts.shape[2:]), ("dp", "seq"), 0, 0, tiled=True
    )
    video_grad = keys(scale, expo, packed, float(frames * P_SIZE))
    pair_loss = loss[:, :, ::slots].reshape(-1, 1)
    parts, video_grad, pair_loss = lax.optimization_barrier((parts, video_grad, pair_loss))
    query_grad = totals(parts.reshape((blocks, shards) + parts.shape[1:]), float(slots))
    return (
        video_grad.reshape(1, frames, patch_loc, E),
        query_grad.reshape(query_dev, slots, E),
        pair_loss,
    )


def solution(mesh):
    placed = (
        P("dp", "seq", None, None),
        P(),
        P(),
        P(),
        P(),
        P(),
        P("dp", None, None),
        P("dp"),
        P("dp"),
    )
    return jax.shard_map(
        body,
        mesh=mesh,
        in_specs=placed,
        out_specs=(P("dp", None, "seq", None), P("dp", None, None), P(None, "dp")),
        check_vma=False,
    )
```

```python
import jax
import jax.numpy as jnp
from jax import lax
from jax.experimental import pallas as pl
from jax.experimental.pallas import tpu as pltpu
from jax.sharding import PartitionSpec as P

HEADS = 12
P_SIZE = 256
TEMPER = 0.05
SLOPE = 10.0
OFFSET = -5.0
SHARP = 10.0
LOG2E = 1.4426950408889634

D = 768
HEAD = D // HEADS
PAIR = 2 * HEAD
PAIRS = HEADS // 2
TILE = 256
SUB = 128
E = 128
F32 = jnp.float32
BF16 = jnp.bfloat16
VMEM = pl.BlockSpec(memory_space=pltpu.VMEM)
SMEM = pl.BlockSpec(memory_space=pltpu.SMEM)
HBM = pl.BlockSpec(memory_space=pltpu.HBM)


def limit(mib):
    return pltpu.CompilerParams(vmem_limit_bytes=mib * 2**20)


def dot(a, b):
    return lax.dot_general(a, b, (((1,), (0,)), ((), ())), preferred_element_type=F32)


def dot_t(a, b):
    return lax.dot_general(a, b, (((1,), (1,)), ((), ())), preferred_element_type=F32)


def iota(shape, dim):
    return lax.broadcasted_iota(jnp.int32, shape, dim)


def layer_norm(tokens):
    values = tokens.astype(F32)
    center = values - jnp.mean(values, axis=-1, keepdims=True)
    spread = jnp.mean(center * center, axis=-1, keepdims=True)
    return (center * lax.rsqrt(spread + 1e-05)).astype(BF16)


def unit_heads(values, gain):
    same = (iota((TILE, TILE), 0) // HEAD == iota((TILE, TILE), 1) // HEAD).astype(BF16)
    parts = []
    for at in range(0, values.shape[1], TILE):
        part = values[:, at : at + TILE]
        squares = dot((part * part).astype(BF16), same)
        parts.append((part * (lax.rsqrt(squares + 1e-06) * gain)).astype(BF16))
    return jnp.concatenate(parts, axis=1)


def pair_blend(query, key, value, keep):
    extent = key.shape[0]
    low = iota((extent, PAIR), 1) < HEAD
    zero = jnp.zeros((extent, PAIR), BF16)
    one = jnp.ones((extent, PAIR), BF16)
    keys = jnp.concatenate([jnp.where(low, key, zero), jnp.where(low, zero, key)], axis=0)
    values = jnp.concatenate(
        [
            jnp.concatenate([jnp.where(low, value, zero), jnp.where(low, one, zero)], axis=1),
            jnp.concatenate([jnp.where(low, zero, value), jnp.where(low, zero, one)], axis=1),
        ],
        axis=0,
    )
    weights = jnp.exp2(dot_t(query, keys))
    if keep is not None:
        weights = jnp.where(keep, weights, 0.0)
    mixed = dot(weights.astype(BF16), values)
    return (mixed[:, :PAIR] / mixed[:, PAIR:]).astype(BF16)


def fetch(pairs, sem):
    copies = [pltpu.make_async_copy(a, b, sem.at[i]) for i, (a, b) in enumerate(pairs)]
    for copy in copies:
        copy.start()
    return copies


def columns(ref, third):
    return ref.at[:, pl.ds(third * D, D)]


def in_hbm(*arrays):
    return [pltpu.with_memory_space_constraint(array, pltpu.HBM) for array in arrays]


def qkv_all(normed, weight_s, copies, outs):
    for third, (out, gain) in enumerate(zip(outs, (SHARP * LOG2E, 1.0, None))):
        copies[third].wait()
        part = dot(normed, weight_s[:, third * D : (third + 1) * D])
        out[...] = part.astype(BF16) if gain is None else unit_heads(part, gain)


def space_kernel(
    video_ref, qkv_ref, out_w_ref, out_ref, x_s, qkv_s, w_s, n_s, q_s, k_s, v_s, y_s, sem, out_sem
):
    frames, patches, _ = x_s.shape
    video = fetch([(video_ref.at[f], x_s.at[f]) for f in range(frames)], sem)
    weights = fetch(
        [(columns(qkv_ref, i), columns(qkv_s, i)) for i in range(3)] + [(out_w_ref, w_s)],
        sem.at[pl.ds(frames, 4)],
    )
    for f in range(frames):
        video[f].wait()
        n_s[f * patches : (f + 1) * patches, :] = layer_norm(x_s[f])
    qkv_all(n_s[...], qkv_s, weights, (q_s, k_s, v_s))
    weights[3].wait()
    stores = []
    for f in range(frames):
        down = slice(f * patches, (f + 1) * patches)
        blended = []
        for pair in range(PAIRS):
            at = slice(pair * PAIR, (pair + 1) * PAIR)
            blended.append(pair_blend(q_s[down, at], k_s[down, at], v_s[down, at], None))
        update = dot(jnp.concatenate(blended, axis=1), w_s[...])
        y_s[f] = (x_s[f].astype(F32) + update).astype(BF16).reshape(y_s.shape[1:])
        stores.append(pltpu.make_async_copy(y_s.at[f], out_ref.at[:, f], out_sem.at[f]))
        stores[-1].start()
    for store in stores:
        store.wait()


def space(video, qkv_weight, out_weight, shards):
    frames, patches, _ = video.shape
    local = patches // shards
    return pl.pallas_call(
        space_kernel,
        in_specs=[HBM] * 3,
        out_specs=HBM,
        out_shape=pltpu.HBM((shards, frames, local, D), BF16),
        scratch_shapes=[
            pltpu.VMEM((frames, patches, D), BF16),
            pltpu.VMEM((D, 3 * D), BF16),
            pltpu.VMEM((D, D), BF16),
        ]
        + [pltpu.VMEM((frames * patches, D), BF16)] * 4
        + [
            pltpu.VMEM((frames, shards, local, D), BF16),
            pltpu.SemaphoreType.DMA((frames + 4,)),
            pltpu.SemaphoreType.DMA((frames,)),
        ],
        compiler_params=limit(40),
        name="space",
    )(*in_hbm(video, qkv_weight, out_weight))


def swap_rows(rows, side):
    extent = side * side
    row, col = iota((extent, extent), 0), iota((extent, extent), 1)
    swap = (col == (row % side) * side + row // side).astype(BF16)
    return dot(swap, rows).astype(BF16)


def time_kernel(
    x_ref, qkv_ref, out_w_ref, proj_ref, khat_ref,
    x_s, n_s, qkv_s, w_s, p_s, q_s, k_s, v_s, b_s, kh_s, sem,
):
    side, frames, _ = x_s.shape
    rows = x_ref.shape[0]
    weights = fetch(
        [(columns(qkv_ref, i), columns(qkv_s, i)) for i in range(3)]
        + [(out_w_ref, w_s), (proj_ref, p_s)],
        sem,
    )
    for tile in range(rows // TILE):
        tokens = swap_rows(x_ref[tile * TILE : (tile + 1) * TILE, :], side)
        at = slice(tile * side, (tile + 1) * side)
        x_s[:, at, :] = tokens.reshape(side, side, D)
        n_s[:, at, :] = layer_norm(tokens).reshape(side, side, D)
    qkv_all(n_s[...].reshape(rows, D), qkv_s, weights, (q_s, k_s, v_s))
    keep = iota((SUB, 2 * SUB), 0) // frames == (iota((SUB, 2 * SUB), 1) % SUB) // frames
    for sub in range(rows // SUB):
        down = slice(sub * SUB, (sub + 1) * SUB)
        for pair in range(PAIRS):
            at = slice(pair * PAIR, (pair + 1) * PAIR)
            b_s[down, at] = pair_blend(q_s[down, at], k_s[down, at], v_s[down, at], keep)
    weights[3].wait()
    weights[4].wait()
    update = dot(b_s[...], w_s[...])
    mixed = (x_s[...].reshape(rows, D).astype(F32) + update).astype(BF16)
    projected = dot(layer_norm(mixed), p_s[...])
    norm = jnp.sum(projected * projected, axis=-1, keepdims=True)
    kh_s[...] = (projected * lax.rsqrt(norm + 1e-06)).astype(BF16).reshape(kh_s.shape)
    for tile in range(rows // TILE):
        part = kh_s[:, tile * side : (tile + 1) * side, :].reshape(TILE, E)
        khat_ref[tile * TILE : (tile + 1) * TILE, :] = swap_rows(part, side)


def time(x, qkv_weight, out_weight, proj_weight, patches):
    rows = x.shape[0]
    frames = rows // patches
    return pl.pallas_call(
        time_kernel,
        in_specs=[VMEM] + [HBM] * 3,
        out_specs=VMEM,
        out_shape=jax.ShapeDtypeStruct((rows, E), BF16),
        scratch_shapes=[
            pltpu.VMEM((patches, frames, D), BF16),
            pltpu.VMEM((patches, frames, D), BF16),
            pltpu.VMEM((D, 3 * D), BF16),
            pltpu.VMEM((D, D), BF16),
            pltpu.VMEM((D, E), BF16),
        ]
        + [pltpu.VMEM((rows, D), BF16)] * 4
        + [pltpu.VMEM((patches, frames, E), BF16), pltpu.SemaphoreType.DMA((5,))],
        compiler_params=limit(40),
        name="time",
    )(x, *in_hbm(qkv_weight, out_weight, proj_weight))


EXTRA = 16


def query_kernel(len_ref, pos_ref, q_ref, out_ref):
    rows = q_ref.shape[0]
    values = q_ref[...].astype(F32)
    norm = jnp.sum(values * values, axis=-1, keepdims=True)
    out_ref[:rows, :] = (values / jnp.sqrt(norm + 1e-06)).astype(BF16)
    slots = rows // len_ref.shape[0]
    row, lane = iota((EXTRA, E), 0), iota((EXTRA, E), 1)
    owner = ((row % 2) * E + lane) // slots
    extra = jnp.zeros((EXTRA, E), F32)
    for query in range(len_ref.shape[0]):
        picked = jnp.where(row < 2, len_ref[query], pos_ref[query]).astype(F32)
        extra = jnp.where((owner == query) & (row < 4), picked, extra)
    out_ref[rows:, :] = extra.astype(BF16)


def pack_queries(queries, query_len, positive):
    rows = queries.shape[0]
    return pl.pallas_call(
        query_kernel,
        in_specs=[SMEM, SMEM, VMEM],
        out_specs=VMEM,
        out_shape=jax.ShapeDtypeStruct((rows + EXTRA, E), BF16),
        name="pack_queries",
    )(query_len, positive, queries)


def group_of(mine, blocks, block):
    side, step = divmod(block, blocks // 2)
    return lax.rem(mine + blocks - 2 * step, blocks) ^ side


def block_of(packed_refs, block):
    side, step = divmod(block, packed_refs[0].shape[0])
    return packed_refs[side].at[step]


def expo_terms(query, khat):
    gain = LOG2E / TEMPER
    return jnp.exp2(dot_t(query, khat) * gain - gain).astype(BF16)


def terms_kernel(blocks, at_ref, khat_ref, *refs):
    packed_refs, (keep_ref, send_ref, sums_ref) = refs[:-3], refs[-3:]
    rows = packed_refs[0].shape[1] - EXTRA
    first = at_ref[1] == 0
    khat = khat_ref[...]
    wide = jnp.concatenate([khat, jnp.ones_like(khat)], axis=1)
    eye = iota((E, E), 0) == iota((E, E), 1)
    sums = []
    for block in range(blocks):
        both = dot(expo_terms(block_of(packed_refs, block)[:rows, :], khat), wide)
        low, high = both[:E, :E], both[E:, :E]
        keep_ref[block] = jnp.where(first, low, high)
        send_ref[block] = jnp.where(first, high, low).astype(BF16)
        for part in range(rows // E):
            square = both[part * E : (part + 1) * E, E:]
            sums.append(jnp.sum(jnp.where(eye, square, 0.0), axis=0, keepdims=True))
    sums_ref[...] = jnp.concatenate(sums, axis=0)


def terms(packed, khat, place):
    blocks, rows = 2 * packed[0].shape[0], packed[0].shape[1] - EXTRA
    return pl.pallas_call(
        lambda *refs: terms_kernel(blocks, *refs),
        in_specs=[SMEM] + [VMEM] * (1 + len(packed)),
        out_specs=[VMEM] * 3,
        out_shape=[
            jax.ShapeDtypeStruct((blocks, rows // 2, E), F32),
            jax.ShapeDtypeStruct((blocks, rows // 2, E), BF16),
            jax.ShapeDtypeStruct((blocks * rows // E, E), F32),
        ],
        compiler_params=limit(16),
        name="terms",
    )(place, khat, *packed)


def join_kernel(keep_ref, got_ref, sums_ref, others_ref, out_ref):
    blocks, half, _ = keep_ref.shape
    chips = out_ref.shape[0]
    piece = half // chips
    sums = sums_ref[...] + others_ref[...]
    upper = sums.astype(BF16)
    lower = (sums - upper.astype(F32)).astype(BF16)
    notes = jnp.concatenate([upper, lower], axis=0)
    for block in range(blocks):
        both = (keep_ref[block] + got_ref[block].astype(F32)).astype(BF16)
        for chip in range(chips):
            out_ref[chip, block * piece : (block + 1) * piece, :] = both[
                chip * piece : (chip + 1) * piece
            ]
    for chip in range(chips):
        out_ref[chip, blocks * piece :, :] = notes


def join(keep, got, sums, others, chips):
    blocks, half, _ = keep.shape
    return pl.pallas_call(
        join_kernel,
        in_specs=[VMEM] * 4,
        out_specs=VMEM,
        out_shape=jax.ShapeDtypeStruct(
            (chips, blocks * half // chips + 2 * sums.shape[0], E), BF16
        ),
        compiler_params=limit(8),
        name="join",
    )(keep, got, sums, others)


def scale_kernel(slots, at_ref, got_ref, *refs):
    packed_refs, (part_ref, scale_ref, loss_ref) = refs[:-3], refs[-3:]
    blocks, shards, piece, _ = part_ref.shape
    rows = packed_refs[0].shape[1] - EXTRA
    per = rows // E
    got = jnp.sum(got_ref[...].astype(F32), axis=0)
    blend, notes = got[: blocks * piece], got[blocks * piece :]
    total = notes[: blocks * per] + notes[blocks * per :]
    notes = [block_of(packed_refs, b)[rows:, :].astype(F32) for b in range(blocks)]
    lens = jnp.concatenate([note[:per] for note in notes], axis=0)
    pos = jnp.concatenate([note[per : 2 * per] for note in notes], axis=0)
    mask = ((iota(total.shape, 1) % slots).astype(F32) < lens).astype(F32)
    smooth = (1.0 + TEMPER * jnp.log(total)) * mask
    same = (iota((E, E), 0) // slots == iota((E, E), 1) // slots).astype(F32)
    score = (
        lax.dot_general(
            smooth,
            same,
            (((1,), (0,)), ((), ())),
            preferred_element_type=F32,
            precision=lax.Precision.HIGHEST,
        )
        / lens
    )
    sign = jnp.where(pos == at_ref[0].astype(F32), 1.0, -1.0)
    margin = sign * (SLOPE * score + OFFSET)
    loss = jnp.maximum(-margin, 0.0) + jnp.log1p(jnp.exp(-jnp.abs(margin)))
    coeff = -SLOPE * sign / (1.0 + jnp.exp(margin)) * mask / lens
    scale_ref[...] = (coeff / total).T
    scale = scale_ref[pl.ds(pl.multiple_of(at_ref[2] * piece, piece), piece), :]
    first = at_ref[1] == 0
    for block in range(blocks):
        group = group_of(at_ref[0], blocks, block)
        at = block * per
        column = jnp.where(first, scale[:, at : at + 1], scale[:, at + 1 : at + 2])
        part = (blend[block * piece : (block + 1) * piece] * column).astype(BF16)
        for shard in range(shards):
            part_ref[group, shard] = part
        loss_ref[group] = loss[at : at + per]


def scales(got, packed, place, slots, shards):
    blocks, rows = 2 * packed[0].shape[0], packed[0].shape[1] - EXTRA
    piece = rows // shards
    return pl.pallas_call(
        lambda *refs: scale_kernel(slots, *refs),
        in_specs=[SMEM] + [VMEM] * (1 + len(packed)),
        out_specs=[VMEM] * 3,
        out_shape=[
            jax.ShapeDtypeStruct((blocks, shards, piece, E), BF16),
            jax.ShapeDtypeStruct((E, blocks * rows // E), F32),
            jax.ShapeDtypeStruct((blocks, rows // E, E), F32),
        ],
        compiler_params=limit(8),
        name="scales",
    )(place, got, *packed)


def keys_kernel(gain, blocks, scale_ref, khat_ref, *refs):
    packed_refs, out_ref = refs[:-1], refs[-1]
    khat = khat_ref[...]
    rows = packed_refs[0].shape[1] - EXTRA
    per = rows // E
    total = jnp.zeros((E, khat.shape[0]), F32)
    for block in range(blocks):
        query = block_of(packed_refs, block)[:rows, :]
        parts = []
        for part in range(per):
            at = block * per + part
            scaled = query[part * E : (part + 1) * E].astype(F32) * scale_ref[:, at : at + 1]
            parts.append(scaled.T.astype(BF16))
        total = total + dot(jnp.concatenate(parts, axis=1), expo_terms(query, khat))
    out_ref[...] = (total.T * gain).astype(BF16)


def keys(scale, khat, packed, gain):
    return pl.pallas_call(
        lambda *refs: keys_kernel(gain, 2 * packed[0].shape[0], *refs),
        in_specs=[VMEM] * (2 + len(packed)),
        out_specs=VMEM,
        out_shape=jax.ShapeDtypeStruct(khat.shape, BF16),
        compiler_params=limit(16),
        name="keys",
    )(scale, khat, *packed)


def total_kernel(gain, in_ref, out_ref):
    _, shards, piece, _ = in_ref.shape
    total = (jnp.sum(in_ref[...].astype(F32), axis=0) * gain).astype(BF16)
    for shard in range(shards):
        at = (shard % 2) * (shards // 2) + shard // 2
        out_ref[at * piece : (at + 1) * piece, :] = total[shard]


def totals(parts, gain):
    _, shards, piece, _ = parts.shape
    return pl.pallas_call(
        lambda *refs: total_kernel(gain, *refs),
        in_specs=[VMEM],
        out_specs=VMEM,
        out_shape=jax.ShapeDtypeStruct((shards * piece, E), BF16),
        compiler_params=limit(4),
        name="totals",
    )(parts)


def body(
    video, space_qkv, space_out, time_qkv, time_out, proj_weight, queries, query_len, positive
):
    _, frames_dev, patches, _ = video.shape
    shards = lax.axis_size("seq")
    blocks = lax.axis_size("dp")
    patch_loc = patches // shards
    frames = frames_dev * shards
    query_dev, slots, _ = queries.shape
    rows = query_dev * slots
    seat = lax.axis_index("seq")
    place = jnp.stack([lax.axis_index("dp"), lax.rem(seat, 2), seat // 2]).astype(jnp.int32)
    partner = [(i, i ^ 1) for i in range(shards)]
    chips = [[2 * chip + own for chip in range(shards // 2)] for own in range(2)]

    spatial = space(video[0], space_qkv, space_out, shards)
    spatial, flat = lax.optimization_barrier((spatial, queries.reshape(rows, E)))
    items = lax.all_to_all(spatial, "seq", 0, 0, tiled=True)
    mine = pack_queries(flat, query_len, positive)
    lane = jnp.stack(
        [mine]
        + [
            lax.ppermute(mine, "dp", [(i, (i + by) % blocks) for i in range(blocks)])
            for by in range(2, blocks, 2)
        ]
    )
    items, lane = lax.optimization_barrier((items, lane))
    packed = [lane, lax.ppermute(lane, "dp", [(i, i ^ 1) for i in range(blocks)])]
    khat = time(items.reshape(-1, D), time_qkv, time_out, proj_weight, patch_loc)

    keep, send, sums = terms(packed, khat, place)
    got = lax.ppermute(send, "seq", partner)
    others = lax.ppermute(sums, "seq", partner)
    joined = join(keep, got, sums, others, shards // 2)
    joined = lax.all_to_all(joined, "seq", 0, 0, tiled=True, axis_index_groups=chips)
    parts, scale, loss = scales(joined, packed, place, slots, shards)
    parts = lax.all_to_all(
        parts.reshape((-1,) + parts.shape[2:]), ("dp", "seq"), 0, 0, tiled=True
    )
    video_grad = keys(scale, khat, packed, float(frames * P_SIZE))
    pair_loss = loss[:, :, ::slots].reshape(-1, 1)
    parts, video_grad, pair_loss = lax.optimization_barrier((parts, video_grad, pair_loss))
    query_grad = totals(parts.reshape((blocks, shards) + parts.shape[1:]), float(slots))
    return (
        video_grad.reshape(1, frames, patch_loc, E),
        query_grad.reshape(query_dev, slots, E),
        pair_loss,
    )


def solution(mesh):
    placed = (
        P("dp", "seq", None, None),
        P(),
        P(),
        P(),
        P(),
        P(),
        P("dp", None, None),
        P("dp"),
        P("dp"),
    )
    return jax.shard_map(
        body,
        mesh=mesh,
        in_specs=placed,
        out_specs=(P("dp", None, "seq", None), P("dp", None, None), P(None, "dp")),
        check_vma=False,
    )
```

```python
import jax
import jax.numpy as jnp
from jax import lax
from jax.experimental import pallas as pl
from jax.experimental.pallas import tpu as pltpu
from jax.sharding import PartitionSpec as P

HEADS = 12
P_SIZE = 256
TEMPER = 0.05
SLOPE = 10.0
OFFSET = -5.0
SHARP = 10.0
LOG2E = 1.4426950408889634

D = 768
HEAD = D // HEADS
PAIR = 2 * HEAD
PAIRS = HEADS // 2
TILE = 256
SUB = 128
E = 128
F32 = jnp.float32
BF16 = jnp.bfloat16
VMEM = pl.BlockSpec(memory_space=pltpu.VMEM)
SMEM = pl.BlockSpec(memory_space=pltpu.SMEM)
HBM = pl.BlockSpec(memory_space=pltpu.HBM)


def limit(mib):
    return pltpu.CompilerParams(vmem_limit_bytes=mib * 2**20)


def dot(a, b):
    return lax.dot_general(a, b, (((1,), (0,)), ((), ())), preferred_element_type=F32)


def dot_t(a, b):
    return lax.dot_general(a, b, (((1,), (1,)), ((), ())), preferred_element_type=F32)


def iota(shape, dim):
    return lax.broadcasted_iota(jnp.int32, shape, dim)


def layer_norm(tokens):
    values = tokens.astype(F32)
    center = values - jnp.mean(values, axis=-1, keepdims=True)
    spread = jnp.mean(center * center, axis=-1, keepdims=True)
    return (center * lax.rsqrt(spread + 1e-05)).astype(BF16)


def unit_heads(values, gain):
    same = (iota((TILE, TILE), 0) // HEAD == iota((TILE, TILE), 1) // HEAD).astype(BF16)
    parts = []
    for at in range(0, values.shape[1], TILE):
        part = values[:, at : at + TILE]
        squares = dot((part * part).astype(BF16), same)
        parts.append((part * (lax.rsqrt(squares + 1e-06) * gain)).astype(BF16))
    return jnp.concatenate(parts, axis=1)


def pair_blend(query, key, value, keep):
    extent = key.shape[0]
    low = iota((extent, PAIR), 1) < HEAD
    zero = jnp.zeros((extent, PAIR), BF16)
    one = jnp.ones((extent, PAIR), BF16)
    keys = jnp.concatenate([jnp.where(low, key, zero), jnp.where(low, zero, key)], axis=0)
    values = jnp.concatenate(
        [
            jnp.concatenate([jnp.where(low, value, zero), jnp.where(low, one, zero)], axis=1),
            jnp.concatenate([jnp.where(low, zero, value), jnp.where(low, zero, one)], axis=1),
        ],
        axis=0,
    )
    weights = jnp.exp2(dot_t(query, keys))
    if keep is not None:
        weights = jnp.where(keep, weights, 0.0)
    mixed = dot(weights.astype(BF16), values)
    return (mixed[:, :PAIR] / mixed[:, PAIR:]).astype(BF16)


def fetch(pairs, sem):
    copies = [pltpu.make_async_copy(a, b, sem.at[i]) for i, (a, b) in enumerate(pairs)]
    for copy in copies:
        copy.start()
    return copies


def columns(ref, third):
    return ref.at[:, pl.ds(third * D, D)]


def in_hbm(*arrays):
    return [pltpu.with_memory_space_constraint(array, pltpu.HBM) for array in arrays]


def qkv_all(normed, weight_s, copies, outs):
    for third, (out, gain) in enumerate(zip(outs, (SHARP * LOG2E, 1.0, None))):
        copies[third].wait()
        part = dot(normed, weight_s[:, third * D : (third + 1) * D])
        out[...] = part.astype(BF16) if gain is None else unit_heads(part, gain)


def space_kernel(
    video_ref, qkv_ref, out_w_ref, out_ref, x_s, qkv_s, w_s, n_s, q_s, k_s, v_s, y_s, sem, out_sem
):
    frames, patches, _ = x_s.shape
    video = fetch([(video_ref.at[f], x_s.at[f]) for f in range(frames)], sem)
    weights = fetch(
        [(columns(qkv_ref, i), columns(qkv_s, i)) for i in range(3)] + [(out_w_ref, w_s)],
        sem.at[pl.ds(frames, 4)],
    )
    for f in range(frames):
        video[f].wait()
        n_s[f * patches : (f + 1) * patches, :] = layer_norm(x_s[f])
    qkv_all(n_s[...], qkv_s, weights, (q_s, k_s, v_s))
    weights[3].wait()
    stores = []
    for f in range(frames):
        down = slice(f * patches, (f + 1) * patches)
        blended = []
        for pair in range(PAIRS):
            at = slice(pair * PAIR, (pair + 1) * PAIR)
            blended.append(pair_blend(q_s[down, at], k_s[down, at], v_s[down, at], None))
        update = dot(jnp.concatenate(blended, axis=1), w_s[...])
        y_s[f] = (x_s[f].astype(F32) + update).astype(BF16).reshape(y_s.shape[1:])
        stores.append(pltpu.make_async_copy(y_s.at[f], out_ref.at[:, f], out_sem.at[f]))
        stores[-1].start()
    for store in stores:
        store.wait()


def space(video, qkv_weight, out_weight, shards):
    frames, patches, _ = video.shape
    local = patches // shards
    return pl.pallas_call(
        space_kernel,
        in_specs=[HBM] * 3,
        out_specs=HBM,
        out_shape=pltpu.HBM((shards, frames, local, D), BF16),
        scratch_shapes=[
            pltpu.VMEM((frames, patches, D), BF16),
            pltpu.VMEM((D, 3 * D), BF16),
            pltpu.VMEM((D, D), BF16),
        ]
        + [pltpu.VMEM((frames * patches, D), BF16)] * 4
        + [
            pltpu.VMEM((frames, shards, local, D), BF16),
            pltpu.SemaphoreType.DMA((frames + 4,)),
            pltpu.SemaphoreType.DMA((frames,)),
        ],
        compiler_params=limit(40),
        name="space",
    )(*in_hbm(video, qkv_weight, out_weight))


def swap_rows(rows, side):
    extent = side * side
    row, col = iota((extent, extent), 0), iota((extent, extent), 1)
    swap = (col == (row % side) * side + row // side).astype(BF16)
    return dot(swap, rows).astype(BF16)


def time_kernel(
    x_ref, qkv_ref, out_w_ref, proj_ref, khat_ref,
    x_s, n_s, qkv_s, w_s, p_s, q_s, k_s, v_s, b_s, kh_s, sem,
):
    side, frames, _ = x_s.shape
    rows = x_ref.shape[0]
    weights = fetch(
        [(columns(qkv_ref, i), columns(qkv_s, i)) for i in range(3)]
        + [(out_w_ref, w_s), (proj_ref, p_s)],
        sem,
    )
    for tile in range(rows // TILE):
        tokens = swap_rows(x_ref[tile * TILE : (tile + 1) * TILE, :], side)
        at = slice(tile * side, (tile + 1) * side)
        x_s[:, at, :] = tokens.reshape(side, side, D)
        n_s[:, at, :] = layer_norm(tokens).reshape(side, side, D)
    qkv_all(n_s[...].reshape(rows, D), qkv_s, weights, (q_s, k_s, v_s))
    keep = iota((SUB, 2 * SUB), 0) // frames == (iota((SUB, 2 * SUB), 1) % SUB) // frames
    for sub in range(rows // SUB):
        down = slice(sub * SUB, (sub + 1) * SUB)
        for pair in range(PAIRS):
            at = slice(pair * PAIR, (pair + 1) * PAIR)
            b_s[down, at] = pair_blend(q_s[down, at], k_s[down, at], v_s[down, at], keep)
    weights[3].wait()
    weights[4].wait()
    update = dot(b_s[...], w_s[...])
    mixed = (x_s[...].reshape(rows, D).astype(F32) + update).astype(BF16)
    projected = dot(layer_norm(mixed), p_s[...])
    norm = jnp.sum(projected * projected, axis=-1, keepdims=True)
    kh_s[...] = (projected * lax.rsqrt(norm + 1e-06)).astype(BF16).reshape(kh_s.shape)
    for tile in range(rows // TILE):
        part = kh_s[:, tile * side : (tile + 1) * side, :].reshape(TILE, E)
        khat_ref[tile * TILE : (tile + 1) * TILE, :] = swap_rows(part, side)


def time(x, qkv_weight, out_weight, proj_weight, patches):
    rows = x.shape[0]
    frames = rows // patches
    return pl.pallas_call(
        time_kernel,
        in_specs=[VMEM] + [HBM] * 3,
        out_specs=VMEM,
        out_shape=jax.ShapeDtypeStruct((rows, E), BF16),
        scratch_shapes=[
            pltpu.VMEM((patches, frames, D), BF16),
            pltpu.VMEM((patches, frames, D), BF16),
            pltpu.VMEM((D, 3 * D), BF16),
            pltpu.VMEM((D, D), BF16),
            pltpu.VMEM((D, E), BF16),
        ]
        + [pltpu.VMEM((rows, D), BF16)] * 4
        + [pltpu.VMEM((patches, frames, E), BF16), pltpu.SemaphoreType.DMA((5,))],
        compiler_params=limit(40),
        name="time",
    )(x, *in_hbm(qkv_weight, out_weight, proj_weight))


EXTRA = 16


def query_kernel(len_ref, pos_ref, q_ref, out_ref):
    rows = q_ref.shape[0]
    values = q_ref[...].astype(F32)
    norm = jnp.sum(values * values, axis=-1, keepdims=True)
    out_ref[:rows, :] = (values / jnp.sqrt(norm + 1e-06)).astype(BF16)
    slots = rows // len_ref.shape[0]
    row, lane = iota((EXTRA, E), 0), iota((EXTRA, E), 1)
    owner = ((row % 2) * E + lane) // slots
    extra = jnp.zeros((EXTRA, E), F32)
    for query in range(len_ref.shape[0]):
        picked = jnp.where(row < 2, len_ref[query], pos_ref[query]).astype(F32)
        extra = jnp.where((owner == query) & (row < 4), picked, extra)
    out_ref[rows:, :] = extra.astype(BF16)


def pack_queries(queries, query_len, positive):
    rows = queries.shape[0]
    return pl.pallas_call(
        query_kernel,
        in_specs=[SMEM, SMEM, VMEM],
        out_specs=VMEM,
        out_shape=jax.ShapeDtypeStruct((rows + EXTRA, E), BF16),
        name="pack_queries",
    )(query_len, positive, queries)


def group_of(mine, blocks, block):
    side, step = divmod(block, blocks // 2)
    return lax.rem(mine + blocks - 2 * step, blocks) ^ side


def block_of(packed_refs, block):
    side, step = divmod(block, packed_refs[0].shape[0])
    return packed_refs[side].at[step]


def expo_terms(query, khat):
    gain = LOG2E / TEMPER
    return jnp.exp2(dot_t(query, khat) * gain - gain).astype(BF16)


def terms_kernel(blocks, at_ref, khat_ref, *refs):
    packed_refs, (keep_ref, send_ref, sums_ref) = refs[:-3], refs[-3:]
    rows = packed_refs[0].shape[1] - EXTRA
    first = at_ref[1] == 0
    khat = khat_ref[...]
    wide = jnp.concatenate([khat, jnp.ones_like(khat)], axis=1)
    eye = iota((E, E), 0) == iota((E, E), 1)
    sums = []
    for block in range(blocks):
        both = dot(expo_terms(block_of(packed_refs, block)[:rows, :], khat), wide)
        low, high = both[:E, :E], both[E:, :E]
        keep_ref[block] = jnp.where(first, low, high)
        send_ref[block] = jnp.where(first, high, low).astype(BF16)
        for part in range(rows // E):
            square = both[part * E : (part + 1) * E, E:]
            sums.append(jnp.sum(jnp.where(eye, square, 0.0), axis=0, keepdims=True))
    sums_ref[...] = jnp.concatenate(sums, axis=0)


def terms(packed, khat, place):
    blocks, rows = 2 * packed[0].shape[0], packed[0].shape[1] - EXTRA
    return pl.pallas_call(
        lambda *refs: terms_kernel(blocks, *refs),
        in_specs=[SMEM] + [VMEM] * (1 + len(packed)),
        out_specs=[VMEM] * 3,
        out_shape=[
            jax.ShapeDtypeStruct((blocks, rows // 2, E), F32),
            jax.ShapeDtypeStruct((blocks, rows // 2, E), BF16),
            jax.ShapeDtypeStruct((blocks * rows // E, E), F32),
        ],
        compiler_params=limit(16),
        name="terms",
    )(place, khat, *packed)


def join_kernel(keep_ref, got_ref, sums_ref, others_ref, out_ref):
    blocks, half, _ = keep_ref.shape
    chips = out_ref.shape[0]
    piece = half // chips
    sums = sums_ref[...] + others_ref[...]
    upper = sums.astype(BF16)
    lower = (sums - upper.astype(F32)).astype(BF16)
    notes = jnp.concatenate([upper, lower], axis=0)
    for block in range(blocks):
        both = (keep_ref[block] + got_ref[block].astype(F32)).astype(BF16)
        for chip in range(chips):
            out_ref[chip, block * piece : (block + 1) * piece, :] = both[
                chip * piece : (chip + 1) * piece
            ]
    for chip in range(chips):
        out_ref[chip, blocks * piece :, :] = notes


def join(keep, got, sums, others, chips):
    blocks, half, _ = keep.shape
    return pl.pallas_call(
        join_kernel,
        in_specs=[VMEM] * 4,
        out_specs=VMEM,
        out_shape=jax.ShapeDtypeStruct(
            (chips, blocks * half // chips + 2 * sums.shape[0], E), BF16
        ),
        compiler_params=limit(8),
        name="join",
    )(keep, got, sums, others)


def scale_kernel(slots, at_ref, got_ref, *refs):
    packed_refs, (part_ref, scale_ref, loss_ref) = refs[:-3], refs[-3:]
    blocks, shards, share, _ = part_ref.shape
    piece = 2 * share
    rows = packed_refs[0].shape[1] - EXTRA
    per = rows // E
    got = jnp.sum(got_ref[...].astype(F32), axis=0)
    blend, notes = got[: blocks * piece], got[blocks * piece :]
    total = notes[: blocks * per] + notes[blocks * per :]
    notes = [block_of(packed_refs, b)[rows:, :].astype(F32) for b in range(blocks)]
    lens = jnp.concatenate([note[:per] for note in notes], axis=0)
    pos = jnp.concatenate([note[per : 2 * per] for note in notes], axis=0)
    mask = ((iota(total.shape, 1) % slots).astype(F32) < lens).astype(F32)
    smooth = (1.0 + TEMPER * jnp.log(total)) * mask
    same = (iota((E, E), 0) // slots == iota((E, E), 1) // slots).astype(F32)
    score = (
        lax.dot_general(
            smooth,
            same,
            (((1,), (0,)), ((), ())),
            preferred_element_type=F32,
            precision=lax.Precision.HIGHEST,
        )
        / lens
    )
    sign = jnp.where(pos == at_ref[0].astype(F32), 1.0, -1.0)
    margin = sign * (SLOPE * score + OFFSET)
    loss = jnp.maximum(-margin, 0.0) + jnp.log1p(jnp.exp(-jnp.abs(margin)))
    coeff = -SLOPE * sign / (1.0 + jnp.exp(margin)) * mask / lens
    scale_ref[...] = (coeff / total).T
    scale = scale_ref[pl.ds(pl.multiple_of(at_ref[2] * piece, piece), piece), :]
    first = at_ref[1] == 0
    for block in range(blocks):
        group = group_of(at_ref[0], blocks, block)
        at = block * per
        column = jnp.where(first, scale[:, at : at + 1], scale[:, at + 1 : at + 2])
        part = (blend[block * piece : (block + 1) * piece] * column).astype(BF16)
        for shard in range(shards):
            part_ref[group, shard] = part[shard % 2 * share : (shard % 2 + 1) * share]
        loss_ref[group] = loss[at : at + per]


def scales(got, packed, place, slots, shards):
    blocks, rows = 2 * packed[0].shape[0], packed[0].shape[1] - EXTRA
    share = rows // shards // 2
    return pl.pallas_call(
        lambda *refs: scale_kernel(slots, *refs),
        in_specs=[SMEM] + [VMEM] * (1 + len(packed)),
        out_specs=[VMEM] * 3,
        out_shape=[
            jax.ShapeDtypeStruct((blocks, shards, share, E), BF16),
            jax.ShapeDtypeStruct((E, blocks * rows // E), F32),
            jax.ShapeDtypeStruct((blocks, rows // E, E), F32),
        ],
        compiler_params=limit(8),
        name="scales",
    )(place, got, *packed)


def keys_kernel(gain, blocks, scale_ref, khat_ref, *refs):
    packed_refs, out_ref = refs[:-1], refs[-1]
    khat = khat_ref[...]
    rows = packed_refs[0].shape[1] - EXTRA
    per = rows // E
    total = jnp.zeros((E, khat.shape[0]), F32)
    for block in range(blocks):
        query = block_of(packed_refs, block)[:rows, :]
        parts = []
        for part in range(per):
            at = block * per + part
            scaled = query[part * E : (part + 1) * E].astype(F32) * scale_ref[:, at : at + 1]
            parts.append(scaled.T.astype(BF16))
        total = total + dot(jnp.concatenate(parts, axis=1), expo_terms(query, khat))
    out_ref[...] = (total.T * gain).astype(BF16)


def keys(scale, khat, packed, gain):
    return pl.pallas_call(
        lambda *refs: keys_kernel(gain, 2 * packed[0].shape[0], *refs),
        in_specs=[VMEM] * (2 + len(packed)),
        out_specs=VMEM,
        out_shape=jax.ShapeDtypeStruct(khat.shape, BF16),
        compiler_params=limit(16),
        name="keys",
    )(scale, khat, *packed)


def total_kernel(gain, in_ref, out_ref):
    out_ref[...] = (jnp.sum(in_ref[...].astype(F32), axis=0) * gain).astype(BF16)


def totals(parts, gain):
    return pl.pallas_call(
        lambda *refs: total_kernel(gain, *refs),
        in_specs=[VMEM],
        out_specs=VMEM,
        out_shape=jax.ShapeDtypeStruct(parts.shape[1:], BF16),
        compiler_params=limit(4),
        name="totals",
    )(parts)


def weave_kernel(at_ref, mine_ref, other_ref, out_ref):
    shards, share, _ = mine_ref.shape
    first = at_ref[1] == 0
    for shard in range(shards):
        at = ((shard % 2) * (shards // 2) + shard // 2) * 2 * share
        mine, other = mine_ref[shard], other_ref[shard]
        out_ref[at : at + share, :] = jnp.where(first, mine, other)
        out_ref[at + share : at + 2 * share, :] = jnp.where(first, other, mine)


def weave(place, mine, other):
    shards, share, _ = mine.shape
    return pl.pallas_call(
        weave_kernel,
        in_specs=[SMEM, VMEM, VMEM],
        out_specs=VMEM,
        out_shape=jax.ShapeDtypeStruct((2 * shards * share, E), BF16),
        compiler_params=limit(4),
        name="weave",
    )(place, mine, other)


def body(
    video, space_qkv, space_out, time_qkv, time_out, proj_weight, queries, query_len, positive
):
    _, frames_dev, patches, _ = video.shape
    shards = lax.axis_size("seq")
    blocks = lax.axis_size("dp")
    patch_loc = patches // shards
    frames = frames_dev * shards
    query_dev, slots, _ = queries.shape
    rows = query_dev * slots
    seat = lax.axis_index("seq")
    place = jnp.stack([lax.axis_index("dp"), lax.rem(seat, 2), seat // 2]).astype(jnp.int32)
    partner = [(i, i ^ 1) for i in range(shards)]
    chips = [[2 * chip + own for chip in range(shards // 2)] for own in range(2)]

    spatial = space(video[0], space_qkv, space_out, shards)
    spatial, flat = lax.optimization_barrier((spatial, queries.reshape(rows, E)))
    items = lax.all_to_all(spatial, "seq", 0, 0, tiled=True)
    mine = pack_queries(flat, query_len, positive)
    lane = jnp.stack(
        [mine]
        + [
            lax.ppermute(mine, "dp", [(i, (i + by) % blocks) for i in range(blocks)])
            for by in range(2, blocks, 2)
        ]
    )
    items, lane = lax.optimization_barrier((items, lane))
    packed = [lane, lax.ppermute(lane, "dp", [(i, i ^ 1) for i in range(blocks)])]
    khat = time(items.reshape(-1, D), time_qkv, time_out, proj_weight, patch_loc)

    keep, send, sums = terms(packed, khat, place)
    got = lax.ppermute(send, "seq", partner)
    others = lax.ppermute(sums, "seq", partner)
    joined = join(keep, got, sums, others, shards // 2)
    joined = lax.all_to_all(joined, "seq", 0, 0, tiled=True, axis_index_groups=chips)
    parts, scale, loss = scales(joined, packed, place, slots, shards)
    parts = lax.all_to_all(
        parts.reshape((-1,) + parts.shape[2:]), ("dp", "seq"), 0, 0, tiled=True
    )
    video_grad = keys(scale, khat, packed, float(frames * P_SIZE))
    pair_loss = loss[:, :, ::slots].reshape(-1, 1)
    parts, video_grad, pair_loss = lax.optimization_barrier((parts, video_grad, pair_loss))
    summed = totals(parts.reshape((blocks, shards) + parts.shape[1:]), float(slots))
    query_grad = weave(place, summed, lax.ppermute(summed, "seq", partner))
    return (
        video_grad.reshape(1, frames, patch_loc, E),
        query_grad.reshape(query_dev, slots, E),
        pair_loss,
    )


def solution(mesh):
    placed = (
        P("dp", "seq", None, None),
        P(),
        P(),
        P(),
        P(),
        P(),
        P("dp", None, None),
        P("dp"),
        P("dp"),
    )
    return jax.shard_map(
        body,
        mesh=mesh,
        in_specs=placed,
        out_specs=(P("dp", None, "seq", None), P("dp", None, None), P(None, "dp")),
        check_vma=False,
    )
```

```python
import jax
import jax.numpy as jnp
from jax import lax
from jax.experimental import pallas as pl
from jax.experimental.pallas import tpu as pltpu
from jax.sharding import PartitionSpec as P

HEADS = 12
P_SIZE = 256
TEMPER = 0.05
SLOPE = 10.0
OFFSET = -5.0
SHARP = 10.0
LOG2E = 1.4426950408889634

D = 768
HEAD = D // HEADS
PAIR = 2 * HEAD
PAIRS = HEADS // 2
TILE = 256
SUB = 128
E = 128
F32 = jnp.float32
BF16 = jnp.bfloat16
VMEM = pl.BlockSpec(memory_space=pltpu.VMEM)
SMEM = pl.BlockSpec(memory_space=pltpu.SMEM)
HBM = pl.BlockSpec(memory_space=pltpu.HBM)


def limit(mib):
    return pltpu.CompilerParams(vmem_limit_bytes=mib * 2**20)


def dot(a, b):
    return lax.dot_general(a, b, (((1,), (0,)), ((), ())), preferred_element_type=F32)


def dot_t(a, b):
    return lax.dot_general(a, b, (((1,), (1,)), ((), ())), preferred_element_type=F32)


def iota(shape, dim):
    return lax.broadcasted_iota(jnp.int32, shape, dim)


def layer_norm(tokens):
    values = tokens.astype(F32)
    center = values - jnp.mean(values, axis=-1, keepdims=True)
    spread = jnp.mean(center * center, axis=-1, keepdims=True)
    return (center * lax.rsqrt(spread + 1e-05)).astype(BF16)


def unit_heads(values, gain):
    same = (iota((TILE, TILE), 0) // HEAD == iota((TILE, TILE), 1) // HEAD).astype(BF16)
    parts = []
    for at in range(0, values.shape[1], TILE):
        part = values[:, at : at + TILE]
        squares = dot((part * part).astype(BF16), same)
        parts.append((part * (lax.rsqrt(squares + 1e-06) * gain)).astype(BF16))
    return jnp.concatenate(parts, axis=1)


def pair_blend(query, key, value, keep):
    extent = key.shape[0]
    low = iota((extent, PAIR), 1) < HEAD
    zero = jnp.zeros((extent, PAIR), BF16)
    one = jnp.ones((extent, PAIR), BF16)
    keys = jnp.concatenate([jnp.where(low, key, zero), jnp.where(low, zero, key)], axis=0)
    values = jnp.concatenate(
        [
            jnp.concatenate([jnp.where(low, value, zero), jnp.where(low, one, zero)], axis=1),
            jnp.concatenate([jnp.where(low, zero, value), jnp.where(low, zero, one)], axis=1),
        ],
        axis=0,
    )
    weights = jnp.exp2(dot_t(query, keys))
    if keep is not None:
        weights = jnp.where(keep, weights, 0.0)
    mixed = dot(weights.astype(BF16), values)
    return (mixed[:, :PAIR] / mixed[:, PAIR:]).astype(BF16)


def fetch(pairs, sem):
    copies = [pltpu.make_async_copy(a, b, sem.at[i]) for i, (a, b) in enumerate(pairs)]
    for copy in copies:
        copy.start()
    return copies


def columns(ref, third):
    return ref.at[:, pl.ds(third * D, D)]


def in_hbm(*arrays):
    return [pltpu.with_memory_space_constraint(array, pltpu.HBM) for array in arrays]


def qkv_all(normed, weight_s, copies, outs):
    for third, (out, gain) in enumerate(zip(outs, (SHARP * LOG2E, 1.0, None))):
        copies[third].wait()
        part = dot(normed, weight_s[:, third * D : (third + 1) * D])
        out[...] = part.astype(BF16) if gain is None else unit_heads(part, gain)


def space_kernel(
    video_ref, qkv_ref, out_w_ref, out_ref, x_s, qkv_s, w_s, n_s, q_s, k_s, v_s, y_s, sem, out_sem
):
    frames, patches, _ = x_s.shape
    video = fetch([(video_ref.at[f], x_s.at[f]) for f in range(frames)], sem)
    weights = fetch(
        [(columns(qkv_ref, i), columns(qkv_s, i)) for i in range(3)] + [(out_w_ref, w_s)],
        sem.at[pl.ds(frames, 4)],
    )
    for f in range(frames):
        video[f].wait()
        n_s[f * patches : (f + 1) * patches, :] = layer_norm(x_s[f])
    qkv_all(n_s[...], qkv_s, weights, (q_s, k_s, v_s))
    weights[3].wait()
    stores = []
    for f in range(frames):
        down = slice(f * patches, (f + 1) * patches)
        blended = []
        for pair in range(PAIRS):
            at = slice(pair * PAIR, (pair + 1) * PAIR)
            blended.append(pair_blend(q_s[down, at], k_s[down, at], v_s[down, at], None))
        update = dot(jnp.concatenate(blended, axis=1), w_s[...])
        y_s[f] = (x_s[f].astype(F32) + update).astype(BF16).reshape(y_s.shape[1:])
        stores.append(pltpu.make_async_copy(y_s.at[f], out_ref.at[:, f], out_sem.at[f]))
        stores[-1].start()
    for store in stores:
        store.wait()


def space(video, qkv_weight, out_weight, shards):
    frames, patches, _ = video.shape
    local = patches // shards
    return pl.pallas_call(
        space_kernel,
        in_specs=[HBM] * 3,
        out_specs=HBM,
        out_shape=pltpu.HBM((shards, frames, local, D), BF16),
        scratch_shapes=[
            pltpu.VMEM((frames, patches, D), BF16),
            pltpu.VMEM((D, 3 * D), BF16),
            pltpu.VMEM((D, D), BF16),
        ]
        + [pltpu.VMEM((frames * patches, D), BF16)] * 4
        + [
            pltpu.VMEM((frames, shards, local, D), BF16),
            pltpu.SemaphoreType.DMA((frames + 4,)),
            pltpu.SemaphoreType.DMA((frames,)),
        ],
        compiler_params=limit(40),
        name="space",
    )(*in_hbm(video, qkv_weight, out_weight))


def swap_rows(rows, side):
    extent = side * side
    row, col = iota((extent, extent), 0), iota((extent, extent), 1)
    swap = (col == (row % side) * side + row // side).astype(BF16)
    return dot(swap, rows).astype(BF16)


def time_kernel(
    x_ref, qkv_ref, out_w_ref, proj_ref, khat_ref,
    x_s, n_s, qkv_s, w_s, p_s, q_s, k_s, v_s, b_s, kh_s, sem,
):
    side, frames, _ = x_s.shape
    rows = x_ref.shape[0]
    weights = fetch(
        [(columns(qkv_ref, i), columns(qkv_s, i)) for i in range(3)]
        + [(out_w_ref, w_s), (proj_ref, p_s)],
        sem,
    )
    for tile in range(rows // TILE):
        tokens = swap_rows(x_ref[tile * TILE : (tile + 1) * TILE, :], side)
        at = slice(tile * side, (tile + 1) * side)
        x_s[:, at, :] = tokens.reshape(side, side, D)
        n_s[:, at, :] = layer_norm(tokens).reshape(side, side, D)
    qkv_all(n_s[...].reshape(rows, D), qkv_s, weights, (q_s, k_s, v_s))
    keep = iota((SUB, 2 * SUB), 0) // frames == (iota((SUB, 2 * SUB), 1) % SUB) // frames
    for sub in range(rows // SUB):
        down = slice(sub * SUB, (sub + 1) * SUB)
        for pair in range(PAIRS):
            at = slice(pair * PAIR, (pair + 1) * PAIR)
            b_s[down, at] = pair_blend(q_s[down, at], k_s[down, at], v_s[down, at], keep)
    weights[3].wait()
    weights[4].wait()
    update = dot(b_s[...], w_s[...])
    mixed = (x_s[...].reshape(rows, D).astype(F32) + update).astype(BF16)
    projected = dot(layer_norm(mixed), p_s[...])
    norm = jnp.sum(projected * projected, axis=-1, keepdims=True)
    kh_s[...] = (projected * lax.rsqrt(norm + 1e-06)).astype(BF16).reshape(kh_s.shape)
    for tile in range(rows // TILE):
        part = kh_s[:, tile * side : (tile + 1) * side, :].reshape(TILE, E)
        khat_ref[tile * TILE : (tile + 1) * TILE, :] = swap_rows(part, side)


def time(x, qkv_weight, out_weight, proj_weight, patches):
    rows = x.shape[0]
    frames = rows // patches
    return pl.pallas_call(
        time_kernel,
        in_specs=[VMEM] + [HBM] * 3,
        out_specs=VMEM,
        out_shape=jax.ShapeDtypeStruct((rows, E), BF16),
        scratch_shapes=[
            pltpu.VMEM((patches, frames, D), BF16),
            pltpu.VMEM((patches, frames, D), BF16),
            pltpu.VMEM((D, 3 * D), BF16),
            pltpu.VMEM((D, D), BF16),
            pltpu.VMEM((D, E), BF16),
        ]
        + [pltpu.VMEM((rows, D), BF16)] * 4
        + [pltpu.VMEM((patches, frames, E), BF16), pltpu.SemaphoreType.DMA((5,))],
        compiler_params=limit(40),
        name="time",
    )(x, *in_hbm(qkv_weight, out_weight, proj_weight))


EXTRA = 16


def query_kernel(len_ref, pos_ref, q_ref, out_ref):
    rows = q_ref.shape[0]
    values = q_ref[...].astype(F32)
    norm = jnp.sum(values * values, axis=-1, keepdims=True)
    out_ref[:rows, :] = (values / jnp.sqrt(norm + 1e-06)).astype(BF16)
    slots = rows // len_ref.shape[0]
    row, lane = iota((EXTRA, E), 0), iota((EXTRA, E), 1)
    owner = ((row % 2) * E + lane) // slots
    extra = jnp.zeros((EXTRA, E), F32)
    for query in range(len_ref.shape[0]):
        picked = jnp.where(row < 2, len_ref[query], pos_ref[query]).astype(F32)
        extra = jnp.where((owner == query) & (row < 4), picked, extra)
    out_ref[rows:, :] = extra.astype(BF16)


def pack_queries(queries, query_len, positive):
    rows = queries.shape[0]
    return pl.pallas_call(
        query_kernel,
        in_specs=[SMEM, SMEM, VMEM],
        out_specs=VMEM,
        out_shape=jax.ShapeDtypeStruct((rows + EXTRA, E), BF16),
        compiler_params=limit(4),
        name="pack_queries",
    )(query_len, positive, queries)


def own_place():
    seat = lax.axis_index("seq")
    return lax.axis_index("dp"), lax.rem(seat, 2), seat // 2


def group_of(mine, blocks, block):
    side, step = divmod(block, blocks // 2)
    return lax.rem(mine + blocks - 2 * step, blocks) ^ side


def block_of(packed_refs, block):
    side, step = divmod(block, packed_refs[0].shape[0])
    return packed_refs[side].at[step]


def expo_terms(query, khat):
    gain = LOG2E / TEMPER
    return jnp.exp2(dot_t(query, khat) * gain - gain).astype(BF16)


def terms_kernel(blocks, khat_ref, *refs):
    packed_refs, (keep_ref, send_ref, sums_ref) = refs[:-3], refs[-3:]
    rows = packed_refs[0].shape[1] - EXTRA
    first = own_place()[1] == 0
    khat = khat_ref[...]
    wide = jnp.concatenate([khat, jnp.ones_like(khat)], axis=1)
    eye = iota((E, E), 0) == iota((E, E), 1)
    sums = []
    for block in range(blocks):
        both = dot(expo_terms(block_of(packed_refs, block)[:rows, :], khat), wide)
        low, high = both[:E, :E], both[E:, :E]
        keep_ref[block] = jnp.where(first, low, high)
        send_ref[block] = jnp.where(first, high, low).astype(BF16)
        for part in range(rows // E):
            square = both[part * E : (part + 1) * E, E:]
            sums.append(jnp.sum(jnp.where(eye, square, 0.0), axis=0, keepdims=True))
    sums_ref[...] = jnp.concatenate(sums, axis=0)


def terms(packed, khat):
    blocks, rows = 2 * packed[0].shape[0], packed[0].shape[1] - EXTRA
    return pl.pallas_call(
        lambda *refs: terms_kernel(blocks, *refs),
        in_specs=[VMEM] * (1 + len(packed)),
        out_specs=[VMEM] * 3,
        out_shape=[
            jax.ShapeDtypeStruct((blocks, rows // 2, E), F32),
            jax.ShapeDtypeStruct((blocks, rows // 2, E), BF16),
            jax.ShapeDtypeStruct((blocks * rows // E, E), F32),
        ],
        compiler_params=limit(16),
        name="terms",
    )(khat, *packed)


def join_kernel(keep_ref, got_ref, sums_ref, others_ref, out_ref):
    blocks, half, _ = keep_ref.shape
    chips = out_ref.shape[0]
    piece = half // chips
    sums = sums_ref[...] + others_ref[...]
    upper = sums.astype(BF16)
    lower = (sums - upper.astype(F32)).astype(BF16)
    notes = jnp.concatenate([upper, lower], axis=0)
    for block in range(blocks):
        both = (keep_ref[block] + got_ref[block].astype(F32)).astype(BF16)
        for chip in range(chips):
            out_ref[chip, block * piece : (block + 1) * piece, :] = both[
                chip * piece : (chip + 1) * piece
            ]
    for chip in range(chips):
        out_ref[chip, blocks * piece :, :] = notes


def join(keep, got, sums, others, chips):
    blocks, half, _ = keep.shape
    return pl.pallas_call(
        join_kernel,
        in_specs=[VMEM] * 4,
        out_specs=VMEM,
        out_shape=jax.ShapeDtypeStruct(
            (chips, blocks * half // chips + 2 * sums.shape[0], E), BF16
        ),
        compiler_params=limit(8),
        name="join",
    )(keep, got, sums, others)


def scale_kernel(slots, got_ref, *refs):
    packed_refs, (part_ref, scale_ref, loss_ref) = refs[:-3], refs[-3:]
    blocks, shards, share, _ = part_ref.shape
    piece = 2 * share
    video, core, chip = own_place()
    rows = packed_refs[0].shape[1] - EXTRA
    per = rows // E
    got = jnp.sum(got_ref[...].astype(F32), axis=0)
    blend, notes = got[: blocks * piece], got[blocks * piece :]
    total = notes[: blocks * per] + notes[blocks * per :]
    notes = [block_of(packed_refs, b)[rows:, :].astype(F32) for b in range(blocks)]
    lens = jnp.concatenate([note[:per] for note in notes], axis=0)
    pos = jnp.concatenate([note[per : 2 * per] for note in notes], axis=0)
    mask = ((iota(total.shape, 1) % slots).astype(F32) < lens).astype(F32)
    smooth = (1.0 + TEMPER * jnp.log(total)) * mask
    same = (iota((E, E), 0) // slots == iota((E, E), 1) // slots).astype(F32)
    score = (
        lax.dot_general(
            smooth,
            same,
            (((1,), (0,)), ((), ())),
            preferred_element_type=F32,
            precision=lax.Precision.HIGHEST,
        )
        / lens
    )
    sign = jnp.where(pos == video.astype(F32), 1.0, -1.0)
    margin = sign * (SLOPE * score + OFFSET)
    loss = jnp.maximum(-margin, 0.0) + jnp.log1p(jnp.exp(-jnp.abs(margin)))
    coeff = -SLOPE * sign / (1.0 + jnp.exp(margin)) * mask / lens
    scale_ref[...] = (coeff / total).T
    scale = scale_ref[pl.ds(pl.multiple_of(chip * piece, piece), piece), :]
    first = core == 0
    for block in range(blocks):
        group = group_of(video, blocks, block)
        at = block * per
        column = jnp.where(first, scale[:, at : at + 1], scale[:, at + 1 : at + 2])
        part = (blend[block * piece : (block + 1) * piece] * column).astype(BF16)
        for shard in range(shards):
            part_ref[group, shard] = part[shard % 2 * share : (shard % 2 + 1) * share]
        loss_ref[group] = loss[at : at + per]


def scales(got, packed, slots, shards):
    blocks, rows = 2 * packed[0].shape[0], packed[0].shape[1] - EXTRA
    share = rows // shards // 2
    return pl.pallas_call(
        lambda *refs: scale_kernel(slots, *refs),
        in_specs=[VMEM] * (1 + len(packed)),
        out_specs=[VMEM] * 3,
        out_shape=[
            jax.ShapeDtypeStruct((blocks, shards, share, E), BF16),
            jax.ShapeDtypeStruct((E, blocks * rows // E), F32),
            jax.ShapeDtypeStruct((blocks, rows // E, E), F32),
        ],
        compiler_params=limit(8),
        name="scales",
    )(got, *packed)


def keys_kernel(gain, blocks, scale_ref, khat_ref, *refs):
    packed_refs, out_ref = refs[:-1], refs[-1]
    khat = khat_ref[...]
    rows = packed_refs[0].shape[1] - EXTRA
    per = rows // E
    total = jnp.zeros((E, khat.shape[0]), F32)
    for block in range(blocks):
        query = block_of(packed_refs, block)[:rows, :]
        parts = []
        for part in range(per):
            at = block * per + part
            scaled = query[part * E : (part + 1) * E].astype(F32) * scale_ref[:, at : at + 1]
            parts.append(scaled.T.astype(BF16))
        total = total + dot(jnp.concatenate(parts, axis=1), expo_terms(query, khat))
    out_ref[...] = (total.T * gain).astype(BF16)


def keys(scale, khat, packed, gain):
    return pl.pallas_call(
        lambda *refs: keys_kernel(gain, 2 * packed[0].shape[0], *refs),
        in_specs=[VMEM] * (2 + len(packed)),
        out_specs=VMEM,
        out_shape=jax.ShapeDtypeStruct(khat.shape, BF16),
        compiler_params=limit(16),
        name="keys",
    )(scale, khat, *packed)


def total_kernel(gain, in_ref, out_ref):
    out_ref[...] = (jnp.sum(in_ref[...].astype(F32), axis=0) * gain).astype(BF16)


def totals(parts, gain):
    return pl.pallas_call(
        lambda *refs: total_kernel(gain, *refs),
        in_specs=[VMEM],
        out_specs=VMEM,
        out_shape=jax.ShapeDtypeStruct(parts.shape[1:], BF16),
        compiler_params=limit(4),
        name="totals",
    )(parts)


def weave_kernel(mine_ref, other_ref, out_ref):
    shards, share, _ = mine_ref.shape
    first = own_place()[1] == 0
    for shard in range(shards):
        at = ((shard % 2) * (shards // 2) + shard // 2) * 2 * share
        mine, other = mine_ref[shard], other_ref[shard]
        out_ref[at : at + share, :] = jnp.where(first, mine, other)
        out_ref[at + share : at + 2 * share, :] = jnp.where(first, other, mine)


def weave(mine, other):
    shards, share, _ = mine.shape
    return pl.pallas_call(
        weave_kernel,
        in_specs=[VMEM, VMEM],
        out_specs=VMEM,
        out_shape=jax.ShapeDtypeStruct((2 * shards * share, E), BF16),
        compiler_params=limit(4),
        name="weave",
    )(mine, other)


def body(
    video, space_qkv, space_out, time_qkv, time_out, proj_weight, queries, query_len, positive
):
    _, frames_dev, patches, _ = video.shape
    shards = lax.axis_size("seq")
    blocks = lax.axis_size("dp")
    patch_loc = patches // shards
    frames = frames_dev * shards
    query_dev, slots, _ = queries.shape
    rows = query_dev * slots
    partner = [(i, i ^ 1) for i in range(shards)]
    chips = [[2 * chip + own for chip in range(shards // 2)] for own in range(2)]

    spatial = space(video[0], space_qkv, space_out, shards)
    spatial, flat = lax.optimization_barrier((spatial, queries.reshape(rows, E)))
    items = lax.all_to_all(spatial, "seq", 0, 0, tiled=True)
    mine = pack_queries(flat, query_len, positive)
    lane = jnp.stack(
        [mine]
        + [
            lax.ppermute(mine, "dp", [(i, (i + by) % blocks) for i in range(blocks)])
            for by in range(2, blocks, 2)
        ]
    )
    items, lane = lax.optimization_barrier((items, lane))
    packed = [lane, lax.ppermute(lane, "dp", [(i, i ^ 1) for i in range(blocks)])]
    khat = time(items.reshape(-1, D), time_qkv, time_out, proj_weight, patch_loc)

    keep, send, sums = terms(packed, khat)
    got = lax.ppermute(send, "seq", partner)
    others = lax.ppermute(sums, "seq", partner)
    joined = join(keep, got, sums, others, shards // 2)
    joined = lax.all_to_all(joined, "seq", 0, 0, tiled=True, axis_index_groups=chips)
    parts, scale, loss = scales(joined, packed, slots, shards)
    parts = lax.all_to_all(
        parts.reshape((-1,) + parts.shape[2:]), ("dp", "seq"), 0, 0, tiled=True
    )
    video_grad = keys(scale, khat, packed, float(frames * P_SIZE))
    parts, video_grad = lax.optimization_barrier((parts, video_grad))
    summed = totals(parts.reshape((blocks, shards) + parts.shape[1:]), float(slots))
    query_grad = weave(summed, lax.ppermute(summed, "seq", partner))
    return (
        video_grad.reshape(1, frames, patch_loc, E),
        query_grad.reshape(query_dev, slots, E),
        loss[:, :, ::slots].reshape(-1, 1),
    )


def solution(mesh):
    placed = (
        P("dp", "seq", None, None),
        P(),
        P(),
        P(),
        P(),
        P(),
        P("dp", None, None),
        P("dp"),
        P("dp"),
    )
    return jax.shard_map(
        body,
        mesh=mesh,
        in_specs=placed,
        out_specs=(P("dp", None, "seq", None), P("dp", None, None), P(None, "dp")),
        check_vma=False,
    )
```

```python
import jax
import jax.numpy as jnp
from jax import lax
from jax.experimental import pallas as pl
from jax.experimental.pallas import tpu as pltpu
from jax.sharding import PartitionSpec as P

HEADS = 12
P_SIZE = 256
TEMPER = 0.05
SLOPE = 10.0
OFFSET = -5.0
SHARP = 10.0
LOG2E = 1.4426950408889634

D = 768
HEAD = D // HEADS
PAIR = 2 * HEAD
PAIRS = HEADS // 2
TILE = 256
SUB = 128
E = 128
F32 = jnp.float32
BF16 = jnp.bfloat16
VMEM = pl.BlockSpec(memory_space=pltpu.VMEM)
SMEM = pl.BlockSpec(memory_space=pltpu.SMEM)
HBM = pl.BlockSpec(memory_space=pltpu.HBM)


def limit(mib):
    return pltpu.CompilerParams(vmem_limit_bytes=mib * 2**20)


def dot(a, b):
    return lax.dot_general(a, b, (((1,), (0,)), ((), ())), preferred_element_type=F32)


def dot_t(a, b):
    return lax.dot_general(a, b, (((1,), (1,)), ((), ())), preferred_element_type=F32)


def iota(shape, dim):
    return lax.broadcasted_iota(jnp.int32, shape, dim)


def layer_norm(tokens):
    values = tokens.astype(F32)
    center = values - jnp.mean(values, axis=-1, keepdims=True)
    spread = jnp.mean(center * center, axis=-1, keepdims=True)
    return (center * lax.rsqrt(spread + 1e-05)).astype(BF16)


def unit_heads(values, gain):
    same = (iota((TILE, TILE), 0) // HEAD == iota((TILE, TILE), 1) // HEAD).astype(BF16)
    parts = []
    for at in range(0, values.shape[1], TILE):
        part = values[:, at : at + TILE]
        squares = dot((part * part).astype(BF16), same)
        parts.append((part * (lax.rsqrt(squares + 1e-06) * gain)).astype(BF16))
    return jnp.concatenate(parts, axis=1)


def pair_scores(query, key):
    extent = key.shape[0]
    low = iota((extent, PAIR), 1) < HEAD
    zero = jnp.zeros((extent, PAIR), BF16)
    keys = jnp.concatenate([jnp.where(low, key, zero), jnp.where(low, zero, key)], axis=0)
    return dot_t(query, keys)


def pair_mix(scores, value, keep):
    extent = value.shape[0]
    low = iota((extent, PAIR), 1) < HEAD
    zero = jnp.zeros((extent, PAIR), BF16)
    one = jnp.ones((extent, PAIR), BF16)
    values = jnp.concatenate(
        [
            jnp.concatenate([jnp.where(low, value, zero), jnp.where(low, one, zero)], axis=1),
            jnp.concatenate([jnp.where(low, zero, value), jnp.where(low, zero, one)], axis=1),
        ],
        axis=0,
    )
    weights = jnp.exp2(scores).astype(BF16)
    if keep is not None:
        weights = jnp.where(keep, weights, jnp.zeros_like(weights))
    return dot(weights, values)


def pair_done(mixed):
    return (mixed[:, :PAIR] / mixed[:, PAIR:]).astype(BF16)


class Flat:
    def __init__(self, ref):
        self.ref = ref

    def __getitem__(self, at):
        down, across = at
        extent = self.ref.shape[1]
        part = self.ref[down.start // extent : down.stop // extent, :, across]
        return part.reshape(down.stop - down.start, part.shape[-1])


def blend_all(units, q_s, k_s, v_s, keep, put):
    scores, mixes = {}, {}
    for i in range(len(units) + 2):
        if i < len(units):
            d, a = units[i]
            scores[i] = pair_scores(q_s[d, a], k_s[d, a])
        if 0 <= i - 1 < len(units):
            d, a = units[i - 1]
            mixes[i - 1] = pair_mix(scores.pop(i - 1), v_s[d, a], keep)
        if 0 <= i - 2:
            put(units[i - 2], pair_done(mixes.pop(i - 2)))


def fetch(pairs, sem):
    copies = [pltpu.make_async_copy(a, b, sem.at[i]) for i, (a, b) in enumerate(pairs)]
    for copy in copies:
        copy.start()
    return copies


def columns(ref, third):
    return ref.at[:, pl.ds(third * D, D)]


def in_hbm(*arrays):
    return [pltpu.with_memory_space_constraint(array, pltpu.HBM) for array in arrays]


def qkv_all(chunks, weight_s, copies, outs):
    queue = []

    def flush():
        part, out, gain, at = queue.pop(0)
        part = part.astype(BF16) if gain is None else unit_heads(part, gain)
        out[at] = part.reshape(out[at].shape)

    for third, (out, gain) in enumerate(zip(outs, (SHARP * LOG2E, 1.0, None))):
        copies[third].wait()
        for at, rows in chunks:
            part = dot(rows(third), weight_s[:, third * D : (third + 1) * D])
            queue.append((part, out, gain, at))
            if len(queue) > 1:
                flush()
    while queue:
        flush()


def space_kernel(
    video_ref, qkv_ref, out_w_ref, out_ref, x_s, qkv_s, w_s, n_s, q_s, k_s, v_s, y_s, sem, out_sem
):
    frames, patches, _ = x_s.shape
    video = fetch([(video_ref.at[f], x_s.at[f]) for f in range(frames)], sem)
    weights = fetch(
        [(columns(qkv_ref, i), columns(qkv_s, i)) for i in range(3)] + [(out_w_ref, w_s)],
        sem.at[pl.ds(frames, 4)],
    )
    for f in range(frames):
        video[f].wait()
        n_s[f * patches : (f + 1) * patches, :] = layer_norm(x_s[f])
    chunks = [
        (slice(at, at + 128), lambda third, at=at: n_s[at : at + 128, :])
        for at in range(0, frames * patches, 128)
    ]
    qkv_all(chunks, qkv_s, weights, (q_s, k_s, v_s))
    weights[3].wait()
    units = [
        (slice(f * patches, (f + 1) * patches), slice(pair * PAIR, (pair + 1) * PAIR))
        for f in range(frames)
        for pair in range(PAIRS)
    ]
    stores = []

    def put(unit, blended):
        n_s[unit] = blended
        if unit[1].stop < D:
            return
        f = unit[0].start // patches
        update = dot(n_s[unit[0], :], w_s[...])
        y_s[f] = (x_s[f].astype(F32) + update).astype(BF16).reshape(y_s.shape[1:])
        stores.append(pltpu.make_async_copy(y_s.at[f], out_ref.at[:, f], out_sem.at[f]))
        stores[-1].start()

    blend_all(units, q_s, k_s, v_s, None, put)
    for store in stores:
        store.wait()


def space(video, qkv_weight, out_weight, shards):
    frames, patches, _ = video.shape
    local = patches // shards
    return pl.pallas_call(
        space_kernel,
        in_specs=[HBM] * 3,
        out_specs=HBM,
        out_shape=pltpu.HBM((shards, frames, local, D), BF16),
        scratch_shapes=[
            pltpu.VMEM((frames, patches, D), BF16),
            pltpu.VMEM((D, 3 * D), BF16),
            pltpu.VMEM((D, D), BF16),
        ]
        + [pltpu.VMEM((frames * patches, D), BF16)] * 4
        + [
            pltpu.VMEM((frames, shards, local, D), BF16),
            pltpu.SemaphoreType.DMA((frames + 4,)),
            pltpu.SemaphoreType.DMA((frames,)),
        ],
        compiler_params=limit(40),
        name="space",
    )(*in_hbm(video, qkv_weight, out_weight))


def swap_rows(rows, side):
    extent = side * side
    row, col = iota((extent, extent), 0), iota((extent, extent), 1)
    swap = (col == (row % side) * side + row // side).astype(BF16)
    return dot(swap, rows).astype(BF16)


def time_kernel(
    x_ref, qkv_ref, out_w_ref, proj_ref, khat_ref,
    x_s, n_s, qkv_s, w_s, p_s, q_s, k_s, v_s, b_s, kh_s, sem,
):
    side, frames, _ = x_s.shape
    rows = x_ref.shape[0]
    weights = fetch(
        [(columns(qkv_ref, i), columns(qkv_s, i)) for i in range(3)]
        + [(out_w_ref, w_s), (proj_ref, p_s)],
        sem,
    )
    for tile in range(rows // TILE):
        tokens = swap_rows(x_ref[tile * TILE : (tile + 1) * TILE, :], side)
        at = slice(tile * side, (tile + 1) * side)
        x_s[:, at, :] = tokens.reshape(side, side, D)
        n_s[:, at, :] = layer_norm(tokens).reshape(side, side, D)
    chunks = [
        (
            (slice(at // frames, (at + 128) // frames), slice(None), slice(None)),
            lambda third, at=at: n_s[at // frames : (at + 128) // frames].reshape(128, D),
        )
        for at in range(0, rows, 128)
    ]
    qkv_all(chunks, qkv_s, weights, (q_s, k_s, v_s))
    keep = iota((SUB, 2 * SUB), 0) // frames == (iota((SUB, 2 * SUB), 1) % SUB) // frames
    weights[3].wait()
    weights[4].wait()

    def finish(down):
        groups = slice(down.start // frames, down.stop // frames)
        tokens = x_s[groups].reshape(down.stop - down.start, D)
        update = dot(b_s[down, :], w_s[...])
        mixed = (tokens.astype(F32) + update).astype(BF16)
        projected = dot(layer_norm(mixed), p_s[...])
        norm = jnp.sum(projected * projected, axis=-1, keepdims=True)
        unit = (projected * lax.rsqrt(norm + 1e-06)).astype(BF16)
        kh_s[groups] = unit.reshape(kh_s[groups].shape)

    def put(unit, blended):
        b_s[unit] = blended
        stop = unit[0].stop
        if unit[1].stop == D and stop % 1024 == 0:
            finish(slice(stop - 1024, stop))

    units = [
        (slice(at, at + SUB), slice(pair * PAIR, (pair + 1) * PAIR))
        for at in range(0, rows, SUB)
        for pair in range(PAIRS)
    ]
    blend_all(units, Flat(q_s), Flat(k_s), Flat(v_s), keep, put)
    for tile in range(rows // TILE):
        part = kh_s[:, tile * side : (tile + 1) * side, :].reshape(TILE, E)
        khat_ref[tile * TILE : (tile + 1) * TILE, :] = swap_rows(part, side)


def time(x, qkv_weight, out_weight, proj_weight, patches):
    rows = x.shape[0]
    frames = rows // patches
    return pl.pallas_call(
        time_kernel,
        in_specs=[VMEM] + [HBM] * 3,
        out_specs=VMEM,
        out_shape=jax.ShapeDtypeStruct((rows, E), BF16),
        scratch_shapes=[
            pltpu.VMEM((patches, frames, D), BF16),
            pltpu.VMEM((patches, frames, D), BF16),
            pltpu.VMEM((D, 3 * D), BF16),
            pltpu.VMEM((D, D), BF16),
            pltpu.VMEM((D, E), BF16),
        ]
        + [pltpu.VMEM((patches, frames, D), BF16)] * 3
        + [pltpu.VMEM((rows, D), BF16)]
        + [pltpu.VMEM((patches, frames, E), BF16), pltpu.SemaphoreType.DMA((5,))],
        compiler_params=limit(40),
        name="time",
    )(x, *in_hbm(qkv_weight, out_weight, proj_weight))


EXTRA = 16


def query_kernel(len_ref, pos_ref, q_ref, out_ref):
    rows = q_ref.shape[0]
    values = q_ref[...].astype(F32)
    norm = jnp.sum(values * values, axis=-1, keepdims=True)
    out_ref[:rows, :] = (values / jnp.sqrt(norm + 1e-06)).astype(BF16)
    slots = rows // len_ref.shape[0]
    row, lane = iota((EXTRA, E), 0), iota((EXTRA, E), 1)
    owner = ((row % 2) * E + lane) // slots
    extra = jnp.zeros((EXTRA, E), F32)
    for query in range(len_ref.shape[0]):
        picked = jnp.where(row < 2, len_ref[query], pos_ref[query]).astype(F32)
        extra = jnp.where((owner == query) & (row < 4), picked, extra)
    out_ref[rows:, :] = extra.astype(BF16)


def pack_queries(queries, query_len, positive):
    rows = queries.shape[0]
    return pl.pallas_call(
        query_kernel,
        in_specs=[SMEM, SMEM, VMEM],
        out_specs=VMEM,
        out_shape=jax.ShapeDtypeStruct((rows + EXTRA, E), BF16),
        compiler_params=limit(4),
        name="pack_queries",
    )(query_len, positive, queries)


def own_place():
    seat = lax.axis_index("seq")
    return lax.axis_index("dp"), lax.rem(seat, 2), seat // 2


def group_of(mine, blocks, block):
    side, step = divmod(block, blocks // 2)
    return lax.rem(mine + blocks - 2 * step, blocks) ^ side


def block_of(packed_refs, block):
    side, step = divmod(block, packed_refs[0].shape[0])
    return packed_refs[side].at[step]


def expo_terms(query, khat):
    gain = LOG2E / TEMPER
    return jnp.exp2(dot_t(query, khat) * gain - gain).astype(BF16)


def terms_kernel(blocks, khat_ref, *refs):
    packed_refs, (keep_ref, send_ref, sums_ref) = refs[:-3], refs[-3:]
    rows = packed_refs[0].shape[1] - EXTRA
    first = own_place()[1] == 0
    khat = khat_ref[...]
    wide = jnp.concatenate([khat, jnp.ones_like(khat)], axis=1)
    eye = iota((E, E), 0) == iota((E, E), 1)
    sums = []
    for block in range(blocks):
        both = dot(expo_terms(block_of(packed_refs, block)[:rows, :], khat), wide)
        low, high = both[:E, :E], both[E:, :E]
        keep_ref[block] = jnp.where(first, low, high)
        send_ref[block] = jnp.where(first, high, low).astype(BF16)
        for part in range(rows // E):
            square = both[part * E : (part + 1) * E, E:]
            sums.append(jnp.sum(jnp.where(eye, square, 0.0), axis=0, keepdims=True))
    sums_ref[...] = jnp.concatenate(sums, axis=0)


def terms(packed, khat):
    blocks, rows = 2 * packed[0].shape[0], packed[0].shape[1] - EXTRA
    return pl.pallas_call(
        lambda *refs: terms_kernel(blocks, *refs),
        in_specs=[VMEM] * (1 + len(packed)),
        out_specs=[VMEM] * 3,
        out_shape=[
            jax.ShapeDtypeStruct((blocks, rows // 2, E), F32),
            jax.ShapeDtypeStruct((blocks, rows // 2, E), BF16),
            jax.ShapeDtypeStruct((blocks * rows // E, E), F32),
        ],
        compiler_params=limit(16),
        name="terms",
    )(khat, *packed)


def join_kernel(keep_ref, got_ref, sums_ref, others_ref, out_ref):
    blocks, half, _ = keep_ref.shape
    chips = out_ref.shape[0]
    piece = half // chips
    sums = sums_ref[...] + others_ref[...]
    upper = sums.astype(BF16)
    lower = (sums - upper.astype(F32)).astype(BF16)
    notes = jnp.concatenate([upper, lower], axis=0)
    for block in range(blocks):
        both = (keep_ref[block] + got_ref[block].astype(F32)).astype(BF16)
        for chip in range(chips):
            out_ref[chip, block * piece : (block + 1) * piece, :] = both[
                chip * piece : (chip + 1) * piece
            ]
    for chip in range(chips):
        out_ref[chip, blocks * piece :, :] = notes


def join(keep, got, sums, others, chips):
    blocks, half, _ = keep.shape
    return pl.pallas_call(
        join_kernel,
        in_specs=[VMEM] * 4,
        out_specs=VMEM,
        out_shape=jax.ShapeDtypeStruct(
            (chips, blocks * half // chips + 2 * sums.shape[0], E), BF16
        ),
        compiler_params=limit(8),
        name="join",
    )(keep, got, sums, others)


def scale_kernel(slots, got_ref, *refs):
    packed_refs, (part_ref, scale_ref, loss_ref) = refs[:-3], refs[-3:]
    blocks, shards, share, _ = part_ref.shape
    piece = 2 * share
    video, core, chip = own_place()
    rows = packed_refs[0].shape[1] - EXTRA
    per = rows // E
    got = jnp.sum(got_ref[...].astype(F32), axis=0)
    blend, notes = got[: blocks * piece], got[blocks * piece :]
    total = notes[: blocks * per] + notes[blocks * per :]
    notes = [block_of(packed_refs, b)[rows:, :].astype(F32) for b in range(blocks)]
    lens = jnp.concatenate([note[:per] for note in notes], axis=0)
    pos = jnp.concatenate([note[per : 2 * per] for note in notes], axis=0)
    mask = ((iota(total.shape, 1) % slots).astype(F32) < lens).astype(F32)
    smooth = (1.0 + TEMPER * jnp.log(total)) * mask
    same = (iota((E, E), 0) // slots == iota((E, E), 1) // slots).astype(F32)
    score = (
        lax.dot_general(
            smooth,
            same,
            (((1,), (0,)), ((), ())),
            preferred_element_type=F32,
            precision=lax.Precision.HIGHEST,
        )
        / lens
    )
    sign = jnp.where(pos == video.astype(F32), 1.0, -1.0)
    margin = sign * (SLOPE * score + OFFSET)
    loss = jnp.maximum(-margin, 0.0) + jnp.log1p(jnp.exp(-jnp.abs(margin)))
    coeff = -SLOPE * sign / (1.0 + jnp.exp(margin)) * mask / lens
    scale_ref[...] = (coeff / total).T
    scale = scale_ref[pl.ds(pl.multiple_of(chip * piece, piece), piece), :]
    first = core == 0
    for block in range(blocks):
        group = group_of(video, blocks, block)
        at = block * per
        column = jnp.where(first, scale[:, at : at + 1], scale[:, at + 1 : at + 2])
        part = (blend[block * piece : (block + 1) * piece] * column).astype(BF16)
        for shard in range(shards):
            part_ref[group, shard] = part[shard % 2 * share : (shard % 2 + 1) * share]
        loss_ref[group] = loss[at : at + per]


def scales(got, packed, slots, shards):
    blocks, rows = 2 * packed[0].shape[0], packed[0].shape[1] - EXTRA
    share = rows // shards // 2
    return pl.pallas_call(
        lambda *refs: scale_kernel(slots, *refs),
        in_specs=[VMEM] * (1 + len(packed)),
        out_specs=[VMEM] * 3,
        out_shape=[
            jax.ShapeDtypeStruct((blocks, shards, share, E), BF16),
            jax.ShapeDtypeStruct((E, blocks * rows // E), F32),
            jax.ShapeDtypeStruct((blocks, rows // E, E), F32),
        ],
        compiler_params=limit(8),
        name="scales",
    )(got, *packed)


def keys_kernel(gain, blocks, scale_ref, khat_ref, *refs):
    packed_refs, out_ref = refs[:-1], refs[-1]
    khat = khat_ref[...]
    rows = packed_refs[0].shape[1] - EXTRA
    per = rows // E
    total = jnp.zeros((E, khat.shape[0]), F32)
    for block in range(blocks):
        query = block_of(packed_refs, block)[:rows, :]
        parts = []
        for part in range(per):
            at = block * per + part
            scaled = query[part * E : (part + 1) * E].astype(F32) * scale_ref[:, at : at + 1]
            parts.append(scaled.T.astype(BF16))
        total = total + dot(jnp.concatenate(parts, axis=1), expo_terms(query, khat))
    out_ref[...] = (total.T * gain).astype(BF16)


def keys(scale, khat, packed, gain):
    return pl.pallas_call(
        lambda *refs: keys_kernel(gain, 2 * packed[0].shape[0], *refs),
        in_specs=[VMEM] * (2 + len(packed)),
        out_specs=VMEM,
        out_shape=jax.ShapeDtypeStruct(khat.shape, BF16),
        compiler_params=limit(16),
        name="keys",
    )(scale, khat, *packed)


def total_kernel(gain, in_ref, out_ref):
    out_ref[...] = (jnp.sum(in_ref[...].astype(F32), axis=0) * gain).astype(BF16)


def totals(parts, gain):
    return pl.pallas_call(
        lambda *refs: total_kernel(gain, *refs),
        in_specs=[VMEM],
        out_specs=VMEM,
        out_shape=jax.ShapeDtypeStruct(parts.shape[1:], BF16),
        compiler_params=limit(4),
        name="totals",
    )(parts)


def weave_kernel(mine_ref, other_ref, out_ref):
    shards, share, _ = mine_ref.shape
    first = own_place()[1] == 0
    for shard in range(shards):
        at = ((shard % 2) * (shards // 2) + shard // 2) * 2 * share
        mine, other = mine_ref[shard], other_ref[shard]
        out_ref[at : at + share, :] = jnp.where(first, mine, other)
        out_ref[at + share : at + 2 * share, :] = jnp.where(first, other, mine)


def weave(mine, other):
    shards, share, _ = mine.shape
    return pl.pallas_call(
        weave_kernel,
        in_specs=[VMEM, VMEM],
        out_specs=VMEM,
        out_shape=jax.ShapeDtypeStruct((2 * shards * share, E), BF16),
        compiler_params=limit(4),
        name="weave",
    )(mine, other)


def body(
    video, space_qkv, space_out, time_qkv, time_out, proj_weight, queries, query_len, positive
):
    _, frames_dev, patches, _ = video.shape
    shards = lax.axis_size("seq")
    blocks = lax.axis_size("dp")
    patch_loc = patches // shards
    frames = frames_dev * shards
    query_dev, slots, _ = queries.shape
    rows = query_dev * slots
    partner = [(i, i ^ 1) for i in range(shards)]
    chips = [[2 * chip + own for chip in range(shards // 2)] for own in range(2)]

    spatial = space(video[0], space_qkv, space_out, shards)
    spatial, flat = lax.optimization_barrier((spatial, queries.reshape(rows, E)))
    items = lax.all_to_all(spatial, "seq", 0, 0, tiled=True)
    mine = pack_queries(flat, query_len, positive)
    lane = jnp.stack(
        [mine]
        + [
            lax.ppermute(mine, "dp", [(i, (i + by) % blocks) for i in range(blocks)])
            for by in range(2, blocks, 2)
        ]
    )
    items, lane = lax.optimization_barrier((items, lane))
    packed = [lane, lax.ppermute(lane, "dp", [(i, i ^ 1) for i in range(blocks)])]
    khat = time(items.reshape(-1, D), time_qkv, time_out, proj_weight, patch_loc)

    keep, send, sums = terms(packed, khat)
    got = lax.ppermute(send, "seq", partner)
    others = lax.ppermute(sums, "seq", partner)
    joined = join(keep, got, sums, others, shards // 2)
    joined = lax.all_to_all(joined, "seq", 0, 0, tiled=True, axis_index_groups=chips)
    parts, scale, loss = scales(joined, packed, slots, shards)
    parts = lax.all_to_all(
        parts.reshape((-1,) + parts.shape[2:]), ("dp", "seq"), 0, 0, tiled=True
    )
    video_grad = keys(scale, khat, packed, float(frames * P_SIZE))
    parts, video_grad = lax.optimization_barrier((parts, video_grad))
    summed = totals(parts.reshape((blocks, shards) + parts.shape[1:]), float(slots))
    query_grad = weave(summed, lax.ppermute(summed, "seq", partner))
    return (
        video_grad.reshape(1, frames, patch_loc, E),
        query_grad.reshape(query_dev, slots, E),
        loss[:, :, ::slots].reshape(-1, 1),
    )


def solution(mesh):
    placed = (
        P("dp", "seq", None, None),
        P(),
        P(),
        P(),
        P(),
        P(),
        P("dp", None, None),
        P("dp"),
        P("dp"),
    )
    return jax.shard_map(
        body,
        mesh=mesh,
        in_specs=placed,
        out_specs=(P("dp", None, "seq", None), P("dp", None, None), P(None, "dp")),
        check_vma=False,
    )
```

```python
import jax
import jax.numpy as jnp
from jax import lax
from jax.experimental import pallas as pl
from jax.experimental.pallas import tpu as pltpu
from jax.sharding import PartitionSpec as P

HEADS = 12
P_SIZE = 256
TEMPER = 0.05
SLOPE = 10.0
OFFSET = -5.0
SHARP = 10.0
LOG2E = 1.4426950408889634

D = 768
HEAD = D // HEADS
PAIR = 2 * HEAD
PAIRS = HEADS // 2
TILE = 256
SUB = 128
E = 128
F32 = jnp.float32
BF16 = jnp.bfloat16
VMEM = pl.BlockSpec(memory_space=pltpu.VMEM)
SMEM = pl.BlockSpec(memory_space=pltpu.SMEM)
HBM = pl.BlockSpec(memory_space=pltpu.HBM)


def limit(mib):
    return pltpu.CompilerParams(vmem_limit_bytes=mib * 2**20)


def dot(a, b):
    return lax.dot_general(a, b, (((1,), (0,)), ((), ())), preferred_element_type=F32)


def dot_t(a, b):
    return lax.dot_general(a, b, (((1,), (1,)), ((), ())), preferred_element_type=F32)


def iota(shape, dim):
    return lax.broadcasted_iota(jnp.int32, shape, dim)


def layer_norm(tokens):
    values = tokens.astype(F32)
    center = values - jnp.mean(values, axis=-1, keepdims=True)
    spread = jnp.mean(center * center, axis=-1, keepdims=True)
    return (center * lax.rsqrt(spread + 1e-05)).astype(BF16)


def unit_heads(values, gain):
    same = (iota((TILE, TILE), 0) // HEAD == iota((TILE, TILE), 1) // HEAD).astype(BF16)
    parts = []
    for at in range(0, values.shape[1], TILE):
        part = values[:, at : at + TILE]
        squares = dot((part * part).astype(BF16), same)
        parts.append((part * (lax.rsqrt(squares + 1e-06) * gain)).astype(BF16))
    return jnp.concatenate(parts, axis=1)


def pair_scores(query, key):
    extent = key.shape[0]
    low = iota((extent, PAIR), 1) < HEAD
    zero = jnp.zeros((extent, PAIR), BF16)
    keys = jnp.concatenate([jnp.where(low, key, zero), jnp.where(low, zero, key)], axis=0)
    return dot_t(query, keys)


def pair_mix(scores, value, keep):
    extent = value.shape[0]
    low = iota((extent, PAIR), 1) < HEAD
    zero = jnp.zeros((extent, PAIR), BF16)
    one = jnp.ones((extent, PAIR), BF16)
    values = jnp.concatenate(
        [
            jnp.concatenate([jnp.where(low, value, zero), jnp.where(low, one, zero)], axis=1),
            jnp.concatenate([jnp.where(low, zero, value), jnp.where(low, zero, one)], axis=1),
        ],
        axis=0,
    )
    weights = jnp.exp2(scores).astype(BF16)
    if keep is not None:
        weights = jnp.where(keep, weights, jnp.zeros_like(weights))
    return dot(weights, values)


def pair_done(mixed):
    return (mixed[:, :PAIR] / mixed[:, PAIR:]).astype(BF16)


class Flat:
    def __init__(self, ref):
        self.ref = ref

    def __getitem__(self, at):
        down, across = at
        extent = self.ref.shape[1]
        part = self.ref[down.start // extent : down.stop // extent, :, across]
        return part.reshape(down.stop - down.start, part.shape[-1])


def blend_all(units, q_s, k_s, v_s, keep, put):
    scores, mixes = {}, {}
    for i in range(len(units) + 2):
        if i < len(units):
            d, a = units[i]
            scores[i] = pair_scores(q_s[d, a], k_s[d, a])
        if 0 <= i - 1 < len(units):
            d, a = units[i - 1]
            mixes[i - 1] = pair_mix(scores.pop(i - 1), v_s[d, a], keep)
        if 0 <= i - 2:
            put(units[i - 2], pair_done(mixes.pop(i - 2)))


def fetch(pairs, sem):
    copies = [pltpu.make_async_copy(a, b, sem.at[i]) for i, (a, b) in enumerate(pairs)]
    for copy in copies:
        copy.start()
    return copies


def columns(ref, third):
    return ref.at[:, pl.ds(third * D, D)]


def in_hbm(*arrays):
    return [pltpu.with_memory_space_constraint(array, pltpu.HBM) for array in arrays]


def qkv_all(chunks, weight_s, copies, outs):
    queue = []

    def flush():
        part, out, gain, at = queue.pop(0)
        part = part.astype(BF16) if gain is None else unit_heads(part, gain)
        out[at] = part.reshape(out[at].shape)

    for third, (out, gain) in enumerate(zip(outs, (SHARP * LOG2E, 1.0, None))):
        copies[third].wait()
        for at, rows in chunks:
            part = dot(rows(third), weight_s[:, third * D : (third + 1) * D])
            queue.append((part, out, gain, at))
            if len(queue) > 1:
                flush()
    while queue:
        flush()


def space_kernel(
    video_ref, qkv_ref, out_w_ref, out_ref, x_s, qkv_s, w_s, n_s, q_s, k_s, v_s, y_s, sem, out_sem
):
    frames, patches, _ = x_s.shape
    video = fetch([(video_ref.at[f], x_s.at[f]) for f in range(frames)], sem)
    weights = fetch(
        [(columns(qkv_ref, i), columns(qkv_s, i)) for i in range(3)] + [(out_w_ref, w_s)],
        sem.at[pl.ds(frames, 4)],
    )
    for f in range(frames):
        video[f].wait()
        n_s[f * patches : (f + 1) * patches, :] = layer_norm(x_s[f])
    chunks = [
        (slice(at, at + 128), lambda third, at=at: n_s[at : at + 128, :])
        for at in range(0, frames * patches, 128)
    ]
    qkv_all(chunks, qkv_s, weights, (q_s, k_s, v_s))
    weights[3].wait()
    units = [
        (slice(f * patches, (f + 1) * patches), slice(pair * PAIR, (pair + 1) * PAIR))
        for f in range(frames)
        for pair in range(PAIRS)
    ]
    stores = []

    def put(unit, blended):
        n_s[unit] = blended
        if unit[1].stop < D:
            return
        f = unit[0].start // patches
        update = dot(n_s[unit[0], :], w_s[...])
        y_s[f] = (x_s[f].astype(F32) + update).astype(BF16).reshape(y_s.shape[1:])
        stores.append(pltpu.make_async_copy(y_s.at[f], out_ref.at[:, f], out_sem.at[f]))
        stores[-1].start()

    blend_all(units, q_s, k_s, v_s, None, put)
    for store in stores:
        store.wait()


def space(video, qkv_weight, out_weight, shards):
    frames, patches, _ = video.shape
    local = patches // shards
    return pl.pallas_call(
        space_kernel,
        in_specs=[HBM] * 3,
        out_specs=HBM,
        out_shape=pltpu.HBM((shards, frames, local, D), BF16),
        scratch_shapes=[
            pltpu.VMEM((frames, patches, D), BF16),
            pltpu.VMEM((D, 3 * D), BF16),
            pltpu.VMEM((D, D), BF16),
        ]
        + [pltpu.VMEM((frames * patches, D), BF16)] * 4
        + [
            pltpu.VMEM((frames, shards, local, D), BF16),
            pltpu.SemaphoreType.DMA((frames + 4,)),
            pltpu.SemaphoreType.DMA((frames,)),
        ],
        compiler_params=limit(40),
        name="space",
    )(*in_hbm(video, qkv_weight, out_weight))


def swap_rows(rows, side):
    extent = side * side
    row, col = iota((extent, extent), 0), iota((extent, extent), 1)
    swap = (col == (row % side) * side + row // side).astype(BF16)
    return dot(swap, rows).astype(BF16)


def time_kernel(
    x_ref, qkv_ref, out_w_ref, proj_ref, khat_ref,
    x_s, n_s, qkv_s, w_s, p_s, q_s, k_s, v_s, b_s, kh_s, sem,
):
    side, frames, _ = x_s.shape
    rows = x_ref.shape[0]
    weights = fetch(
        [(columns(qkv_ref, i), columns(qkv_s, i)) for i in range(3)]
        + [(out_w_ref, w_s), (proj_ref, p_s)],
        sem,
    )
    for tile in range(rows // TILE):
        tokens = swap_rows(x_ref[tile * TILE : (tile + 1) * TILE, :], side)
        at = slice(tile * side, (tile + 1) * side)
        x_s[:, at, :] = tokens.reshape(side, side, D)
        n_s[:, at, :] = layer_norm(tokens).reshape(side, side, D)
    chunks = [
        (
            (slice(at // frames, (at + 128) // frames), slice(None), slice(None)),
            lambda third, at=at: n_s[at // frames : (at + 128) // frames].reshape(128, D),
        )
        for at in range(0, rows, 128)
    ]
    qkv_all(chunks, qkv_s, weights, (q_s, k_s, v_s))
    keep = iota((SUB, 2 * SUB), 0) // frames == (iota((SUB, 2 * SUB), 1) % SUB) // frames
    weights[3].wait()
    weights[4].wait()

    def put(unit, blended):
        b_s[unit] = blended

    units = [
        (slice(at, at + SUB), slice(pair * PAIR, (pair + 1) * PAIR))
        for at in range(0, rows, SUB)
        for pair in range(PAIRS)
    ]
    blend_all(units, Flat(q_s), Flat(k_s), Flat(v_s), keep, put)
    ahead = []

    def mixed(groups, update):
        tokens = x_s[groups].reshape(update.shape)
        normed = layer_norm((tokens.astype(F32) + update).astype(BF16))
        projected = dot(normed, p_s[...])
        norm = jnp.sum(projected * projected, axis=-1, keepdims=True)
        unit = (projected * lax.rsqrt(norm + 1e-06)).astype(BF16)
        kh_s[groups] = unit.reshape(kh_s[groups].shape)

    for at in range(0, rows, 256):
        groups = slice(at // frames, (at + 256) // frames)
        ahead.append((groups, dot(b_s[at : at + 256, :], w_s[...])))
        if len(ahead) > 1:
            mixed(*ahead.pop(0))
    mixed(*ahead.pop(0))
    for tile in range(rows // TILE):
        part = kh_s[:, tile * side : (tile + 1) * side, :].reshape(TILE, E)
        khat_ref[tile * TILE : (tile + 1) * TILE, :] = swap_rows(part, side)


def time(x, qkv_weight, out_weight, proj_weight, patches):
    rows = x.shape[0]
    frames = rows // patches
    return pl.pallas_call(
        time_kernel,
        in_specs=[VMEM] + [HBM] * 3,
        out_specs=VMEM,
        out_shape=jax.ShapeDtypeStruct((rows, E), BF16),
        scratch_shapes=[
            pltpu.VMEM((patches, frames, D), BF16),
            pltpu.VMEM((patches, frames, D), BF16),
            pltpu.VMEM((D, 3 * D), BF16),
            pltpu.VMEM((D, D), BF16),
            pltpu.VMEM((D, E), BF16),
        ]
        + [pltpu.VMEM((patches, frames, D), BF16)] * 3
        + [pltpu.VMEM((rows, D), BF16)]
        + [pltpu.VMEM((patches, frames, E), BF16), pltpu.SemaphoreType.DMA((5,))],
        compiler_params=limit(40),
        name="time",
    )(x, *in_hbm(qkv_weight, out_weight, proj_weight))


EXTRA = 16


def query_kernel(len_ref, pos_ref, q_ref, out_ref):
    rows = q_ref.shape[0]
    values = q_ref[...].astype(F32)
    norm = jnp.sum(values * values, axis=-1, keepdims=True)
    out_ref[:rows, :] = (values / jnp.sqrt(norm + 1e-06)).astype(BF16)
    slots = rows // len_ref.shape[0]
    row, lane = iota((EXTRA, E), 0), iota((EXTRA, E), 1)
    owner = ((row % 2) * E + lane) // slots
    extra = jnp.zeros((EXTRA, E), F32)
    for query in range(len_ref.shape[0]):
        picked = jnp.where(row < 2, len_ref[query], pos_ref[query]).astype(F32)
        extra = jnp.where((owner == query) & (row < 4), picked, extra)
    out_ref[rows:, :] = extra.astype(BF16)


def pack_queries(queries, query_len, positive):
    rows = queries.shape[0]
    return pl.pallas_call(
        query_kernel,
        in_specs=[SMEM, SMEM, VMEM],
        out_specs=VMEM,
        out_shape=jax.ShapeDtypeStruct((rows + EXTRA, E), BF16),
        compiler_params=limit(4),
        name="pack_queries",
    )(query_len, positive, queries)


def own_place():
    seat = lax.axis_index("seq")
    return lax.axis_index("dp"), lax.rem(seat, 2), seat // 2


def group_of(mine, blocks, block):
    side, step = divmod(block, blocks // 2)
    return lax.rem(mine + blocks - 2 * step, blocks) ^ side


def block_of(packed_refs, block):
    side, step = divmod(block, packed_refs[0].shape[0])
    return packed_refs[side].at[step]


def expo_of(dots):
    gain = LOG2E / TEMPER
    return jnp.exp2(dots * gain - gain).astype(BF16)


def dots_ahead(packed_refs, blocks, rows, khat):
    ahead = []
    for block in range(blocks):
        ahead.append(dot_t(block_of(packed_refs, block)[:rows, :], khat))
        if block > 0:
            yield block - 1, ahead.pop(0)
    yield blocks - 1, ahead.pop(0)


def terms_kernel(blocks, khat_ref, *refs):
    packed_refs, (keep_ref, send_ref, sums_ref) = refs[:-3], refs[-3:]
    rows = packed_refs[0].shape[1] - EXTRA
    first = own_place()[1] == 0
    khat = khat_ref[...]
    wide = jnp.concatenate([khat, jnp.ones_like(khat)], axis=1)
    eye = iota((E, E), 0) == iota((E, E), 1)
    sums = []
    for block, dots in dots_ahead(packed_refs, blocks, rows, khat):
        both = dot(expo_of(dots), wide)
        low, high = both[:E, :E], both[E:, :E]
        keep_ref[block] = jnp.where(first, low, high)
        send_ref[block] = jnp.where(first, high, low).astype(BF16)
        for part in range(rows // E):
            square = both[part * E : (part + 1) * E, E:]
            sums.append(jnp.sum(jnp.where(eye, square, 0.0), axis=0, keepdims=True))
    sums_ref[...] = jnp.concatenate(sums, axis=0)


def terms(packed, khat):
    blocks, rows = 2 * packed[0].shape[0], packed[0].shape[1] - EXTRA
    return pl.pallas_call(
        lambda *refs: terms_kernel(blocks, *refs),
        in_specs=[VMEM] * (1 + len(packed)),
        out_specs=[VMEM] * 3,
        out_shape=[
            jax.ShapeDtypeStruct((blocks, rows // 2, E), F32),
            jax.ShapeDtypeStruct((blocks, rows // 2, E), BF16),
            jax.ShapeDtypeStruct((blocks * rows // E, E), F32),
        ],
        compiler_params=limit(16),
        name="terms",
    )(khat, *packed)


def join_kernel(keep_ref, got_ref, sums_ref, others_ref, out_ref):
    blocks, half, _ = keep_ref.shape
    chips = out_ref.shape[0]
    piece = half // chips
    sums = sums_ref[...] + others_ref[...]
    upper = sums.astype(BF16)
    lower = (sums - upper.astype(F32)).astype(BF16)
    notes = jnp.concatenate([upper, lower], axis=0)
    for block in range(blocks):
        both = (keep_ref[block] + got_ref[block].astype(F32)).astype(BF16)
        for chip in range(chips):
            out_ref[chip, block * piece : (block + 1) * piece, :] = both[
                chip * piece : (chip + 1) * piece
            ]
    for chip in range(chips):
        out_ref[chip, blocks * piece :, :] = notes


def join(keep, got, sums, others, chips):
    blocks, half, _ = keep.shape
    return pl.pallas_call(
        join_kernel,
        in_specs=[VMEM] * 4,
        out_specs=VMEM,
        out_shape=jax.ShapeDtypeStruct(
            (chips, blocks * half // chips + 2 * sums.shape[0], E), BF16
        ),
        compiler_params=limit(8),
        name="join",
    )(keep, got, sums, others)


def scale_kernel(slots, got_ref, *refs):
    packed_refs, (part_ref, scale_ref, loss_ref) = refs[:-3], refs[-3:]
    blocks, shards, share, _ = part_ref.shape
    piece = 2 * share
    video, core, chip = own_place()
    rows = packed_refs[0].shape[1] - EXTRA
    per = rows // E
    got = jnp.sum(got_ref[...].astype(F32), axis=0)
    blend, notes = got[: blocks * piece], got[blocks * piece :]
    total = notes[: blocks * per] + notes[blocks * per :]
    notes = [block_of(packed_refs, b)[rows:, :].astype(F32) for b in range(blocks)]
    lens = jnp.concatenate([note[:per] for note in notes], axis=0)
    pos = jnp.concatenate([note[per : 2 * per] for note in notes], axis=0)
    mask = ((iota(total.shape, 1) % slots).astype(F32) < lens).astype(F32)
    smooth = (1.0 + TEMPER * jnp.log(total)) * mask
    same = (iota((E, E), 0) // slots == iota((E, E), 1) // slots).astype(F32)
    score = (
        lax.dot_general(
            smooth,
            same,
            (((1,), (0,)), ((), ())),
            preferred_element_type=F32,
            precision=lax.Precision.HIGHEST,
        )
        / lens
    )
    sign = jnp.where(pos == video.astype(F32), 1.0, -1.0)
    margin = sign * (SLOPE * score + OFFSET)
    loss = jnp.maximum(-margin, 0.0) + jnp.log1p(jnp.exp(-jnp.abs(margin)))
    coeff = -SLOPE * sign / (1.0 + jnp.exp(margin)) * mask / lens
    scale_ref[...] = (coeff / total).T
    scale = scale_ref[pl.ds(pl.multiple_of(chip * piece, piece), piece), :]
    first = core == 0
    for block in range(blocks):
        group = group_of(video, blocks, block)
        at = block * per
        column = jnp.where(first, scale[:, at : at + 1], scale[:, at + 1 : at + 2])
        part = (blend[block * piece : (block + 1) * piece] * column).astype(BF16)
        for shard in range(shards):
            part_ref[group, shard] = part[shard % 2 * share : (shard % 2 + 1) * share]
        loss_ref[group] = loss[at : at + per]


def scales(got, packed, slots, shards):
    blocks, rows = 2 * packed[0].shape[0], packed[0].shape[1] - EXTRA
    share = rows // shards // 2
    return pl.pallas_call(
        lambda *refs: scale_kernel(slots, *refs),
        in_specs=[VMEM] * (1 + len(packed)),
        out_specs=[VMEM] * 3,
        out_shape=[
            jax.ShapeDtypeStruct((blocks, shards, share, E), BF16),
            jax.ShapeDtypeStruct((E, blocks * rows // E), F32),
            jax.ShapeDtypeStruct((blocks, rows // E, E), F32),
        ],
        compiler_params=limit(8),
        name="scales",
    )(got, *packed)


def keys_kernel(gain, blocks, scale_ref, khat_ref, *refs):
    packed_refs, out_ref = refs[:-1], refs[-1]
    khat = khat_ref[...]
    rows = packed_refs[0].shape[1] - EXTRA
    per = rows // E
    total = jnp.zeros((E, khat.shape[0]), F32)
    for block, dots in dots_ahead(packed_refs, blocks, rows, khat):
        query = block_of(packed_refs, block)[:rows, :]
        parts = []
        for part in range(per):
            at = block * per + part
            scaled = query[part * E : (part + 1) * E].astype(F32) * scale_ref[:, at : at + 1]
            parts.append(scaled.T.astype(BF16))
        total = total + dot(jnp.concatenate(parts, axis=1), expo_of(dots))
    out_ref[...] = (total.T * gain).astype(BF16)


def keys(scale, khat, packed, gain):
    return pl.pallas_call(
        lambda *refs: keys_kernel(gain, 2 * packed[0].shape[0], *refs),
        in_specs=[VMEM] * (2 + len(packed)),
        out_specs=VMEM,
        out_shape=jax.ShapeDtypeStruct(khat.shape, BF16),
        compiler_params=limit(16),
        name="keys",
    )(scale, khat, *packed)


def total_kernel(gain, in_ref, out_ref):
    out_ref[...] = (jnp.sum(in_ref[...].astype(F32), axis=0) * gain).astype(BF16)


def totals(parts, gain):
    return pl.pallas_call(
        lambda *refs: total_kernel(gain, *refs),
        in_specs=[VMEM],
        out_specs=VMEM,
        out_shape=jax.ShapeDtypeStruct(parts.shape[1:], BF16),
        compiler_params=limit(4),
        name="totals",
    )(parts)


def weave_kernel(mine_ref, other_ref, out_ref):
    shards, share, _ = mine_ref.shape
    first = own_place()[1] == 0
    for shard in range(shards):
        at = ((shard % 2) * (shards // 2) + shard // 2) * 2 * share
        mine, other = mine_ref[shard], other_ref[shard]
        out_ref[at : at + share, :] = jnp.where(first, mine, other)
        out_ref[at + share : at + 2 * share, :] = jnp.where(first, other, mine)


def weave(mine, other):
    shards, share, _ = mine.shape
    return pl.pallas_call(
        weave_kernel,
        in_specs=[VMEM, VMEM],
        out_specs=VMEM,
        out_shape=jax.ShapeDtypeStruct((2 * shards * share, E), BF16),
        compiler_params=limit(4),
        name="weave",
    )(mine, other)


def body(
    video, space_qkv, space_out, time_qkv, time_out, proj_weight, queries, query_len, positive
):
    _, frames_dev, patches, _ = video.shape
    shards = lax.axis_size("seq")
    blocks = lax.axis_size("dp")
    patch_loc = patches // shards
    frames = frames_dev * shards
    query_dev, slots, _ = queries.shape
    rows = query_dev * slots
    partner = [(i, i ^ 1) for i in range(shards)]
    chips = [[2 * chip + own for chip in range(shards // 2)] for own in range(2)]

    spatial = space(video[0], space_qkv, space_out, shards)
    spatial, flat = lax.optimization_barrier((spatial, queries.reshape(rows, E)))
    items = lax.all_to_all(spatial, "seq", 0, 0, tiled=True)
    mine = pack_queries(flat, query_len, positive)
    lane = jnp.stack(
        [mine]
        + [
            lax.ppermute(mine, "dp", [(i, (i + by) % blocks) for i in range(blocks)])
            for by in range(2, blocks, 2)
        ]
    )
    items, lane = lax.optimization_barrier((items, lane))
    packed = [lane, lax.ppermute(lane, "dp", [(i, i ^ 1) for i in range(blocks)])]
    khat = time(items.reshape(-1, D), time_qkv, time_out, proj_weight, patch_loc)

    keep, send, sums = terms(packed, khat)
    got = lax.ppermute(send, "seq", partner)
    others = lax.ppermute(sums, "seq", partner)
    joined = join(keep, got, sums, others, shards // 2)
    joined = lax.all_to_all(joined, "seq", 0, 0, tiled=True, axis_index_groups=chips)
    parts, scale, loss = scales(joined, packed, slots, shards)
    parts = lax.all_to_all(
        parts.reshape((-1,) + parts.shape[2:]), ("dp", "seq"), 0, 0, tiled=True
    )
    video_grad = keys(scale, khat, packed, float(frames * P_SIZE))
    parts, video_grad = lax.optimization_barrier((parts, video_grad))
    summed = totals(parts.reshape((blocks, shards) + parts.shape[1:]), float(slots))
    query_grad = weave(summed, lax.ppermute(summed, "seq", partner))
    return (
        video_grad.reshape(1, frames, patch_loc, E),
        query_grad.reshape(query_dev, slots, E),
        loss[:, :, ::slots].reshape(-1, 1),
    )


def solution(mesh):
    placed = (
        P("dp", "seq", None, None),
        P(),
        P(),
        P(),
        P(),
        P(),
        P("dp", None, None),
        P("dp"),
        P("dp"),
    )
    return jax.shard_map(
        body,
        mesh=mesh,
        in_specs=placed,
        out_specs=(P("dp", None, "seq", None), P("dp", None, None), P(None, "dp")),
        check_vma=False,
    )
```

```python
import jax
import jax.numpy as jnp
from jax import lax
from jax.experimental import pallas as pl
from jax.experimental.pallas import tpu as pltpu
from jax.sharding import PartitionSpec as P

HEADS = 12
P_SIZE = 256
TEMPER = 0.05
SLOPE = 10.0
OFFSET = -5.0
SHARP = 10.0
LOG2E = 1.4426950408889634

D = 768
HEAD = D // HEADS
PAIR = 2 * HEAD
PAIRS = HEADS // 2
TILE = 256
SUB = 128
E = 128
F32 = jnp.float32
BF16 = jnp.bfloat16
VMEM = pl.BlockSpec(memory_space=pltpu.VMEM)
SMEM = pl.BlockSpec(memory_space=pltpu.SMEM)
HBM = pl.BlockSpec(memory_space=pltpu.HBM)


def limit(mib):
    return pltpu.CompilerParams(vmem_limit_bytes=mib * 2**20)


def dot(a, b):
    return lax.dot_general(a, b, (((1,), (0,)), ((), ())), preferred_element_type=F32)


def dot_t(a, b):
    return lax.dot_general(a, b, (((1,), (1,)), ((), ())), preferred_element_type=F32)


def iota(shape, dim):
    return lax.broadcasted_iota(jnp.int32, shape, dim)


def layer_norm(tokens):
    values = tokens.astype(F32)
    center = values - jnp.mean(values, axis=-1, keepdims=True)
    spread = jnp.mean(center * center, axis=-1, keepdims=True)
    return (center * lax.rsqrt(spread + 1e-05)).astype(BF16)


def unit_heads(values, gain):
    same = (iota((TILE, TILE), 0) // HEAD == iota((TILE, TILE), 1) // HEAD).astype(BF16)
    parts = []
    for at in range(0, values.shape[1], TILE):
        part = values[:, at : at + TILE]
        squares = dot((part * part).astype(BF16), same)
        parts.append((part * (lax.rsqrt(squares + 1e-06) * gain)).astype(BF16))
    return jnp.concatenate(parts, axis=1)


def pair_scores(query, key):
    extent = key.shape[0]
    low = iota((extent, PAIR), 1) < HEAD
    zero = jnp.zeros((extent, PAIR), BF16)
    keys = jnp.concatenate([jnp.where(low, key, zero), jnp.where(low, zero, key)], axis=0)
    return dot_t(query, keys)


def pair_mix(scores, value, keep):
    extent = value.shape[0]
    low = iota((extent, PAIR), 1) < HEAD
    zero = jnp.zeros((extent, PAIR), BF16)
    one = jnp.ones((extent, PAIR), BF16)
    values = jnp.concatenate(
        [
            jnp.concatenate([jnp.where(low, value, zero), jnp.where(low, one, zero)], axis=1),
            jnp.concatenate([jnp.where(low, zero, value), jnp.where(low, zero, one)], axis=1),
        ],
        axis=0,
    )
    weights = jnp.exp2(scores).astype(BF16)
    if keep is not None:
        weights = jnp.where(keep, weights, jnp.zeros_like(weights))
    return dot(weights, values)


def pair_done(mixed):
    return (mixed[:, :PAIR] / mixed[:, PAIR:]).astype(BF16)


class Flat:
    def __init__(self, ref):
        self.ref = ref

    def __getitem__(self, at):
        down, across = at
        extent = self.ref.shape[1]
        part = self.ref[down.start // extent : down.stop // extent, :, across]
        return part.reshape(down.stop - down.start, part.shape[-1])


def blend_all(units, q_s, k_s, v_s, keep, put):
    scores, mixes = {}, {}
    for i in range(len(units) + 3):
        if i < len(units):
            d, a = units[i]
            scores[i] = pair_scores(q_s[d, a], k_s[d, a])
        if 0 <= i - 2 < len(units):
            d, a = units[i - 2]
            mixes[i - 2] = pair_mix(scores.pop(i - 2), v_s[d, a], keep)
        if 0 <= i - 3:
            put(units[i - 3], pair_done(mixes.pop(i - 3)))


def fetch(pairs, sem):
    copies = [pltpu.make_async_copy(a, b, sem.at[i]) for i, (a, b) in enumerate(pairs)]
    for copy in copies:
        copy.start()
    return copies


def columns(ref, third):
    return ref.at[:, pl.ds(third * D, D)]


def in_hbm(*arrays):
    return [pltpu.with_memory_space_constraint(array, pltpu.HBM) for array in arrays]


def qkv_all(chunks, weight_s, copies, outs):
    queue = []

    def flush():
        part, out, gain, at = queue.pop(0)
        part = part.astype(BF16) if gain is None else unit_heads(part, gain)
        out[at] = part.reshape(out[at].shape)

    for third, (out, gain) in enumerate(zip(outs, (SHARP * LOG2E, 1.0, None))):
        copies[third].wait()
        for at, rows in chunks:
            part = dot(rows(third), weight_s[:, third * D : (third + 1) * D])
            queue.append((part, out, gain, at))
            if len(queue) > 1:
                flush()
    while queue:
        flush()


def space_kernel(
    video_ref, qkv_ref, out_w_ref, out_ref, x_s, qkv_s, w_s, n_s, q_s, k_s, v_s, y_s, sem, out_sem
):
    frames, patches, _ = x_s.shape
    video = fetch([(video_ref.at[f], x_s.at[f]) for f in range(frames)], sem)
    weights = fetch(
        [(columns(qkv_ref, i), columns(qkv_s, i)) for i in range(3)] + [(out_w_ref, w_s)],
        sem.at[pl.ds(frames, 4)],
    )
    for f in range(frames):
        video[f].wait()
        n_s[f * patches : (f + 1) * patches, :] = layer_norm(x_s[f])
    chunks = [
        (slice(at, at + 128), lambda third, at=at: n_s[at : at + 128, :])
        for at in range(0, frames * patches, 128)
    ]
    qkv_all(chunks, qkv_s, weights, (q_s, k_s, v_s))
    weights[3].wait()
    units = [
        (slice(f * patches, (f + 1) * patches), slice(pair * PAIR, (pair + 1) * PAIR))
        for f in range(frames)
        for pair in range(PAIRS)
    ]
    stores = []

    def put(unit, blended):
        n_s[unit] = blended
        if unit[1].stop < D:
            return
        f = unit[0].start // patches
        update = dot(n_s[unit[0], :], w_s[...])
        y_s[f] = (x_s[f].astype(F32) + update).astype(BF16).reshape(y_s.shape[1:])
        stores.append(pltpu.make_async_copy(y_s.at[f], out_ref.at[:, f], out_sem.at[f]))
        stores[-1].start()

    blend_all(units, q_s, k_s, v_s, None, put)
    for store in stores:
        store.wait()


def space(video, qkv_weight, out_weight, shards):
    frames, patches, _ = video.shape
    local = patches // shards
    return pl.pallas_call(
        space_kernel,
        in_specs=[HBM] * 3,
        out_specs=HBM,
        out_shape=pltpu.HBM((shards, frames, local, D), BF16),
        scratch_shapes=[
            pltpu.VMEM((frames, patches, D), BF16),
            pltpu.VMEM((D, 3 * D), BF16),
            pltpu.VMEM((D, D), BF16),
        ]
        + [pltpu.VMEM((frames * patches, D), BF16)] * 4
        + [
            pltpu.VMEM((frames, shards, local, D), BF16),
            pltpu.SemaphoreType.DMA((frames + 4,)),
            pltpu.SemaphoreType.DMA((frames,)),
        ],
        compiler_params=limit(40),
        name="space",
    )(*in_hbm(video, qkv_weight, out_weight))


def swap_rows(rows, side):
    extent = side * side
    row, col = iota((extent, extent), 0), iota((extent, extent), 1)
    swap = (col == (row % side) * side + row // side).astype(BF16)
    return dot(swap, rows).astype(BF16)


def time_kernel(
    x_ref, qkv_ref, out_w_ref, proj_ref, khat_ref,
    x_s, n_s, qkv_s, w_s, p_s, q_s, k_s, v_s, b_s, kh_s, sem,
):
    side, frames, _ = x_s.shape
    rows = x_ref.shape[0]
    weights = fetch(
        [(columns(qkv_ref, i), columns(qkv_s, i)) for i in range(3)]
        + [(out_w_ref, w_s), (proj_ref, p_s)],
        sem,
    )
    for tile in range(rows // TILE):
        tokens = swap_rows(x_ref[tile * TILE : (tile + 1) * TILE, :], side)
        at = slice(tile * side, (tile + 1) * side)
        x_s[:, at, :] = tokens.reshape(side, side, D)
        n_s[:, at, :] = layer_norm(tokens).reshape(side, side, D)
    chunks = [
        (
            (slice(at // frames, (at + 128) // frames), slice(None), slice(None)),
            lambda third, at=at: n_s[at // frames : (at + 128) // frames].reshape(128, D),
        )
        for at in range(0, rows, 128)
    ]
    qkv_all(chunks, qkv_s, weights, (q_s, k_s, v_s))
    keep = iota((SUB, 2 * SUB), 0) // frames == (iota((SUB, 2 * SUB), 1) % SUB) // frames
    weights[3].wait()
    weights[4].wait()

    def put(unit, blended):
        b_s[unit] = blended

    units = [
        (slice(at, at + SUB), slice(pair * PAIR, (pair + 1) * PAIR))
        for at in range(0, rows, SUB)
        for pair in range(PAIRS)
    ]
    blend_all(units, Flat(q_s), Flat(k_s), Flat(v_s), keep, put)
    ahead = []

    def mixed(groups, update):
        tokens = x_s[groups].reshape(update.shape)
        normed = layer_norm((tokens.astype(F32) + update).astype(BF16))
        projected = dot(normed, p_s[...])
        norm = jnp.sum(projected * projected, axis=-1, keepdims=True)
        unit = (projected * lax.rsqrt(norm + 1e-06)).astype(BF16)
        kh_s[groups] = unit.reshape(kh_s[groups].shape)

    for at in range(0, rows, 256):
        groups = slice(at // frames, (at + 256) // frames)
        ahead.append((groups, dot(b_s[at : at + 256, :], w_s[...])))
        if len(ahead) > 1:
            mixed(*ahead.pop(0))
    mixed(*ahead.pop(0))
    for tile in range(rows // TILE):
        part = kh_s[:, tile * side : (tile + 1) * side, :].reshape(TILE, E)
        khat_ref[tile * TILE : (tile + 1) * TILE, :] = swap_rows(part, side)


def time(x, qkv_weight, out_weight, proj_weight, patches):
    rows = x.shape[0]
    frames = rows // patches
    return pl.pallas_call(
        time_kernel,
        in_specs=[VMEM] + [HBM] * 3,
        out_specs=VMEM,
        out_shape=jax.ShapeDtypeStruct((rows, E), BF16),
        scratch_shapes=[
            pltpu.VMEM((patches, frames, D), BF16),
            pltpu.VMEM((patches, frames, D), BF16),
            pltpu.VMEM((D, 3 * D), BF16),
            pltpu.VMEM((D, D), BF16),
            pltpu.VMEM((D, E), BF16),
        ]
        + [pltpu.VMEM((patches, frames, D), BF16)] * 3
        + [pltpu.VMEM((rows, D), BF16)]
        + [pltpu.VMEM((patches, frames, E), BF16), pltpu.SemaphoreType.DMA((5,))],
        compiler_params=limit(40),
        name="time",
    )(x, *in_hbm(qkv_weight, out_weight, proj_weight))


EXTRA = 16


def query_kernel(len_ref, pos_ref, q_ref, out_ref):
    rows = q_ref.shape[0]
    values = q_ref[...].astype(F32)
    norm = jnp.sum(values * values, axis=-1, keepdims=True)
    out_ref[:rows, :] = (values / jnp.sqrt(norm + 1e-06)).astype(BF16)
    slots = rows // len_ref.shape[0]
    row, lane = iota((EXTRA, E), 0), iota((EXTRA, E), 1)
    owner = ((row % 2) * E + lane) // slots
    extra = jnp.zeros((EXTRA, E), F32)
    for query in range(len_ref.shape[0]):
        picked = jnp.where(row < 2, len_ref[query], pos_ref[query]).astype(F32)
        extra = jnp.where((owner == query) & (row < 4), picked, extra)
    out_ref[rows:, :] = extra.astype(BF16)


def pack_queries(queries, query_len, positive):
    rows = queries.shape[0]
    return pl.pallas_call(
        query_kernel,
        in_specs=[SMEM, SMEM, VMEM],
        out_specs=VMEM,
        out_shape=jax.ShapeDtypeStruct((rows + EXTRA, E), BF16),
        compiler_params=limit(4),
        name="pack_queries",
    )(query_len, positive, queries)


def own_place():
    seat = lax.axis_index("seq")
    return lax.axis_index("dp"), lax.rem(seat, 2), seat // 2


def group_of(mine, blocks, block):
    side, step = divmod(block, blocks // 2)
    return lax.rem(mine + blocks - 2 * step, blocks) ^ side


def block_of(packed_refs, block):
    side, step = divmod(block, packed_refs[0].shape[0])
    return packed_refs[side].at[step]


def expo_of(dots):
    gain = LOG2E / TEMPER
    return jnp.exp2(dots * gain - gain).astype(BF16)


def dots_ahead(packed_refs, blocks, rows, khat):
    ahead = []
    for block in range(blocks):
        ahead.append(dot_t(block_of(packed_refs, block)[:rows, :], khat))
        if block > 0:
            yield block - 1, ahead.pop(0)
    yield blocks - 1, ahead.pop(0)


def terms_kernel(blocks, khat_ref, *refs):
    packed_refs, (keep_ref, send_ref, sums_ref) = refs[:-3], refs[-3:]
    rows = packed_refs[0].shape[1] - EXTRA
    first = own_place()[1] == 0
    khat = khat_ref[...]
    wide = jnp.concatenate([khat, jnp.ones_like(khat)], axis=1)
    eye = iota((E, E), 0) == iota((E, E), 1)
    sums = []
    for block, dots in dots_ahead(packed_refs, blocks, rows, khat):
        both = dot(expo_of(dots), wide)
        low, high = both[:E, :E], both[E:, :E]
        keep_ref[block] = jnp.where(first, low, high)
        send_ref[block] = jnp.where(first, high, low).astype(BF16)
        for part in range(rows // E):
            square = both[part * E : (part + 1) * E, E:]
            sums.append(jnp.sum(jnp.where(eye, square, 0.0), axis=0, keepdims=True))
    sums_ref[...] = jnp.concatenate(sums, axis=0)


def terms(packed, khat):
    blocks, rows = 2 * packed[0].shape[0], packed[0].shape[1] - EXTRA
    return pl.pallas_call(
        lambda *refs: terms_kernel(blocks, *refs),
        in_specs=[VMEM] * (1 + len(packed)),
        out_specs=[VMEM] * 3,
        out_shape=[
            jax.ShapeDtypeStruct((blocks, rows // 2, E), F32),
            jax.ShapeDtypeStruct((blocks, rows // 2, E), BF16),
            jax.ShapeDtypeStruct((blocks * rows // E, E), F32),
        ],
        compiler_params=limit(16),
        name="terms",
    )(khat, *packed)


def join_kernel(keep_ref, got_ref, sums_ref, others_ref, out_ref):
    blocks, half, _ = keep_ref.shape
    chips = out_ref.shape[0]
    piece = half // chips
    sums = sums_ref[...] + others_ref[...]
    upper = sums.astype(BF16)
    lower = (sums - upper.astype(F32)).astype(BF16)
    notes = jnp.concatenate([upper, lower], axis=0)
    for block in range(blocks):
        both = (keep_ref[block] + got_ref[block].astype(F32)).astype(BF16)
        for chip in range(chips):
            out_ref[chip, block * piece : (block + 1) * piece, :] = both[
                chip * piece : (chip + 1) * piece
            ]
    for chip in range(chips):
        out_ref[chip, blocks * piece :, :] = notes


def join(keep, got, sums, others, chips):
    blocks, half, _ = keep.shape
    return pl.pallas_call(
        join_kernel,
        in_specs=[VMEM] * 4,
        out_specs=VMEM,
        out_shape=jax.ShapeDtypeStruct(
            (chips, blocks * half // chips + 2 * sums.shape[0], E), BF16
        ),
        compiler_params=limit(8),
        name="join",
    )(keep, got, sums, others)


def scale_kernel(slots, got_ref, *refs):
    packed_refs, (part_ref, scale_ref, loss_ref) = refs[:-3], refs[-3:]
    blocks, shards, share, _ = part_ref.shape
    piece = 2 * share
    video, core, chip = own_place()
    rows = packed_refs[0].shape[1] - EXTRA
    per = rows // E
    got = jnp.sum(got_ref[...].astype(F32), axis=0)
    blend, notes = got[: blocks * piece], got[blocks * piece :]
    total = notes[: blocks * per] + notes[blocks * per :]
    notes = [block_of(packed_refs, b)[rows:, :].astype(F32) for b in range(blocks)]
    lens = jnp.concatenate([note[:per] for note in notes], axis=0)
    pos = jnp.concatenate([note[per : 2 * per] for note in notes], axis=0)
    mask = ((iota(total.shape, 1) % slots).astype(F32) < lens).astype(F32)
    smooth = (1.0 + TEMPER * jnp.log(total)) * mask
    same = (iota((E, E), 0) // slots == iota((E, E), 1) // slots).astype(F32)
    score = (
        lax.dot_general(
            smooth,
            same,
            (((1,), (0,)), ((), ())),
            preferred_element_type=F32,
            precision=lax.Precision.HIGHEST,
        )
        / lens
    )
    sign = jnp.where(pos == video.astype(F32), 1.0, -1.0)
    margin = sign * (SLOPE * score + OFFSET)
    loss = jnp.maximum(-margin, 0.0) + jnp.log1p(jnp.exp(-jnp.abs(margin)))
    coeff = -SLOPE * sign / (1.0 + jnp.exp(margin)) * mask / lens
    scale_ref[...] = (coeff / total).T
    scale = scale_ref[pl.ds(pl.multiple_of(chip * piece, piece), piece), :]
    first = core == 0
    for block in range(blocks):
        group = group_of(video, blocks, block)
        at = block * per
        column = jnp.where(first, scale[:, at : at + 1], scale[:, at + 1 : at + 2])
        part = (blend[block * piece : (block + 1) * piece] * column).astype(BF16)
        for shard in range(shards):
            part_ref[group, shard] = part[shard % 2 * share : (shard % 2 + 1) * share]
        loss_ref[group] = loss[at : at + per]


def scales(got, packed, slots, shards):
    blocks, rows = 2 * packed[0].shape[0], packed[0].shape[1] - EXTRA
    share = rows // shards // 2
    return pl.pallas_call(
        lambda *refs: scale_kernel(slots, *refs),
        in_specs=[VMEM] * (1 + len(packed)),
        out_specs=[VMEM] * 3,
        out_shape=[
            jax.ShapeDtypeStruct((blocks, shards, share, E), BF16),
            jax.ShapeDtypeStruct((E, blocks * rows // E), F32),
            jax.ShapeDtypeStruct((blocks, rows // E, E), F32),
        ],
        compiler_params=limit(8),
        name="scales",
    )(got, *packed)


def keys_kernel(gain, blocks, scale_ref, khat_ref, *refs):
    packed_refs, out_ref = refs[:-1], refs[-1]
    khat = khat_ref[...]
    rows = packed_refs[0].shape[1] - EXTRA
    per = rows // E
    total = jnp.zeros((E, khat.shape[0]), F32)
    for block, dots in dots_ahead(packed_refs, blocks, rows, khat):
        query = block_of(packed_refs, block)[:rows, :]
        parts = []
        for part in range(per):
            at = block * per + part
            scaled = query[part * E : (part + 1) * E].astype(F32) * scale_ref[:, at : at + 1]
            parts.append(scaled.T.astype(BF16))
        total = total + dot(jnp.concatenate(parts, axis=1), expo_of(dots))
    out_ref[...] = (total.T * gain).astype(BF16)


def keys(scale, khat, packed, gain):
    return pl.pallas_call(
        lambda *refs: keys_kernel(gain, 2 * packed[0].shape[0], *refs),
        in_specs=[VMEM] * (2 + len(packed)),
        out_specs=VMEM,
        out_shape=jax.ShapeDtypeStruct(khat.shape, BF16),
        compiler_params=limit(16),
        name="keys",
    )(scale, khat, *packed)


def total_kernel(gain, in_ref, out_ref):
    out_ref[...] = (jnp.sum(in_ref[...].astype(F32), axis=0) * gain).astype(BF16)


def totals(parts, gain):
    return pl.pallas_call(
        lambda *refs: total_kernel(gain, *refs),
        in_specs=[VMEM],
        out_specs=VMEM,
        out_shape=jax.ShapeDtypeStruct(parts.shape[1:], BF16),
        compiler_params=limit(4),
        name="totals",
    )(parts)


def weave_kernel(mine_ref, other_ref, out_ref):
    shards, share, _ = mine_ref.shape
    first = own_place()[1] == 0
    for shard in range(shards):
        at = ((shard % 2) * (shards // 2) + shard // 2) * 2 * share
        mine, other = mine_ref[shard], other_ref[shard]
        out_ref[at : at + share, :] = jnp.where(first, mine, other)
        out_ref[at + share : at + 2 * share, :] = jnp.where(first, other, mine)


def weave(mine, other):
    shards, share, _ = mine.shape
    return pl.pallas_call(
        weave_kernel,
        in_specs=[VMEM, VMEM],
        out_specs=VMEM,
        out_shape=jax.ShapeDtypeStruct((2 * shards * share, E), BF16),
        compiler_params=limit(4),
        name="weave",
    )(mine, other)


def body(
    video, space_qkv, space_out, time_qkv, time_out, proj_weight, queries, query_len, positive
):
    _, frames_dev, patches, _ = video.shape
    shards = lax.axis_size("seq")
    blocks = lax.axis_size("dp")
    patch_loc = patches // shards
    frames = frames_dev * shards
    query_dev, slots, _ = queries.shape
    rows = query_dev * slots
    partner = [(i, i ^ 1) for i in range(shards)]
    chips = [[2 * chip + own for chip in range(shards // 2)] for own in range(2)]

    spatial = space(video[0], space_qkv, space_out, shards)
    spatial, flat = lax.optimization_barrier((spatial, queries.reshape(rows, E)))
    items = lax.all_to_all(spatial, "seq", 0, 0, tiled=True)
    mine = pack_queries(flat, query_len, positive)
    lane = jnp.stack(
        [mine]
        + [
            lax.ppermute(mine, "dp", [(i, (i + by) % blocks) for i in range(blocks)])
            for by in range(2, blocks, 2)
        ]
    )
    items, lane = lax.optimization_barrier((items, lane))
    packed = [lane, lax.ppermute(lane, "dp", [(i, i ^ 1) for i in range(blocks)])]
    khat = time(items.reshape(-1, D), time_qkv, time_out, proj_weight, patch_loc)

    keep, send, sums = terms(packed, khat)
    got = lax.ppermute(send, "seq", partner)
    others = lax.ppermute(sums, "seq", partner)
    joined = join(keep, got, sums, others, shards // 2)
    joined = lax.all_to_all(joined, "seq", 0, 0, tiled=True, axis_index_groups=chips)
    parts, scale, loss = scales(joined, packed, slots, shards)
    parts = lax.all_to_all(
        parts.reshape((-1,) + parts.shape[2:]), ("dp", "seq"), 0, 0, tiled=True
    )
    video_grad = keys(scale, khat, packed, float(frames * P_SIZE))
    parts, video_grad = lax.optimization_barrier((parts, video_grad))
    summed = totals(parts.reshape((blocks, shards) + parts.shape[1:]), float(slots))
    query_grad = weave(summed, lax.ppermute(summed, "seq", partner))
    return (
        video_grad.reshape(1, frames, patch_loc, E),
        query_grad.reshape(query_dev, slots, E),
        loss[:, :, ::slots].reshape(-1, 1),
    )


def solution(mesh):
    placed = (
        P("dp", "seq", None, None),
        P(),
        P(),
        P(),
        P(),
        P(),
        P("dp", None, None),
        P("dp"),
        P("dp"),
    )
    return jax.shard_map(
        body,
        mesh=mesh,
        in_specs=placed,
        out_specs=(P("dp", None, "seq", None), P("dp", None, None), P(None, "dp")),
        check_vma=False,
    )
```

```python
import jax
import jax.numpy as jnp
from jax import lax
from jax.experimental import pallas as pl
from jax.experimental.pallas import tpu as pltpu
from jax.sharding import PartitionSpec as P

HEADS = 12
P_SIZE = 256
TEMPER = 0.05
SLOPE = 10.0
OFFSET = -5.0
SHARP = 10.0
LOG2E = 1.4426950408889634

D = 768
HEAD = D // HEADS
PAIR = 2 * HEAD
PAIRS = HEADS // 2
TILE = 256
SUB = 128
E = 128
F32 = jnp.float32
BF16 = jnp.bfloat16
VMEM = pl.BlockSpec(memory_space=pltpu.VMEM)
SMEM = pl.BlockSpec(memory_space=pltpu.SMEM)
HBM = pl.BlockSpec(memory_space=pltpu.HBM)


def limit(mib):
    return pltpu.CompilerParams(vmem_limit_bytes=mib * 2**20)


def dot(a, b):
    return lax.dot_general(a, b, (((1,), (0,)), ((), ())), preferred_element_type=F32)


def dot_t(a, b):
    return lax.dot_general(a, b, (((1,), (1,)), ((), ())), preferred_element_type=F32)


def iota(shape, dim):
    return lax.broadcasted_iota(jnp.int32, shape, dim)


def layer_norm(tokens):
    values = tokens.astype(F32)
    center = values - jnp.mean(values, axis=-1, keepdims=True)
    spread = jnp.mean(center * center, axis=-1, keepdims=True)
    return (center * lax.rsqrt(spread + 1e-05)).astype(BF16)


def unit_heads(values, gain):
    same = (iota((TILE, TILE), 0) // HEAD == iota((TILE, TILE), 1) // HEAD).astype(BF16)
    parts = []
    for at in range(0, values.shape[1], TILE):
        part = values[:, at : at + TILE]
        squares = dot((part * part).astype(BF16), same)
        parts.append((part * (lax.rsqrt(squares + 1e-06) * gain)).astype(BF16))
    return jnp.concatenate(parts, axis=1)


def pair_scores(query, key):
    extent = key.shape[0]
    low = iota((extent, PAIR), 1) < HEAD
    zero = jnp.zeros((extent, PAIR), BF16)
    keys = jnp.concatenate([jnp.where(low, key, zero), jnp.where(low, zero, key)], axis=0)
    return dot_t(query, keys)


def pair_mix(scores, value, keep):
    extent = value.shape[0]
    low = iota((extent, PAIR), 1) < HEAD
    zero = jnp.zeros((extent, PAIR), BF16)
    one = jnp.ones((extent, PAIR), BF16)
    values = jnp.concatenate(
        [
            jnp.concatenate([jnp.where(low, value, zero), jnp.where(low, one, zero)], axis=1),
            jnp.concatenate([jnp.where(low, zero, value), jnp.where(low, zero, one)], axis=1),
        ],
        axis=0,
    )
    weights = jnp.exp2(scores).astype(BF16)
    if keep is not None:
        weights = jnp.where(keep, weights, jnp.zeros_like(weights))
    return dot(weights, values)


def pair_done(mixed):
    return (mixed[:, :PAIR] / mixed[:, PAIR:]).astype(BF16)


class Flat:
    def __init__(self, ref):
        self.ref = ref

    def __getitem__(self, at):
        down, across = at
        extent = self.ref.shape[1]
        part = self.ref[down.start // extent : down.stop // extent, :, across]
        return part.reshape(down.stop - down.start, part.shape[-1])


def blend_all(units, q_s, k_s, v_s, keep, put):
    scores, mixes = {}, {}
    for i in range(len(units) + 2):
        if i < len(units):
            d, a = units[i]
            scores[i] = pair_scores(q_s[d, a], k_s[d, a])
        if 0 <= i - 1 < len(units):
            d, a = units[i - 1]
            mixes[i - 1] = pair_mix(scores.pop(i - 1), v_s[d, a], keep)
        if 0 <= i - 2:
            put(units[i - 2], pair_done(mixes.pop(i - 2)))


def fetch(pairs, sem):
    copies = [pltpu.make_async_copy(a, b, sem.at[i]) for i, (a, b) in enumerate(pairs)]
    for copy in copies:
        copy.start()
    return copies


def columns(ref, third):
    return ref.at[:, pl.ds(third * D, D)]


def in_hbm(*arrays):
    return [pltpu.with_memory_space_constraint(array, pltpu.HBM) for array in arrays]


def qkv_all(chunks, weight_s, copies, outs):
    queue = []

    def flush():
        part, out, gain, at = queue.pop(0)
        part = part.astype(BF16) if gain is None else unit_heads(part, gain)
        out[at] = part.reshape(out[at].shape)

    for third, (out, gain) in enumerate(zip(outs, (SHARP * LOG2E, 1.0, None))):
        copies[third].wait()
        for at, rows in chunks:
            part = dot(rows(third), weight_s[:, third * D : (third + 1) * D])
            queue.append((part, out, gain, at))
            if len(queue) > 1:
                flush()
    while queue:
        flush()


def space_kernel(
    video_ref, qkv_ref, out_w_ref, out_ref, x_s, qkv_s, w_s, n_s, q_s, k_s, v_s, y_s, sem, out_sem
):
    frames, patches, _ = x_s.shape
    video = fetch([(video_ref.at[f], x_s.at[f]) for f in range(frames)], sem)
    weights = fetch(
        [(columns(qkv_ref, i), columns(qkv_s, i)) for i in range(3)] + [(out_w_ref, w_s)],
        sem.at[pl.ds(frames, 4)],
    )
    for f in range(frames):
        video[f].wait()
        n_s[f * patches : (f + 1) * patches, :] = layer_norm(x_s[f])
    chunks = [
        (slice(at, at + 128), lambda third, at=at: n_s[at : at + 128, :])
        for at in range(0, frames * patches, 128)
    ]
    qkv_all(chunks, qkv_s, weights, (q_s, k_s, v_s))
    weights[3].wait()
    units = [
        (slice(f * patches, (f + 1) * patches), slice(pair * PAIR, (pair + 1) * PAIR))
        for f in range(frames)
        for pair in range(PAIRS)
    ]
    stores = []

    def put(unit, blended):
        n_s[unit] = blended
        if unit[1].stop < D:
            return
        f = unit[0].start // patches
        update = dot(n_s[unit[0], :], w_s[...])
        y_s[f] = (x_s[f].astype(F32) + update).astype(BF16).reshape(y_s.shape[1:])
        stores.append(pltpu.make_async_copy(y_s.at[f], out_ref.at[:, f], out_sem.at[f]))
        stores[-1].start()

    blend_all(units, q_s, k_s, v_s, None, put)
    for store in stores:
        store.wait()


def space(video, qkv_weight, out_weight, shards):
    frames, patches, _ = video.shape
    local = patches // shards
    return pl.pallas_call(
        space_kernel,
        in_specs=[HBM] * 3,
        out_specs=HBM,
        out_shape=pltpu.HBM((shards, frames, local, D), BF16),
        scratch_shapes=[
            pltpu.VMEM((frames, patches, D), BF16),
            pltpu.VMEM((D, 3 * D), BF16),
            pltpu.VMEM((D, D), BF16),
        ]
        + [pltpu.VMEM((frames * patches, D), BF16)] * 4
        + [
            pltpu.VMEM((frames, shards, local, D), BF16),
            pltpu.SemaphoreType.DMA((frames + 4,)),
            pltpu.SemaphoreType.DMA((frames,)),
        ],
        compiler_params=limit(40),
        name="space",
    )(*in_hbm(video, qkv_weight, out_weight))


def swap_rows(rows, side):
    extent = side * side
    row, col = iota((extent, extent), 0), iota((extent, extent), 1)
    swap = (col == (row % side) * side + row // side).astype(BF16)
    return dot(swap, rows).astype(BF16)


def time_kernel(
    x_ref, qkv_ref, out_w_ref, proj_ref, khat_ref,
    x_s, n_s, qkv_s, w_s, p_s, q_s, k_s, v_s, b_s, kh_s, sem,
):
    side, frames, _ = x_s.shape
    rows = x_ref.shape[0]
    weights = fetch(
        [(columns(qkv_ref, i), columns(qkv_s, i)) for i in range(3)]
        + [(out_w_ref, w_s), (proj_ref, p_s)],
        sem,
    )
    for tile in range(rows // TILE):
        tokens = swap_rows(x_ref[tile * TILE : (tile + 1) * TILE, :], side)
        at = slice(tile * side, (tile + 1) * side)
        x_s[:, at, :] = tokens.reshape(side, side, D)
        n_s[:, at, :] = layer_norm(tokens).reshape(side, side, D)
    chunks = [
        (
            (slice(at // frames, (at + 128) // frames), slice(None), slice(None)),
            lambda third, at=at: n_s[at // frames : (at + 128) // frames].reshape(128, D),
        )
        for at in range(0, rows, 128)
    ]
    qkv_all(chunks, qkv_s, weights, (q_s, k_s, v_s))
    keep = iota((SUB, 2 * SUB), 0) // frames == (iota((SUB, 2 * SUB), 1) % SUB) // frames
    weights[3].wait()
    weights[4].wait()

    def put(unit, blended):
        b_s[unit] = blended

    units = [
        (slice(at, at + SUB), slice(pair * PAIR, (pair + 1) * PAIR))
        for at in range(0, rows, SUB)
        for pair in range(PAIRS)
    ]
    blend_all(units, Flat(q_s), Flat(k_s), Flat(v_s), keep, put)
    ahead = []

    def mixed(groups, update):
        tokens = x_s[groups].reshape(update.shape)
        normed = layer_norm((tokens.astype(F32) + update).astype(BF16))
        projected = dot(normed, p_s[...])
        norm = jnp.sum(projected * projected, axis=-1, keepdims=True)
        unit = (projected * lax.rsqrt(norm + 1e-06)).astype(BF16)
        kh_s[groups] = unit.reshape(kh_s[groups].shape)

    for at in range(0, rows, 256):
        groups = slice(at // frames, (at + 256) // frames)
        ahead.append((groups, dot(b_s[at : at + 256, :], w_s[...])))
        if len(ahead) > 1:
            mixed(*ahead.pop(0))
    mixed(*ahead.pop(0))
    for tile in range(rows // TILE):
        part = kh_s[:, tile * side : (tile + 1) * side, :].reshape(TILE, E)
        khat_ref[tile * TILE : (tile + 1) * TILE, :] = swap_rows(part, side)


def time(x, qkv_weight, out_weight, proj_weight, patches):
    rows = x.shape[0]
    frames = rows // patches
    return pl.pallas_call(
        time_kernel,
        in_specs=[VMEM] + [HBM] * 3,
        out_specs=VMEM,
        out_shape=jax.ShapeDtypeStruct((rows, E), BF16),
        scratch_shapes=[
            pltpu.VMEM((patches, frames, D), BF16),
            pltpu.VMEM((patches, frames, D), BF16),
            pltpu.VMEM((D, 3 * D), BF16),
            pltpu.VMEM((D, D), BF16),
            pltpu.VMEM((D, E), BF16),
        ]
        + [pltpu.VMEM((patches, frames, D), BF16)] * 3
        + [pltpu.VMEM((rows, D), BF16)]
        + [pltpu.VMEM((patches, frames, E), BF16), pltpu.SemaphoreType.DMA((5,))],
        compiler_params=limit(40),
        name="time",
    )(x, *in_hbm(qkv_weight, out_weight, proj_weight))


EXTRA = 16


def query_kernel(len_ref, pos_ref, q_ref, out_ref):
    rows = q_ref.shape[0]
    values = q_ref[...].astype(F32)
    norm = jnp.sum(values * values, axis=-1, keepdims=True)
    out_ref[:rows, :] = (values / jnp.sqrt(norm + 1e-06)).astype(BF16)
    slots = rows // len_ref.shape[0]
    row, lane = iota((EXTRA, E), 0), iota((EXTRA, E), 1)
    owner = ((row % 2) * E + lane) // slots
    extra = jnp.zeros((EXTRA, E), F32)
    for query in range(len_ref.shape[0]):
        picked = jnp.where(row < 2, len_ref[query], pos_ref[query]).astype(F32)
        extra = jnp.where((owner == query) & (row < 4), picked, extra)
    out_ref[rows:, :] = extra.astype(BF16)


def pack_queries(queries, query_len, positive):
    rows = queries.shape[0]
    return pl.pallas_call(
        query_kernel,
        in_specs=[SMEM, SMEM, VMEM],
        out_specs=VMEM,
        out_shape=jax.ShapeDtypeStruct((rows + EXTRA, E), BF16),
        compiler_params=limit(4),
        name="pack_queries",
    )(query_len, positive, queries)


def own_place():
    seat = lax.axis_index("seq")
    return lax.axis_index("dp"), lax.rem(seat, 2), seat // 2


def group_of(mine, blocks, block):
    side, step = divmod(block, blocks // 2)
    return lax.rem(mine + blocks - 2 * step, blocks) ^ side


def block_of(packed_refs, block):
    side, step = divmod(block, packed_refs[0].shape[0])
    return packed_refs[side].at[step]


def expo_of(dots):
    gain = LOG2E / TEMPER
    return jnp.exp2(dots * gain - gain).astype(BF16)


def dots_ahead(packed_refs, blocks, rows, khat):
    ahead = []
    for block in range(blocks):
        ahead.append(dot_t(block_of(packed_refs, block)[:rows, :], khat))
        if block > 0:
            yield block - 1, ahead.pop(0)
    yield blocks - 1, ahead.pop(0)


def terms_kernel(blocks, khat_ref, *refs):
    packed_refs, (keep_ref, send_ref, sums_ref) = refs[:-3], refs[-3:]
    rows = packed_refs[0].shape[1] - EXTRA
    first = own_place()[1] == 0
    khat = khat_ref[...]
    wide = jnp.concatenate([khat, jnp.ones_like(khat)], axis=1)
    eye = iota((E, E), 0) == iota((E, E), 1)
    sums = []
    for block, dots in dots_ahead(packed_refs, blocks, rows, khat):
        both = dot(expo_of(dots), wide)
        low, high = both[:E, :E], both[E:, :E]
        keep_ref[block] = jnp.where(first, low, high)
        send_ref[block] = jnp.where(first, high, low).astype(BF16)
        for part in range(rows // E):
            square = both[part * E : (part + 1) * E, E:]
            sums.append(jnp.sum(jnp.where(eye, square, 0.0), axis=0, keepdims=True))
    sums = jnp.concatenate(sums, axis=0)
    sums_ref[...] = sums
    upper = sums.astype(BF16)
    send_ref[blocks, : sums.shape[0], :] = upper
    send_ref[blocks, sums.shape[0] : 2 * sums.shape[0], :] = (sums - upper.astype(F32)).astype(BF16)
    send_ref[blocks, 2 * sums.shape[0] :, :] = jnp.zeros((E - 2 * sums.shape[0], E), BF16)


def terms(packed, khat):
    blocks, rows = 2 * packed[0].shape[0], packed[0].shape[1] - EXTRA
    return pl.pallas_call(
        lambda *refs: terms_kernel(blocks, *refs),
        in_specs=[VMEM] * (1 + len(packed)),
        out_specs=[VMEM] * 3,
        out_shape=[
            jax.ShapeDtypeStruct((blocks, rows // 2, E), F32),
            jax.ShapeDtypeStruct((blocks + 1, rows // 2, E), BF16),
            jax.ShapeDtypeStruct((blocks * rows // E, E), F32),
        ],
        compiler_params=limit(16),
        name="terms",
    )(khat, *packed)


def join_kernel(keep_ref, got_ref, sums_ref, out_ref):
    blocks, half, _ = keep_ref.shape
    chips = out_ref.shape[0]
    piece = half // chips
    count = sums_ref.shape[0]
    others = got_ref[blocks, : 2 * count, :].astype(F32)
    sums = sums_ref[...] + others[:count] + others[count:]
    upper = sums.astype(BF16)
    lower = (sums - upper.astype(F32)).astype(BF16)
    notes = jnp.concatenate([upper, lower], axis=0)
    for block in range(blocks):
        both = (keep_ref[block] + got_ref[block].astype(F32)).astype(BF16)
        for chip in range(chips):
            out_ref[chip, block * piece : (block + 1) * piece, :] = both[
                chip * piece : (chip + 1) * piece
            ]
    for chip in range(chips):
        out_ref[chip, blocks * piece :, :] = notes


def join(keep, got, sums, chips):
    blocks, half, _ = keep.shape
    return pl.pallas_call(
        join_kernel,
        in_specs=[VMEM] * 3,
        out_specs=VMEM,
        out_shape=jax.ShapeDtypeStruct(
            (chips, blocks * half // chips + 2 * sums.shape[0], E), BF16
        ),
        compiler_params=limit(8),
        name="join",
    )(keep, got, sums)


def scale_kernel(slots, got_ref, *refs):
    packed_refs, (part_ref, scale_ref, loss_ref) = refs[:-3], refs[-3:]
    blocks, shards, share, _ = part_ref.shape
    piece = 2 * share
    video, core, chip = own_place()
    rows = packed_refs[0].shape[1] - EXTRA
    per = rows // E
    got = jnp.sum(got_ref[...].astype(F32), axis=0)
    blend, notes = got[: blocks * piece], got[blocks * piece :]
    total = notes[: blocks * per] + notes[blocks * per :]
    notes = [block_of(packed_refs, b)[rows:, :].astype(F32) for b in range(blocks)]
    lens = jnp.concatenate([note[:per] for note in notes], axis=0)
    pos = jnp.concatenate([note[per : 2 * per] for note in notes], axis=0)
    mask = ((iota(total.shape, 1) % slots).astype(F32) < lens).astype(F32)
    smooth = (1.0 + TEMPER * jnp.log(total)) * mask
    same = (iota((E, E), 0) // slots == iota((E, E), 1) // slots).astype(F32)
    score = (
        lax.dot_general(
            smooth,
            same,
            (((1,), (0,)), ((), ())),
            preferred_element_type=F32,
            precision=lax.Precision.HIGHEST,
        )
        / lens
    )
    sign = jnp.where(pos == video.astype(F32), 1.0, -1.0)
    margin = sign * (SLOPE * score + OFFSET)
    loss = jnp.maximum(-margin, 0.0) + jnp.log1p(jnp.exp(-jnp.abs(margin)))
    coeff = -SLOPE * sign / (1.0 + jnp.exp(margin)) * mask / lens
    scale_ref[...] = (coeff / total).T
    scale = scale_ref[pl.ds(pl.multiple_of(chip * piece, piece), piece), :]
    first = core == 0
    for block in range(blocks):
        group = group_of(video, blocks, block)
        at = block * per
        column = jnp.where(first, scale[:, at : at + 1], scale[:, at + 1 : at + 2])
        part = (blend[block * piece : (block + 1) * piece] * column).astype(BF16)
        for shard in range(shards):
            part_ref[group, shard] = part[shard % 2 * share : (shard % 2 + 1) * share]
        loss_ref[group] = loss[at : at + per]


def scales(got, packed, slots, shards):
    blocks, rows = 2 * packed[0].shape[0], packed[0].shape[1] - EXTRA
    share = rows // shards // 2
    return pl.pallas_call(
        lambda *refs: scale_kernel(slots, *refs),
        in_specs=[VMEM] * (1 + len(packed)),
        out_specs=[VMEM] * 3,
        out_shape=[
            jax.ShapeDtypeStruct((blocks, shards, share, E), BF16),
            jax.ShapeDtypeStruct((E, blocks * rows // E), F32),
            jax.ShapeDtypeStruct((blocks, rows // E, E), F32),
        ],
        compiler_params=limit(8),
        name="scales",
    )(got, *packed)


def keys_kernel(gain, blocks, scale_ref, khat_ref, *refs):
    packed_refs, out_ref = refs[:-1], refs[-1]
    khat = khat_ref[...]
    rows = packed_refs[0].shape[1] - EXTRA
    per = rows // E
    total = jnp.zeros((E, khat.shape[0]), F32)
    for block, dots in dots_ahead(packed_refs, blocks, rows, khat):
        query = block_of(packed_refs, block)[:rows, :]
        parts = []
        for part in range(per):
            at = block * per + part
            scaled = query[part * E : (part + 1) * E].astype(F32) * scale_ref[:, at : at + 1]
            parts.append(scaled.T.astype(BF16))
        total = total + dot(jnp.concatenate(parts, axis=1), expo_of(dots))
    out_ref[...] = (total.T * gain).astype(BF16)


def keys(scale, khat, packed, gain):
    return pl.pallas_call(
        lambda *refs: keys_kernel(gain, 2 * packed[0].shape[0], *refs),
        in_specs=[VMEM] * (2 + len(packed)),
        out_specs=VMEM,
        out_shape=jax.ShapeDtypeStruct(khat.shape, BF16),
        compiler_params=limit(16),
        name="keys",
    )(scale, khat, *packed)


def total_kernel(gain, in_ref, out_ref):
    out_ref[...] = (jnp.sum(in_ref[...].astype(F32), axis=0) * gain).astype(BF16)


def totals(parts, gain):
    return pl.pallas_call(
        lambda *refs: total_kernel(gain, *refs),
        in_specs=[VMEM],
        out_specs=VMEM,
        out_shape=jax.ShapeDtypeStruct(parts.shape[1:], BF16),
        compiler_params=limit(4),
        name="totals",
    )(parts)


def weave_kernel(mine_ref, other_ref, out_ref):
    shards, share, _ = mine_ref.shape
    first = own_place()[1] == 0
    for shard in range(shards):
        at = ((shard % 2) * (shards // 2) + shard // 2) * 2 * share
        mine, other = mine_ref[shard], other_ref[shard]
        out_ref[at : at + share, :] = jnp.where(first, mine, other)
        out_ref[at + share : at + 2 * share, :] = jnp.where(first, other, mine)


def weave(mine, other):
    shards, share, _ = mine.shape
    return pl.pallas_call(
        weave_kernel,
        in_specs=[VMEM, VMEM],
        out_specs=VMEM,
        out_shape=jax.ShapeDtypeStruct((2 * shards * share, E), BF16),
        compiler_params=limit(4),
        name="weave",
    )(mine, other)


def body(
    video, space_qkv, space_out, time_qkv, time_out, proj_weight, queries, query_len, positive
):
    _, frames_dev, patches, _ = video.shape
    shards = lax.axis_size("seq")
    blocks = lax.axis_size("dp")
    patch_loc = patches // shards
    frames = frames_dev * shards
    query_dev, slots, _ = queries.shape
    rows = query_dev * slots
    partner = [(i, i ^ 1) for i in range(shards)]
    chips = [[2 * chip + own for chip in range(shards // 2)] for own in range(2)]

    spatial = space(video[0], space_qkv, space_out, shards)
    spatial, flat = lax.optimization_barrier((spatial, queries.reshape(rows, E)))
    items = lax.all_to_all(spatial, "seq", 0, 0, tiled=True)
    mine = pack_queries(flat, query_len, positive)
    lane = jnp.stack(
        [mine]
        + [
            lax.ppermute(mine, "dp", [(i, (i + by) % blocks) for i in range(blocks)])
            for by in range(2, blocks, 2)
        ]
    )
    items, lane = lax.optimization_barrier((items, lane))
    packed = [lane, lax.ppermute(lane, "dp", [(i, i ^ 1) for i in range(blocks)])]
    khat = time(items.reshape(-1, D), time_qkv, time_out, proj_weight, patch_loc)

    keep, send, sums = terms(packed, khat)
    got = lax.ppermute(send, "seq", partner)
    joined = join(keep, got, sums, shards // 2)
    joined = lax.all_to_all(joined, "seq", 0, 0, tiled=True, axis_index_groups=chips)
    parts, scale, loss = scales(joined, packed, slots, shards)
    parts = lax.all_to_all(
        parts.reshape((-1,) + parts.shape[2:]), ("dp", "seq"), 0, 0, tiled=True
    )
    video_grad = keys(scale, khat, packed, float(frames * P_SIZE))
    parts, video_grad = lax.optimization_barrier((parts, video_grad))
    summed = totals(parts.reshape((blocks, shards) + parts.shape[1:]), float(slots))
    query_grad = weave(summed, lax.ppermute(summed, "seq", partner))
    return (
        video_grad.reshape(1, frames, patch_loc, E),
        query_grad.reshape(query_dev, slots, E),
        loss[:, :, ::slots].reshape(-1, 1),
    )


def solution(mesh):
    placed = (
        P("dp", "seq", None, None),
        P(),
        P(),
        P(),
        P(),
        P(),
        P("dp", None, None),
        P("dp"),
        P("dp"),
    )
    return jax.shard_map(
        body,
        mesh=mesh,
        in_specs=placed,
        out_specs=(P("dp", None, "seq", None), P("dp", None, None), P(None, "dp")),
        check_vma=False,
    )
```
